128 devices in a mesh: vessel: 8 (over z, core), tissue: 16 (over y, x).
Axes of the slice: x: 4, y: 4, z: 4, core: 2. Of those that a mesh axis runs over, the one named last changes fastest.
Arguments:
- tissue_start: float32 [3, 32, 128, 128], P(None, 'vessel', 'tissue'), may hold values from 0 to 1
- consumption: float32 [3, 32, 128, 128], P(None, 'vessel', 'tissue'), may hold values from 0.002 to 0.05
- inlet: float32 [3, 512], P(None, ('vessel', 'tissue')), may hold values from 0.5 to 2
- flow: float32 [512, 256], P(('vessel', 'tissue')), may hold values from 0.3 to 30
- permeability: float32 [3], replicated, may hold values from 0.3 to 3
- intersection_count: int32 [512, 16], P(('vessel', 'tissue')), may hold values from 64 to 128, as said below
- intersection_segment: int32 [512, 16, 128], P(('vessel', 'tissue')), may hold values from 0 to 255
- intersection_voxel: int32 [512, 16, 128], P(('vessel', 'tissue')), may hold values from 0 to 4095
- intersection_weight: float32 [512, 16, 128], P(('vessel', 'tissue')), may hold values from 0.1 to 1
- upstream: int32 [512], P(('vessel', 'tissue')), may hold values from 0 to 511
Outputs:
- tissue_field: float32 [3, 32, 128, 128], P(None, 'vessel', 'tissue')
- vessel_field: float32 [3, 512, 256], P(None, ('vessel', 'tissue'))
The draws below stay inside these ranges and needn't reach their ends.
Inputs may be any that keep to these rules, and one draw needn't show every extreme that they name: `intersection_count`: every block has all 128 slots live toward at least one tissue brick of its vessel part, at most 128 toward any, and at least 64 toward every other.
All inputs are finite; a program needn't handle non-finite values.
Results may differ from the reference program's by a relative error of at most 0.0001.
Values sent between devices are 32-bit elements; how exact they have to be, the bound alone decides.
No kernel may reach another device: no remote copies, remote signals or barrier semaphores. Data moves between devices by JAX's collectives and lax.ppermute only.
A program may use at most 128 MiB of HBM per device.

```python
import math
import jax
import jax.numpy as jnp
from jax import lax

SPECIES = 3
SEG = 256
CAP = 128
OUTER = 2
SWEEPS = 4
CZ = 4
CY = 8
NX = 128
BLK_DEV = 4
NZ = 32
NY = 128
VOX = 4096
BLOCKS = 512
N_TISSUE = 16


def draw_intersection_count(key, part):
    bricks = NY // CY
    home_brick = jax.random.randint(jax.random.fold_in(key, 11), (BLOCKS,), 0, bricks)
    others = jax.random.randint(jax.random.fold_in(key, 12), (BLOCKS, bricks), CAP // 2, CAP + 1)
    column = jnp.arange(bricks)[None, :]
    return jnp.where(column == home_brick[:, None], CAP, others).astype(jnp.int32)


def place_ends(drawn, stream_key, smallest, largest):
    longest = drawn.shape.index(max(drawn.shape))
    spots = []
    for shift in (0, 1):
        where = [jax.random.randint(jax.random.fold_in(stream_key, axis), (), 0, length) for axis, length in enumerate(drawn.shape)]
        where[longest] = (where[longest] + shift) % drawn.shape[longest]
        spots.append(tuple(where))
    return drawn.at[spots[0]].set(smallest).at[spots[1]].set(largest)


def block_levels(own_key, dims, shards, low, high):
    gain, own = 1.0, jax.random.fold_in(own_key, 6)
    for axis_at, blocks in shards:
        heights = jnp.exp(jax.random.uniform(jax.random.fold_in(own, axis_at), (blocks,), jnp.float32, low / len(shards), high / len(shards)))
        gain = gain * jnp.repeat(heights, dims[axis_at] // blocks).reshape([-1 if axis == axis_at else 1 for axis in range(len(dims))])
    return gain


def setup_inputs(seed: int = 0) -> dict:
    arg_keys = jax.random.split(jax.random.key(seed), 11)
    return {
        "tissue_start": jnp.clip(1.0 * jax.random.uniform(arg_keys[0], (SPECIES, NZ, NY, NX), jnp.float32) ** block_levels(arg_keys[0], (SPECIES, NZ, NY, NX), ((1, 8), (2, 16)), -0.2, 0.2), 0.0, 1.0),
        "consumption": jnp.clip(jnp.exp(math.log(0.05) - 3.218876 * jax.random.uniform(arg_keys[1], (SPECIES, NZ, NY, NX), jnp.float32) ** block_levels(arg_keys[1], (SPECIES, NZ, NY, NX), ((1, 8), (2, 16)), -0.2, 0.2)), 0.002, 0.05),
        "inlet": jnp.clip(0.5 + 1.5 * jax.random.uniform(arg_keys[2], (SPECIES, BLOCKS), jnp.float32) ** block_levels(arg_keys[2], (SPECIES, BLOCKS), ((1, 128),), -0.2, 0.2), 0.5, 2.0),
        "flow": jnp.clip(jnp.exp(math.log(30.0) - 4.6051701 * jax.random.uniform(arg_keys[3], (BLOCKS, SEG), jnp.float32) ** block_levels(arg_keys[3], (BLOCKS, SEG), ((0, 128),), -0.2, 0.2)), 0.3, 30.0),
        "permeability": jnp.clip(jnp.exp(jax.random.uniform(arg_keys[4], (SPECIES,), jnp.float32, math.log(0.3), math.log(3.0))), 0.3, 3.0),
        "intersection_count": draw_intersection_count(jax.random.fold_in(arg_keys[10], 71), 0),
        "intersection_segment": place_ends(jax.random.randint(arg_keys[6], (BLOCKS, NY // CY, CAP), 0, SEG), jax.random.fold_in(arg_keys[6], 1), 0, SEG - 1).astype(jnp.int32),
        "intersection_voxel": place_ends(jax.random.randint(arg_keys[7], (BLOCKS, NY // CY, CAP), 0, VOX), jax.random.fold_in(arg_keys[7], 1), 0, VOX - 1).astype(jnp.int32),
        "intersection_weight": jnp.clip(jnp.exp(math.log(1.0) - 2.3025851 * jax.random.uniform(arg_keys[8], (BLOCKS, NY // CY, CAP), jnp.float32) ** block_levels(arg_keys[8], (BLOCKS, NY // CY, CAP), ((0, 128),), -0.2, 0.2)), 0.1, 1.0),
        "upstream": place_ends(jax.random.randint(arg_keys[9], (BLOCKS,), 0, BLOCKS), jax.random.fold_in(arg_keys[9], 1), 0, BLOCKS - 1).astype(jnp.int32),
    }


DIFFUSION = (1.0, 0.7, 0.7)


def combine(earlier, later):
    return earlier[0] * later[0], later[0] * earlier[1] + later[1]


def relax_sweep(tissue, source, consumption):
    padded = jnp.pad(tissue, ((0, 0), (1, 1), (1, 1), (1, 1)))
    neighbours = padded[:, 2:, 1:-1, 1:-1] + padded[:, :-2, 1:-1, 1:-1]
    neighbours = neighbours + padded[:, 1:-1, 2:, 1:-1] + padded[:, 1:-1, :-2, 1:-1]
    neighbours = neighbours + padded[:, 1:-1, 1:-1, 2:] + padded[:, 1:-1, 1:-1, :-2]
    rates = jnp.array(DIFFUSION, jnp.float32)[:, None, None, None]
    produced = jnp.zeros_like(tissue).at[2].set(2.0 * consumption[1] * tissue[1])
    return (source + produced + rates * neighbours) / (6.0 * rates + consumption)


def reference(tissue_start, consumption, inlet, flow, permeability, intersection_count, intersection_segment, intersection_voxel, intersection_weight, upstream):
    live_slot = jnp.arange(CAP).astype(jnp.int32)[None, None, :] < intersection_count[:, :, None]
    weight = jnp.where(live_slot, intersection_weight, 0.0).reshape(-1)
    block_index = jnp.arange(BLOCKS).astype(jnp.int32)[:, None, None]
    vessel_part = block_index // (BLK_DEV * N_TISSUE)
    column = jnp.arange(N_TISSUE).astype(jnp.int32)[None, :, None]
    voxel = intersection_voxel
    depth_index = vessel_part * CZ + voxel // (CY * NX)
    row_index = column * CY + (voxel // NX) % CY
    cell_index = ((depth_index * NY + row_index) * NX + voxel % NX).reshape(-1).astype(jnp.int32)
    owner = (block_index * SEG + intersection_segment).reshape(-1).astype(jnp.int32)
    weight_sum = jax.ops.segment_sum(weight, owner, BLOCKS * SEG).reshape(BLOCKS, SEG)
    tissue = tissue_start
    inflow = inlet
    vessel = jnp.zeros((SPECIES, BLOCKS, SEG), jnp.float32)
    for outer_step in range(OUTER):
        flat_field = tissue.reshape(SPECIES, -1)
        slot_values = flat_field[:, cell_index]
        gathered = jax.vmap(lambda species_row: jax.ops.segment_sum(species_row, owner, BLOCKS * SEG))(slot_values * weight[None, :])
        gathered = gathered.reshape(SPECIES, BLOCKS, SEG)
        denominator = flow[None] + permeability[:, None, None] * weight_sum[None]
        decay_rate = flow[None] / denominator
        drive_term = permeability[:, None, None] * gathered / denominator
        drive_term = drive_term.at[:, :, 0].add(decay_rate[:, :, 0] * inflow)
        _, vessel = lax.associative_scan(combine, (decay_rate, drive_term), axis=2)
        at_slot = vessel.reshape(SPECIES, -1)[:, owner]
        slot_flux = permeability[:, None] * weight[None, :] * (at_slot - slot_values)
        source = jax.vmap(lambda species_row: jax.ops.segment_sum(species_row, cell_index, NZ * NY * NX))(slot_flux)
        source = source.reshape(SPECIES, NZ, NY, NX)
        last_values = vessel[:, :, SEG - 1]
        inflow = 0.5 * (inlet + last_values[:, upstream])
        for sweep_step in range(SWEEPS):
            tissue = relax_sweep(tissue, source, consumption)
    return tissue, vessel
```

```python
import jax
import jax.numpy as jnp
from jax import lax
from jax.experimental import pallas as pl
from jax.experimental.pallas import tpu as pltpu
from jax.sharding import PartitionSpec as P


SEG = 256
SWEEPS = 4
DIFFUSION = (1.0, 0.7, 0.7)
BRICKS = 16
PARTS = 8
F32 = jnp.float32
BF16 = jnp.bfloat16
VMEM_LIMIT = 48 * 1024 * 1024


def rows_of(shape):
    return lax.broadcasted_iota(jnp.int32, shape, 0)


def lanes_of(shape):
    return lax.broadcasted_iota(jnp.int32, shape, 1)


def matmul(lhs, rhs):
    return lax.dot_general(lhs, rhs, (((1,), (0,)), ((), ())), preferred_element_type=F32)


def matmul_nt(lhs, rhs):
    return lax.dot_general(lhs, rhs, (((1,), (1,)), ((), ())), preferred_element_type=F32)


def split(value):
    high = value.astype(BF16).astype(F32)
    return high, value - high


def onehot(index, size):
    return jnp.where(rows_of((size, 128)) == index, 1.0, 0.0).astype(BF16)


def split_brick(brick):
    high, low = split(brick)
    return jnp.concatenate([high, low], axis=1).astype(BF16)


def gather_slots(brick_split, cells):
    hot = jnp.concatenate([onehot(cell & 127, 128) for cell in cells], axis=1)
    found = matmul(brick_split, jnp.concatenate([hot, hot], axis=0))
    values = []
    for i, cell in enumerate(cells):
        here = rows_of((32, 128)) == (cell >> 7)
        part = found[:, i * 128 : (i + 1) * 128]
        values.append(
            [
                jnp.sum(jnp.where(here, part[32 * k : 32 * k + 32], 0.0), axis=0, keepdims=True)
                for k in range(3)
            ]
        )
    return values


def pair_tile(rows):
    row = rows_of((8, 128))
    tile = jnp.broadcast_to(rows[7], (8, 128))
    for i in range(7):
        tile = jnp.where(row == i, rows[i], tile)
    return tile


def species_scale(perm_ref, shape):
    species = rows_of(shape) & 3
    return jnp.where(species == 0, perm_ref[0], jnp.where(species == 1, perm_ref[1], perm_ref[2]))


def prepare_slots(t, segment_ref, weight_ref, count_ref, weights, halves, hots):
    row = rows_of((8, 128))
    lane = lanes_of((1, 128))
    for pair in range(2):
        both = []
        for block in (2 * pair, 2 * pair + 1):
            weight = weight_ref[block, pl.ds(t, 1), :]
            both.append(jnp.where(lane < count_ref[block, t], weight, 0.0))
            segment = segment_ref[block, pl.ds(t, 1), :]
            halves[block, t] = jnp.broadcast_to(segment >> 7, (8, 128))
            hots[block, t] = onehot(segment & 127, 128)
        weights[pair, t] = jnp.where(row < 4, both[0], both[1])


def scan_segments(decay, drive):
    lane = lanes_of(decay.shape)
    step = 1
    while step < SEG:
        inside = lane >= step
        earlier_decay = jnp.where(inside, pltpu.roll(decay, step, 1), 1.0)
        earlier_drive = jnp.where(inside, pltpu.roll(drive, step, 1), 0.0)
        drive = decay * earlier_drive + drive
        decay = decay * earlier_decay
        step *= 2
    return drive


def solve_blocks(inflow, values, weights, halves, hots, voxel_ref, flow_ref, perm_ref, send_ref):
    row = rows_of((8, SEG))
    scale = species_scale(perm_ref, (8, SEG))
    wide = lambda ref, i: jnp.concatenate([ref[i, t] for t in range(BRICKS)], axis=1)
    decays, drives = [], []
    for pair in range(2):
        high, low = split(wide(values, pair) * wide(weights, pair))
        sums = []
        for block in (2 * pair, 2 * pair + 1):
            upper = wide(halves, block) == 1
            lhs = jnp.concatenate(
                [
                    jnp.where(upper, 0.0, high),
                    jnp.where(upper, 0.0, low),
                    jnp.where(upper, high, 0.0),
                    jnp.where(upper, low, 0.0),
                ],
                axis=0,
            ).astype(BF16)
            part = matmul_nt(lhs, wide(hots, block))
            sums.append(
                jnp.concatenate([part[0:8] + part[8:16], part[16:24] + part[24:32]], axis=1)
            )
        gathered = jnp.where(row < 4, sums[0], sums[1])
        weight_sum = jnp.where(row < 4, gathered[3:4], gathered[7:8])
        speed = jnp.where(row < 4, flow_ref[2 * pair : 2 * pair + 1], flow_ref[2 * pair + 1 : 2 * pair + 2])
        inverse = 1.0 / (speed + scale * weight_sum)
        decays.append(speed * inverse)
        drives.append(scale * gathered * inverse)
    decay = jnp.concatenate(decays, axis=0)
    drive = jnp.concatenate(drives, axis=0)
    drive = drive + jnp.where(lanes_of((16, SEG)) == 0, decay * inflow, 0.0)
    vessel = scan_segments(decay, drive)

    send_ref[0, 32:48] = jnp.zeros((16, 128), F32)
    send_ref[BRICKS - 1, 16:32] = jnp.zeros((16, 128), F32)
    tile_row = rows_of((8, 128))
    scale = species_scale(perm_ref, (8, 128))
    for pair in range(2):
        high, low = split(vessel[8 * pair : 8 * pair + 8])
        lhs = jnp.concatenate(
            [high[:, :128], low[:, :128], high[:, 128:], low[:, 128:]], axis=0
        ).astype(BF16)
        found = [matmul(lhs, wide(hots, block)) for block in (2 * pair, 2 * pair + 1)]
        for t in range(BRICKS):
            at_slot = []
            for i in range(2):
                part = found[i][:, t * 128 : (t + 1) * 128]
                at_slot.append(
                    jnp.where(
                        halves[2 * pair + i, t] == 1,
                        part[16:24] + part[24:32],
                        part[0:8] + part[8:16],
                    )
                )
            vessel_value = jnp.where(tile_row < 4, at_slot[0], at_slot[1])
            flux = scale * weights[pair, t] * (vessel_value - values[pair, t])
            cell = jnp.where(
                tile_row < 4, voxel_ref[2 * pair, t : t + 1, :], voxel_ref[2 * pair + 1, t : t + 1, :]
            )
            cell_row = (tile_row & 3) == 3
            cell_value = cell.astype(F32)
            first = ((cell >> 7) & 7) < 4
            here = slice(8 * pair, 8 * pair + 8)
            send_ref[t, here] = jnp.where(cell_row, cell_value, flux)
            if t > 0:
                send_ref[t - 1, 16 + 8 * pair : 24 + 8 * pair] = jnp.where(
                    cell_row, cell_value, jnp.where(first, flux, 0.0)
                )
            if t < BRICKS - 1:
                send_ref[t + 1, 32 + 8 * pair : 40 + 8 * pair] = jnp.where(
                    cell_row, cell_value, jnp.where(first, 0.0, flux)
                )
    return vessel


def inlet_column(inlet_ref):
    row = rows_of((16, 1))
    column = jnp.zeros((16, 1), F32)
    for block in range(4):
        for k in range(3):
            column = jnp.where(row == 4 * block + k, inlet_ref[k, block], column)
    return column


def first_solve_kernel(
    place_ref, count_ref, perm_ref, inlet_ref, region_ref, voxel_ref, segment_ref, weight_ref, flow_ref,
    send_ref, ends_ref, around_ref, values, weights, halves, hots,
):
    def brick(t, carry):
        prepare_slots(t, segment_ref, weight_ref, count_ref, weights, halves, hots)
        found = gather_slots(
            split_brick(region_ref[t]), [voxel_ref[block, pl.ds(t, 1), :] for block in range(4)]
        )
        for pair in range(2):
            values[pair, t] = pair_tile([*found[2 * pair], 1.0, *found[2 * pair + 1], 1.0])
        return carry

    lax.fori_loop(0, BRICKS, brick, 0)
    vessel = solve_blocks(
        inlet_column(inlet_ref), values, weights, halves, hots, voxel_ref, flow_ref, perm_ref, send_ref
    )
    part, t = place_ref[0], place_ref[1]
    last = vessel[:, SEG - 1 : SEG]
    spot = lanes_of((16, 128)) == part * 16 + rows_of((16, 128))
    ends = jnp.sum(jnp.where(spot, last, 0.0), axis=0, keepdims=True)
    ends_ref[...] = jnp.broadcast_to(ends[None], (PARTS, 8, 128))
    after = jnp.where(t < BRICKS - 1, region_ref[jnp.minimum(t + 1, BRICKS - 1)], 0.0)
    before = jnp.where(t > 0, region_ref[jnp.maximum(t - 1, 0)], 0.0)
    around_ref[...] = jnp.where((rows_of((96, 128)) & 7) < 4, after, before)


def second_solve_kernel(
    upstream_ref, count_ref, perm_ref, inlet_ref, values_ref, voxel_ref, segment_ref, weight_ref, flow_ref,
    send_ref, vessel_ref, values, weights, halves, hots,
):
    def brick(t, carry):
        prepare_slots(t, segment_ref, weight_ref, count_ref, weights, halves, hots)
        spare = (rows_of((8, 128)) & 3) == 3
        for pair in range(2):
            values[pair, t] = jnp.where(spare, 1.0, values_ref[t, 8 * pair : 8 * pair + 8])
        return carry

    lax.fori_loop(0, BRICKS, brick, 0)
    row, lane = rows_of((16, 128)), lanes_of((16, 128))
    picked = jnp.zeros((16, 128), F32)
    for block in range(4):
        feeder = upstream_ref[block]
        device = feeder >> 2
        ends = values_ref[device & 15, 3:4, :]
        spot = (device >> 4) * 16 + (feeder & 3) * 4
        picked = jnp.where(((row >> 2) == block) & (lane == spot + (row & 3)), ends, picked)
    inflow = 0.5 * (inlet_column(inlet_ref) + jnp.sum(picked, axis=1, keepdims=True))
    vessel = solve_blocks(
        inflow, values, weights, halves, hots, voxel_ref, flow_ref, perm_ref, send_ref
    )
    for block in range(4):
        for k in range(3):
            vessel_ref[k, block : block + 1, :] = vessel[4 * block + k : 4 * block + k + 1]


def scatter_slots(recv_ref, source, first_tile, tiles):
    source[...] = jnp.zeros((192, 128), F32)

    def sender(s, carry):
        hots, parts = [], []
        for i in range(tiles):
            start = first_tile + 8 * i
            for base in (0, 4):
                cell = recv_ref[s, start + base + 3 : start + base + 4, :].astype(jnp.int32)
                hots.append(onehot(cell & 127, 128))
                here = rows_of((32, 128)) == (cell >> 7)
                highs, lows = [], []
                for k in range(3):
                    high, low = split(recv_ref[s, start + base + k : start + base + k + 1, :])
                    highs.append(jnp.where(here, high, 0.0))
                    lows.append(jnp.where(here, low, 0.0))
                parts.append(jnp.concatenate(highs + lows, axis=0).astype(BF16))
        source[...] += matmul_nt(jnp.concatenate(parts, axis=1), jnp.concatenate(hots, axis=1))
        return carry

    lax.fori_loop(0, BRICKS, sender, 0)
    return source[0:96] + source[96:192]


def planes(value):
    return value.reshape(3, 4, 8, 128)


def first_scatter_kernel(
    place_ref, recv_ref, tissue_ref, around_ref, rate_ref, rate_after_ref, rate_before_ref,
    up_ref, down_ref, own_ref, side_ref, rate_side_ref, scratch,
):
    side_rows = (rows_of((96, 128)) & 7) < 4
    rate_side = jnp.where(side_rows, rate_after_ref[...], rate_before_ref[...])
    rate_side_ref[...] = rate_side
    rates = (planes(rate_ref[...]), planes(rate_side))
    for i, value in enumerate(rates):
        here = slice(8 * i, 8 * i + 8)
        up_ref[:, 7:10, here] = value[:, 1:4]
        down_ref[:, 7:10, here] = value[:, 0:3]
    write_messages(recv_ref, planes(tissue_ref[...]), planes(around_ref[...]), up_ref, down_ref, own_ref, side_ref, scratch)


def write_messages(recv_ref, tissue, around, up_ref, down_ref, own_ref, side_ref, scratch):
    own = scatter_slots(recv_ref, scratch, 0, 2)
    side = scatter_slots(recv_ref, scratch, 16, 4)
    own_ref[...] = own
    side_ref[...] = side
    for i, (value, source) in enumerate(((tissue, planes(own)), (around, planes(side)))):
        here = slice(8 * i, 8 * i + 8)
        up_ref[:, 0:4, here] = value
        down_ref[:, 0:4, here] = value
        up_ref[:, 4:7, here] = source[:, 1:4]
        down_ref[:, 4:7, here] = source[:, 0:3]


def unpack_edges(values_ref, t):
    after = values_ref[jnp.minimum(t + 1, BRICKS - 1), 16:64, :]
    before = values_ref[jnp.maximum(t - 1, 0), 16:64, :]
    after = jnp.where(t < BRICKS - 1, after, 0.0).reshape(6, 8, 128)
    before = jnp.where(t > 0, before, 0.0).reshape(6, 8, 128)
    low = lax.broadcasted_iota(jnp.int32, (6, 8, 128), 1) < 4
    even = jnp.where(low, after, pltpu.roll(before, 4, 1))
    odd = jnp.where(low, pltpu.roll(after, 4, 1), before)
    both = [value for i in range(6) for value in (even[i], odd[i])]
    return jnp.concatenate(both, axis=0).reshape(3, 4, 8, 128)


def second_scatter_kernel(
    place_ref, recv_ref, tissue_ref, values_ref, up_ref, down_ref, own_ref, side_ref, around_ref, scratch
):
    around = unpack_edges(values_ref, place_ref[1])
    around_ref[...] = around.reshape(96, 128)
    write_messages(recv_ref, planes(tissue_ref[...]), around, up_ref, down_ref, own_ref, side_ref, scratch)


def run_sweeps(place_ref, below, above, tissue_ref, around_ref, source_ref, side_ref, rate_own, rate_side, rate_below, rate_above, now, later, source, inverse, produced):
    part, t = place_ref[0], place_ref[1]
    row = rows_of((16, 128))
    row_inside = ((row < 8) | ((row >= 12) & (t > 0)) | ((row < 12) & (t < BRICKS - 1))) & (
        (row < 8) | (row >= 12) | (t < BRICKS - 1)
    )
    inside = jnp.where(row_inside, 1.0, 0.0)
    lower = jnp.where(part > 0, inside, 0.0)
    upper = jnp.where(part < PARTS - 1, inside, 0.0)
    for k in range(3):
        now[k, 0:4] = below[k, 0:4]
        now[k, 8:12] = above[k, 0:4]
        now[k, 4:8, 0:8] = planes(tissue_ref[...])[k]
        now[k, 4:8, 8:16] = planes(around_ref[...])[k]
        source[k, 1:4] = below[k, 4:7]
        source[k, 8:11] = above[k, 4:7]
        source[k, 4:8, 0:8] = planes(source_ref[...])[k]
        source[k, 4:8, 8:16] = planes(side_ref[...])[k]
        own, side = planes(rate_own[...])[k], planes(rate_side[...])[k]
        for z in range(1, 11):
            if z < 4:
                rate, valid = rate_below[k, z + 6], lower
            elif z < 8:
                rate, valid = jnp.concatenate([own[z - 4], side[z - 4]], axis=0), inside
            else:
                rate, valid = rate_above[k, z - 1], upper
            inverse[k, z] = valid / (6.0 * DIFFUSION[k] + rate)
            if k == 1:
                produced[z] = 2.0 * rate
    lane = lanes_of((16, 128))
    old, new = now, later
    for sweep in range(1, SWEEPS + 1):
        for k in range(3):
            for z in range(sweep, 12 - sweep):
                middle = old[k, z]
                total = old[k, z - 1] + old[k, z + 1]
                total = total + pltpu.roll(middle, 1, 0) + pltpu.roll(middle, 15, 0)
                total = total + jnp.where(lane > 0, pltpu.roll(middle, 1, 1), 0.0)
                total = total + jnp.where(lane < 127, pltpu.roll(middle, 127, 1), 0.0)
                total = source[k, z] + DIFFUSION[k] * total
                if k == 2:
                    total = total + produced[z] * old[1, z]
                new[k, z] = total * inverse[k, z]
        old, new = new, old
    return old


def first_sweeps_kernel(
    place_ref, below, above, tissue_ref, around_ref, source_ref, side_ref, rate_own, rate_side, recv_ref, ends_ref,
    out_ref, send_ref, now, later, source, inverse, produced,
):
    final = run_sweeps(
        place_ref, below, above, tissue_ref, around_ref, source_ref, side_ref, rate_own, rate_side, below, above,
        now, later, source, inverse, produced,
    )
    t = place_ref[1]
    brick = final[:, 4:8, 0:8].reshape(96, 128)
    out_ref[...] = brick
    brick_split = split_brick(brick)
    tiles = brick.reshape(6, 2, 8, 128)
    low = lax.broadcasted_iota(jnp.int32, (6, 8, 128), 1) < 4
    even, odd = tiles[:, 0], tiles[:, 1]
    first_rows = jnp.where(low, even, pltpu.roll(odd, 4, 1)).reshape(48, 128)
    last_rows = jnp.where(low, pltpu.roll(even, 4, 1), odd).reshape(48, 128)
    ends = ends_ref[0, 0:1]
    for part in range(1, PARTS):
        ends = ends + ends_ref[part, 0:1]

    def receiver(s, carry):
        cells = [recv_ref[s, 4 * b + 3 : 4 * b + 4, :].astype(jnp.int32) for b in range(4)]
        found = gather_slots(brick_split, cells)
        for pair in range(2):
            send_ref[s, 8 * pair : 8 * pair + 8] = pair_tile(
                [*found[2 * pair], ends, *found[2 * pair + 1], ends]
            )
        send_ref[s, 16:64] = jnp.where(s < t, first_rows, last_rows)
        return carry

    lax.fori_loop(0, BRICKS, receiver, 0)


def second_sweeps_kernel(
    place_ref, below, above, tissue_ref, around_ref, source_ref, side_ref, rate_own, rate_side, rate_below, rate_above,
    out_ref, now, later, source, inverse, produced,
):
    final = run_sweeps(
        place_ref, below, above, tissue_ref, around_ref, source_ref, side_ref, rate_own, rate_side, rate_below, rate_above,
        now, later, source, inverse, produced,
    )
    out_ref[...] = final[:, 4:8, 0:8]


def call(kernel, name, outs, args, scalars, scratch):
    whole = pl.BlockSpec(memory_space=pltpu.VMEM)
    scalar = pl.BlockSpec(memory_space=pltpu.SMEM)
    return pl.pallas_call(
        kernel,
        out_shape=[jax.ShapeDtypeStruct(shape, F32) for shape in outs],
        in_specs=[scalar] * scalars + [whole] * (len(args) - scalars),
        out_specs=[whole] * len(outs),
        scratch_shapes=scratch,
        compiler_params=pltpu.CompilerParams(vmem_limit_bytes=VMEM_LIMIT),
        name=name,
    )(*args)


def shards(
    tissue_start,
    consumption,
    inlet,
    flow,
    permeability,
    intersection_count,
    intersection_segment,
    intersection_voxel,
    intersection_weight,
    upstream,
):
    place = jnp.stack([lax.axis_index("vessel"), lax.axis_index("tissue")]).astype(jnp.int32)
    tissue = tissue_start.reshape(96, 128)
    rate = consumption.reshape(96, 128)

    def exchange(value, axis):
        return lax.all_to_all(value, axis, 0, 0, tiled=True)

    def shift(value, axis, step):
        size = lax.axis_size(axis)
        pairs = [(i, i + step) for i in range(size) if 0 <= i + step < size]
        return lax.ppermute(value, axis, pairs)

    solve_scratch = [
        pltpu.VMEM((2, BRICKS, 8, 128), F32),
        pltpu.VMEM((2, BRICKS, 8, 128), F32),
        pltpu.VMEM((4, BRICKS, 8, 128), jnp.int32),
        pltpu.VMEM((4, BRICKS, 128, 128), BF16),
    ]
    sweep_scratch = [
        pltpu.VMEM((3, 12, 16, 128), F32),
        pltpu.VMEM((3, 12, 16, 128), F32),
        pltpu.VMEM((3, 12, 16, 128), F32),
        pltpu.VMEM((3, 12, 16, 128), F32),
        pltpu.VMEM((12, 16, 128), F32),
    ]
    scatter_scratch = [pltpu.VMEM((192, 128), F32)]
    slots = (intersection_voxel, intersection_segment, intersection_weight, flow)

    rate_after = shift(rate, "tissue", -1)
    rate_before = shift(rate, "tissue", 1)
    region = exchange(jnp.broadcast_to(tissue[None], (BRICKS, 96, 128)), "tissue")
    send, ends, around = call(
        first_solve_kernel,
        "first_solve",
        [(BRICKS, 48, 128), (PARTS, 8, 128), (96, 128)],
        [place, intersection_count, permeability, inlet, region, *slots],
        4,
        solve_scratch,
    )
    received = exchange(send, "tissue")
    ends = exchange(ends, "vessel")
    up, down, source, side, rate_side = call(
        first_scatter_kernel,
        "first_scatter",
        [(3, 10, 16, 128), (3, 10, 16, 128), (96, 128), (96, 128), (96, 128)],
        [place, received, tissue, around, rate, rate_after, rate_before],
        1,
        scatter_scratch,
    )
    rate_below = below = shift(up, "vessel", 1)
    rate_above = above = shift(down, "vessel", -1)
    tissue, send = call(
        first_sweeps_kernel,
        "first_sweeps",
        [(96, 128), (BRICKS, 64, 128)],
        [place, below, above, tissue, around, source, side, rate, rate_side, received, ends],
        1,
        sweep_scratch,
    )
    values = exchange(send, "tissue")
    send, vessel = call(
        second_solve_kernel,
        "second_solve",
        [(BRICKS, 48, 128), (3, 4, SEG)],
        [upstream, intersection_count, permeability, inlet, values, *slots],
        4,
        solve_scratch,
    )
    received = exchange(send, "tissue")
    up, down, source, side, around = call(
        second_scatter_kernel,
        "second_scatter",
        [(3, 7, 16, 128), (3, 7, 16, 128), (96, 128), (96, 128), (96, 128)],
        [place, received, tissue, values],
        1,
        scatter_scratch,
    )
    below = shift(up, "vessel", 1)
    above = shift(down, "vessel", -1)
    (tissue,) = call(
        second_sweeps_kernel,
        "second_sweeps",
        [(3, 4, 8, 128)],
        [place, below, above, tissue, around, source, side, rate, rate_side, rate_below, rate_above],
        1,
        sweep_scratch,
    )
    return tissue, vessel


def solution(mesh):
    return jax.shard_map(
        shards,
        mesh=mesh,
        in_specs=(
            P(None, "vessel", "tissue", None),
            P(None, "vessel", "tissue", None),
            P(None, ("vessel", "tissue")),
            P(("vessel", "tissue"), None),
            P(),
            P(("vessel", "tissue"), None),
            P(("vessel", "tissue"), None, None),
            P(("vessel", "tissue"), None, None),
            P(("vessel", "tissue"), None, None),
            P(("vessel", "tissue")),
        ),
        out_specs=(P(None, "vessel", "tissue", None), P(None, ("vessel", "tissue"), None)),
        check_vma=False,
    )
```

```python
import jax
import jax.numpy as jnp
from jax import lax
from jax.experimental import pallas as pl
from jax.experimental.pallas import tpu as pltpu
from jax.sharding import PartitionSpec as P


SEG = 256
SWEEPS = 4
DIFFUSION = (1.0, 0.7, 0.7)
BRICKS = 16
PARTS = 8
F32 = jnp.float32
BF16 = jnp.bfloat16
VMEM_LIMIT = 32 * 1024 * 1024
SENDERS = 4


def rows_of(shape):
    return lax.broadcasted_iota(jnp.int32, shape, 0)


def lanes_of(shape):
    return lax.broadcasted_iota(jnp.int32, shape, 1)


def matmul(lhs, rhs):
    return lax.dot_general(lhs, rhs, (((1,), (0,)), ((), ())), preferred_element_type=F32)


def matmul_nt(lhs, rhs):
    return lax.dot_general(lhs, rhs, (((1,), (1,)), ((), ())), preferred_element_type=F32)


def split(value):
    high = value.astype(BF16).astype(F32)
    return high, value - high


def packed(row):
    return jnp.broadcast_to(row, (16, 128)).astype(F32).astype(BF16)


def matches(index, size):
    row = rows_of((16, 128)).astype(F32).astype(BF16)
    wanted = packed(index)
    return [row + BF16(i) == wanted for i in range(0, size, 16)]


def onehot(index, size):
    one, zero = jnp.ones((16, 128), BF16), jnp.zeros((16, 128), BF16)
    return jnp.concatenate([jnp.where(hit, one, zero) for hit in matches(index, size)], axis=0)


def split_brick(brick):
    high, low = split(brick)
    return jnp.concatenate([high, low], axis=1).astype(BF16)


def gather_slots(brick_split, cells):
    hot = jnp.concatenate([onehot(cell & 127, 128) for cell in cells], axis=1)
    found = matmul(brick_split, jnp.concatenate([hot, hot], axis=0))
    values = []
    for i, cell in enumerate(cells):
        here = rows_of((32, 128)) == (cell >> 7)
        part = found[:, i * 128 : (i + 1) * 128]
        values.append(
            [
                jnp.sum(jnp.where(here, part[32 * k : 32 * k + 32], 0.0), axis=0, keepdims=True)
                for k in range(3)
            ]
        )
    return values


def pair_tile(rows):
    row = rows_of((8, 128))
    tile = jnp.broadcast_to(rows[7], (8, 128))
    for i in range(7):
        tile = jnp.where(row == i, rows[i], tile)
    return tile


def species_scale(perm_ref, shape):
    species = rows_of(shape) & 3
    return jnp.where(species == 0, perm_ref[0], jnp.where(species == 1, perm_ref[1], perm_ref[2]))


def prepare_slots(t, segment_ref, weight_ref, count_ref, weights, halves, hots):
    row = rows_of((8, 128))
    lane = lanes_of((1, 128))
    for pair in range(2):
        both = []
        for block in (2 * pair, 2 * pair + 1):
            weight = weight_ref[block, pl.ds(t, 1), :]
            both.append(jnp.where(lane < count_ref[block, t], weight, 0.0))
            segment = segment_ref[block, pl.ds(t, 1), :]
            halves[block, t] = jnp.broadcast_to(segment >> 7, (8, 128))
            hots[block, t] = onehot(segment & 127, 128)
        weights[pair, t] = jnp.where(row < 4, both[0], both[1])


def scan_segments(decay, drive):
    lane = lanes_of(decay.shape)
    step = 1
    while step < SEG:
        inside = lane >= step
        earlier_decay = jnp.where(inside, pltpu.roll(decay, step, 1), 1.0)
        earlier_drive = jnp.where(inside, pltpu.roll(drive, step, 1), 0.0)
        drive = decay * earlier_drive + drive
        decay = decay * earlier_decay
        step *= 2
    return drive


def solve_blocks(inflow, values, weights, halves, hots, voxel_ref, flow_ref, perm_ref, send_ref, narrow):
    row = rows_of((8, SEG))
    scale = species_scale(perm_ref, (8, SEG))
    wide = lambda ref, i: jnp.concatenate([ref[i, t] for t in range(BRICKS)], axis=1)
    decays, drives = [], []
    for pair in range(2):
        high, low = split(wide(values, pair) * wide(weights, pair))
        sums = []
        for block in (2 * pair, 2 * pair + 1):
            upper = wide(halves, block) == 1
            lhs = jnp.concatenate(
                [
                    jnp.where(upper, 0.0, high),
                    jnp.where(upper, 0.0, low),
                    jnp.where(upper, high, 0.0),
                    jnp.where(upper, low, 0.0),
                ],
                axis=0,
            ).astype(BF16)
            part = matmul_nt(lhs, wide(hots, block))
            sums.append(
                jnp.concatenate([part[0:8] + part[8:16], part[16:24] + part[24:32]], axis=1)
            )
        gathered = jnp.where(row < 4, sums[0], sums[1])
        weight_sum = jnp.where(row < 4, gathered[3:4], gathered[7:8])
        speed = jnp.where(row < 4, flow_ref[2 * pair : 2 * pair + 1], flow_ref[2 * pair + 1 : 2 * pair + 2])
        inverse = 1.0 / (speed + scale * weight_sum)
        decays.append(speed * inverse)
        drives.append(scale * gathered * inverse)
    decay = jnp.concatenate(decays, axis=0)
    drive = jnp.concatenate(drives, axis=0)
    drive = drive + jnp.where(lanes_of((16, SEG)) == 0, decay * inflow, 0.0)
    vessel = scan_segments(decay, drive)

    send_ref[0, 32:48] = jnp.zeros((16, 128), F32)
    send_ref[BRICKS - 1, 16:32] = jnp.zeros((16, 128), F32)
    tile_row = rows_of((8, 128))
    scale = species_scale(perm_ref, (8, 128))
    for pair in range(2):
        high, low = split(vessel[8 * pair : 8 * pair + 8])
        lhs = jnp.concatenate(
            [high[:, :128], low[:, :128], high[:, 128:], low[:, 128:]], axis=0
        ).astype(BF16)
        found = [matmul(lhs, wide(hots, block)) for block in (2 * pair, 2 * pair + 1)]
        for t in range(BRICKS):
            at_slot = []
            for i in range(2):
                part = found[i][:, t * 128 : (t + 1) * 128]
                at_slot.append(
                    jnp.where(
                        halves[2 * pair + i, t] == 1,
                        part[16:24] + part[24:32],
                        part[0:8] + part[8:16],
                    )
                )
            vessel_value = jnp.where(tile_row < 4, at_slot[0], at_slot[1])
            flux = scale * weights[pair, t] * (vessel_value - values[pair, t])
            cell = jnp.where(
                tile_row < 4, voxel_ref[2 * pair, t : t + 1, :], voxel_ref[2 * pair + 1, t : t + 1, :]
            )
            cell_row = (tile_row & 3) == 3
            cell_value = cell.astype(F32)
            here = slice(8 * pair, 8 * pair + 8)
            own = jnp.where(cell_row, cell_value, flux)
            first = last = own
            if narrow:
                is_first = ((cell >> 7) & 7) < 4
                first = jnp.where(cell_row | is_first, own, 0.0)
                last = jnp.where(is_first & ~cell_row, 0.0, own)
            send_ref[t, here] = own
            if t > 0:
                send_ref[t - 1, 16 + 8 * pair : 24 + 8 * pair] = first
            if t < BRICKS - 1:
                send_ref[t + 1, 32 + 8 * pair : 40 + 8 * pair] = last
    return vessel


def inlet_column(inlet_ref):
    row = rows_of((16, 1))
    column = jnp.zeros((16, 1), F32)
    for block in range(4):
        for k in range(3):
            column = jnp.where(row == 4 * block + k, inlet_ref[k, block], column)
    return column


def first_solve_kernel(
    place_ref, count_ref, perm_ref, inlet_ref, region_ref, voxel_ref, segment_ref, weight_ref, flow_ref,
    rate_after_ref, rate_before_ref,
    send_ref, ends_ref, around_ref, values, weights, halves, hots,
):
    def brick(t, carry):
        prepare_slots(t, segment_ref, weight_ref, count_ref, weights, halves, hots)
        found = gather_slots(
            split_brick(region_ref[t]), [voxel_ref[block, pl.ds(t, 1), :] for block in range(4)]
        )
        for pair in range(2):
            values[pair, t] = pair_tile([*found[2 * pair], 1.0, *found[2 * pair + 1], 1.0])
        return carry

    lax.fori_loop(0, BRICKS, brick, 0, unroll=4)
    vessel = solve_blocks(
        inlet_column(inlet_ref), values, weights, halves, hots, voxel_ref, flow_ref, perm_ref, send_ref, False
    )
    part, t = place_ref[0], place_ref[1]
    last = vessel[:, SEG - 1 : SEG]
    spot = lanes_of((16, 128)) == part * 16 + rows_of((16, 128))
    ends = jnp.sum(jnp.where(spot, last, 0.0), axis=0, keepdims=True)
    ends_ref[...] = jnp.broadcast_to(ends[None], (PARTS, 8, 128))
    around_ref[0] = jnp.where(t < BRICKS - 1, region_ref[jnp.minimum(t + 1, BRICKS - 1)], 0.0)
    around_ref[1] = jnp.where(t > 0, region_ref[jnp.maximum(t - 1, 0)], 0.0)


def second_solve_kernel(
    upstream_ref, count_ref, perm_ref, inlet_ref, values_ref, voxel_ref, segment_ref, weight_ref, flow_ref,
    send_ref, vessel_ref, values, weights, halves, hots,
):
    def brick(t, carry):
        prepare_slots(t, segment_ref, weight_ref, count_ref, weights, halves, hots)
        spare = (rows_of((8, 128)) & 3) == 3
        for pair in range(2):
            values[pair, t] = jnp.where(spare, 1.0, values_ref[t, 8 * pair : 8 * pair + 8])
        return carry

    lax.fori_loop(0, BRICKS, brick, 0, unroll=4)
    row, lane = rows_of((16, 128)), lanes_of((16, 128))
    picked = jnp.zeros((16, 128), F32)
    for block in range(4):
        feeder = upstream_ref[block]
        device = feeder >> 2
        ends = values_ref[device & 15, 3:4, :]
        spot = (device >> 4) * 16 + (feeder & 3) * 4
        picked = jnp.where(((row >> 2) == block) & (lane == spot + (row & 3)), ends, picked)
    inflow = 0.5 * (inlet_column(inlet_ref) + jnp.sum(picked, axis=1, keepdims=True))
    vessel = solve_blocks(
        inflow, values, weights, halves, hots, voxel_ref, flow_ref, perm_ref, send_ref, True
    )
    for block in range(4):
        for k in range(3):
            vessel_ref[k, block : block + 1, :] = vessel[4 * block + k : 4 * block + k + 1]


def scatter_slots(recv_ref, source, groups):
    source[...] = jnp.zeros((len(groups), 192, 128), F32)
    zero = jnp.zeros((16, 128), BF16)

    def senders(i, carry):
        for j, tiles in enumerate(groups):
            hots, parts = [], []
            for q in range(SENDERS):
                s = i * SENDERS + q
                for start in tiles:
                    for base in (start, start + 4):
                        cell = recv_ref[s, base + 3 : base + 4, :].astype(jnp.int32)
                        hots.append(onehot(cell & 127, 128))
                        here = matches(cell >> 7, 32)
                        highs, lows = [], []
                        for k in range(3):
                            flux = jnp.broadcast_to(recv_ref[s, base + k : base + k + 1, :], (16, 128))
                            high = flux.astype(BF16)
                            low = (flux - high.astype(F32)).astype(BF16)
                            highs += [jnp.where(hit, high, zero) for hit in here]
                            lows += [jnp.where(hit, low, zero) for hit in here]
                        parts.append(jnp.concatenate(highs + lows, axis=0))
            source[j] += matmul_nt(jnp.concatenate(parts, axis=1), jnp.concatenate(hots, axis=1))
        return carry

    lax.fori_loop(0, BRICKS // SENDERS, senders, 0, unroll=2)
    return [source[j, 0:96] + source[j, 96:192] for j in range(len(groups))]


def planes(value):
    return value.reshape(3, 4, 8, 128)


def write_messages(tissues, sources, up_ref, down_ref):
    for i, (value, source) in enumerate(zip(tissues, sources)):
        here = slice(8 * i, 8 * i + 8)
        value, source = planes(value), planes(source)
        up_ref[:, 0:4, here] = value
        down_ref[:, 0:4, here] = value
        up_ref[:, 4:7, here] = source[:, 1:4]
        down_ref[:, 4:7, here] = source[:, 0:3]


def first_scatter_kernel(
    recv_ref, tissue_ref, around_ref, rate_ref, rate_after_ref, rate_before_ref, ends_ref,
    up_ref, down_ref, sources_ref, ends_row_ref, scratch,
):
    sources = scatter_slots(recv_ref, scratch, ((0, 8), (16, 24), (32, 40)))
    for i in range(3):
        sources_ref[i] = sources[i]
    write_messages((tissue_ref[...], around_ref[0], around_ref[1]), sources, up_ref, down_ref)
    for i, ref in enumerate((rate_ref, rate_after_ref, rate_before_ref)):
        here = slice(8 * i, 8 * i + 8)
        value = planes(ref[...])
        up_ref[:, 7:10, here] = value[:, 1:4]
        down_ref[:, 7:10, here] = value[:, 0:3]
    ends = ends_ref[0]
    for part in range(1, PARTS):
        ends = ends + ends_ref[part]
    ends_row_ref[...] = ends


def second_scatter_kernel(recv_ref, tissue_ref, around_ref, up_ref, down_ref, sources_ref, scratch):
    sources = scatter_slots(recv_ref, scratch, ((0, 8), (16, 24, 32, 40)))
    for i in range(2):
        sources_ref[i] = sources[i]
    write_messages((tissue_ref[...], around_ref[...]), sources, up_ref, down_ref)


def fill(now, source, below, above, tissues, sources):
    for k in range(3):
        now[k, 0:4] = below[k, 0:4]
        now[k, 8:12] = above[k, 0:4]
        source[k, 1:4] = below[k, 4:7]
        source[k, 8:11] = above[k, 4:7]
        for i in range(len(tissues)):
            now[k, 4:8, 8 * i : 8 * i + 8] = planes(tissues[i])[k]
            source[k, 4:8, 8 * i : 8 * i + 8] = planes(sources[i])[k]


def run_sweeps(now, later, source, inverse, produced):
    count = now.shape[2]
    lane = lanes_of((count, 128))
    old, new = now, later
    for sweep in range(1, SWEEPS + 1):
        for k in range(3):
            for z in range(sweep, 12 - sweep):
                middle = old[k, z]
                total = old[k, z - 1] + old[k, z + 1]
                total = total + pltpu.roll(middle, 1, 0) + pltpu.roll(middle, count - 1, 0)
                total = total + jnp.where(lane > 0, pltpu.roll(middle, 1, 1), 0.0)
                total = total + jnp.where(lane < 127, pltpu.roll(middle, 127, 1), 0.0)
                total = source[k, z] + DIFFUSION[k] * total
                if k == 2:
                    total = total + produced[z] * old[1, z]
                new[k, z] = total * inverse[k, z]
        old, new = new, old
    return old


def beside(after, before):
    low = lax.broadcasted_iota(jnp.int32, after.shape, after.ndim - 2) < 4
    return jnp.where(low, after, before)


def first_sweeps_kernel(
    place_ref, below, above, tissue_ref, around_ref, sources_ref, rate_own, rate_after, rate_before, recv_ref, ends_ref,
    out_ref, side_ref, inverse_ref, produced_ref, send_ref, now, later, source, inverse, produced,
):
    part, t = place_ref[0], place_ref[1]
    row = rows_of((24, 128))
    row_inside = (row < 8) | ((row < 16) & (t < BRICKS - 1)) | ((row >= 16) & (t > 0))
    inside = jnp.where(row_inside, 1.0, 0.0)
    lower = jnp.where(part > 0, inside, 0.0)
    upper = jnp.where(part < PARTS - 1, inside, 0.0)
    fill(now, source, below, above, [tissue_ref[...], around_ref[0], around_ref[1]], [sources_ref[i] for i in range(3)])
    for k in range(3):
        rates = [planes(ref[...])[k] for ref in (rate_own, rate_after, rate_before)]
        for z in range(1, 11):
            if z < 4:
                rate, valid = below[k, z + 6], lower
            elif z < 8:
                rate, valid = jnp.concatenate([value[z - 4] for value in rates], axis=0), inside
            else:
                rate, valid = above[k, z - 1], upper
            value = valid / (6.0 * DIFFUSION[k] + rate)
            inverse[k, z] = value
            inverse_ref[k, z, 0:8] = value[0:8]
            inverse_ref[k, z, 8:16] = beside(value[8:16], value[16:24])
            if k == 1:
                rate = 2.0 * rate
                produced[z] = rate
                produced_ref[z, 0:8] = rate[0:8]
                produced_ref[z, 8:16] = beside(rate[8:16], rate[16:24])
    final = run_sweeps(now, later, source, inverse, produced)
    brick = final[:, 4:8, 0:8].reshape(96, 128)
    out_ref[...] = brick
    side_ref[...] = beside(final[:, 4:8, 8:16], final[:, 4:8, 16:24]).reshape(96, 128)
    brick_split = split_brick(brick)
    ends = ends_ref[0:1]

    def receiver(s, carry):
        cells = [recv_ref[s, 4 * b + 3 : 4 * b + 4, :].astype(jnp.int32) for b in range(4)]
        found = gather_slots(brick_split, cells)
        for pair in range(2):
            send_ref[s, 8 * pair : 8 * pair + 8] = pair_tile(
                [*found[2 * pair], ends, *found[2 * pair + 1], ends]
            )
        return carry

    lax.fori_loop(0, BRICKS, receiver, 0, unroll=4)


def second_sweeps_kernel(
    below, above, tissue_ref, side_ref, sources_ref, inverse, produced, out_ref, now, later, source
):
    fill(now, source, below, above, [tissue_ref[...], side_ref[...]], [sources_ref[i] for i in range(2)])
    final = run_sweeps(now, later, source, inverse, produced)
    out_ref[...] = final[:, 4:8, 0:8]


def call(kernel, name, outs, args, scalars, scratch):
    whole = pl.BlockSpec(memory_space=pltpu.VMEM)
    scalar = pl.BlockSpec(memory_space=pltpu.SMEM)
    return pl.pallas_call(
        kernel,
        out_shape=[jax.ShapeDtypeStruct(shape, F32) for shape in outs],
        in_specs=[scalar] * scalars + [whole] * (len(args) - scalars),
        out_specs=[whole] * len(outs),
        scratch_shapes=scratch,
        compiler_params=pltpu.CompilerParams(vmem_limit_bytes=VMEM_LIMIT),
        name=name,
    )(*args)


def shards(
    tissue_start,
    consumption,
    inlet,
    flow,
    permeability,
    intersection_count,
    intersection_segment,
    intersection_voxel,
    intersection_weight,
    upstream,
):
    place = jnp.stack([lax.axis_index("vessel"), lax.axis_index("tissue")]).astype(jnp.int32)
    tissue = tissue_start.reshape(96, 128)
    rate = consumption.reshape(96, 128)

    def exchange(value, axis):
        return lax.all_to_all(value, axis, 0, 0, tiled=True)

    def shift(value, axis, step):
        size = lax.axis_size(axis)
        pairs = [(i, i + step) for i in range(size) if 0 <= i + step < size]
        return lax.ppermute(value, axis, pairs)

    solve_scratch = [
        pltpu.VMEM((2, BRICKS, 8, 128), F32),
        pltpu.VMEM((2, BRICKS, 8, 128), F32),
        pltpu.VMEM((4, BRICKS, 8, 128), jnp.int32),
        pltpu.VMEM((4, BRICKS, 128, 128), BF16),
    ]
    wide, ring = (3, 12, 24, 128), (3, 12, 16, 128)
    slots = (intersection_voxel, intersection_segment, intersection_weight, flow)

    bricks = jnp.broadcast_to(tissue[None], (BRICKS, 96, 128))
    rate_after = shift(rate, "tissue", -1)
    rate_before = shift(rate, "tissue", 1)
    region = exchange(bricks, "tissue")
    send, ends, around = call(
        first_solve_kernel,
        "first_solve",
        [(BRICKS, 48, 128), (PARTS, 8, 128), (2, 96, 128)],
        [place, intersection_count, permeability, inlet, region, *slots, rate_after, rate_before],
        4,
        solve_scratch,
    )
    received = exchange(send, "tissue")
    ends = exchange(ends, "vessel")
    up, down, sources, ends_row = call(
        first_scatter_kernel,
        "first_scatter",
        [(3, 10, 24, 128), (3, 10, 24, 128), (3, 96, 128), (8, 128)],
        [received, tissue, around, rate, rate_after, rate_before, ends],
        0,
        [pltpu.VMEM((3, 192, 128), F32)],
    )
    below = shift(up, "vessel", 1)
    above = shift(down, "vessel", -1)
    tissue, side, inverse, produced, send = call(
        first_sweeps_kernel,
        "first_sweeps",
        [(96, 128), (96, 128), ring, ring[1:], (BRICKS, 16, 128)],
        [place, below, above, tissue, around, sources, rate, rate_after, rate_before, received, ends_row],
        1,
        [pltpu.VMEM(wide, F32)] * 4 + [pltpu.VMEM(wide[1:], F32)],
    )
    values = exchange(send, "tissue")
    send, vessel = call(
        second_solve_kernel,
        "second_solve",
        [(BRICKS, 48, 128), (3, 4, SEG)],
        [upstream, intersection_count, permeability, inlet, values, *slots],
        4,
        solve_scratch,
    )
    received = exchange(send, "tissue")
    up, down, sources = call(
        second_scatter_kernel,
        "second_scatter",
        [(3, 7, 16, 128), (3, 7, 16, 128), (2, 96, 128)],
        [received, tissue, side],
        0,
        [pltpu.VMEM((2, 192, 128), F32)],
    )
    below = shift(up, "vessel", 1)
    above = shift(down, "vessel", -1)
    (tissue,) = call(
        second_sweeps_kernel,
        "second_sweeps",
        [(3, 4, 8, 128)],
        [below, above, tissue, side, sources, inverse, produced],
        0,
        [pltpu.VMEM(ring, F32)] * 3,
    )
    return tissue, vessel


def solution(mesh):
    return jax.shard_map(
        shards,
        mesh=mesh,
        in_specs=(
            P(None, "vessel", "tissue", None),
            P(None, "vessel", "tissue", None),
            P(None, ("vessel", "tissue")),
            P(("vessel", "tissue"), None),
            P(),
            P(("vessel", "tissue"), None),
            P(("vessel", "tissue"), None, None),
            P(("vessel", "tissue"), None, None),
            P(("vessel", "tissue"), None, None),
            P(("vessel", "tissue")),
        ),
        out_specs=(P(None, "vessel", "tissue", None), P(None, ("vessel", "tissue"), None)),
        check_vma=False,
    )
```

```python
import jax
import jax.numpy as jnp
from jax import lax
from jax.experimental import pallas as pl
from jax.experimental.pallas import tpu as pltpu
from jax.sharding import PartitionSpec as P


SEG = 256
SWEEPS = 4
DIFFUSION = (1.0, 0.7, 0.7)
BRICKS = 16
PARTS = 8
F32 = jnp.float32
BF16 = jnp.bfloat16
VMEM_LIMIT = 16 * 1024 * 1024
SENDERS = 4
SCAN_STEPS = 8
WEIGHTS, CELLS, TABLES = 0, 2, 4
DECAY, GAIN, SCALE, INLET = 8, 9, 10, 11


def rows_of(shape):
    return lax.broadcasted_iota(jnp.int32, shape, 0)


def lanes_of(shape):
    return lax.broadcasted_iota(jnp.int32, shape, 1)


def matmul(lhs, rhs):
    return lax.dot_general(lhs, rhs, (((1,), (0,)), ((), ())), preferred_element_type=F32)


def matmul_nt(lhs, rhs):
    return lax.dot_general(lhs, rhs, (((1,), (1,)), ((), ())), preferred_element_type=F32)


def split(value):
    high = value.astype(BF16).astype(F32)
    return high, value - high


def packed(row):
    return jnp.broadcast_to(row, (16, 128)).astype(F32).astype(BF16)


def matches(index, size):
    row = rows_of((16, 128)).astype(F32).astype(BF16)
    wanted = packed(index)
    return [row + BF16(i) == wanted for i in range(0, size, 16)]


def onehot(index, size):
    one, zero = jnp.ones((16, 128), BF16), jnp.zeros((16, 128), BF16)
    return jnp.concatenate([jnp.where(hit, one, zero) for hit in matches(index, size)], axis=0)


def split_brick(brick):
    high, low = split(brick)
    return jnp.concatenate([high, low], axis=1).astype(BF16)


def gather_slots(brick_split, cells):
    hot = jnp.concatenate([onehot(cell & 127, 128) for cell in cells], axis=1)
    found = matmul(brick_split, jnp.concatenate([hot, hot], axis=0))
    values = []
    for i, cell in enumerate(cells):
        here = rows_of((32, 128)) == (cell >> 7)
        part = found[:, i * 128 : (i + 1) * 128]
        values.append(
            [
                jnp.sum(jnp.where(here, part[32 * k : 32 * k + 32], 0.0), axis=0, keepdims=True)
                for k in range(3)
            ]
        )
    return values


def pair_tile(rows):
    row = rows_of((8, 128))
    tile = jnp.broadcast_to(rows[7], (8, 128))
    for i in range(7):
        tile = jnp.where(row == i, rows[i], tile)
    return tile


def spread_kernel(tissue_hbm, rate_hbm, bricks_ref, both_ref, sems):
    copies = [
        pltpu.make_async_copy(ref, both_ref.at[i], sems.at[i]) for i, ref in enumerate((tissue_hbm, rate_hbm))
    ]
    for copy in copies:
        copy.start()
    copies[0].wait()
    for t in range(BRICKS):
        bricks_ref[t] = both_ref[0]
    copies[1].wait()


def wide(ref, i):
    return jnp.concatenate([ref[i, t] for t in range(BRICKS)], axis=1)


def read_table(slots, i):
    tiles = [slots[TABLES + i // 4, 4 * (i % 4) + j] for j in range(4)]
    return jnp.concatenate([jnp.concatenate(tiles[:2], axis=1), jnp.concatenate(tiles[2:], axis=1)], axis=0)


def write_table(slots, i, value):
    for j in range(4):
        rows, lanes = 8 * (j // 2), 128 * (j % 2)
        slots[TABLES + i // 4, 4 * (i % 4) + j] = value[rows : rows + 8, lanes : lanes + 128]


def by_half(rows, upper):
    high, low = split(rows)
    return jnp.concatenate(
        [
            jnp.where(upper, 0.0, high),
            jnp.where(upper, 0.0, low),
            jnp.where(upper, high, 0.0),
            jnp.where(upper, low, 0.0),
        ],
        axis=0,
    ).astype(BF16)


def sum_segments(rows, pair, weights, hots):
    lhs = by_half(rows, weights < 0.0)
    sums = []
    for block in (2 * pair, 2 * pair + 1):
        part = matmul_nt(lhs, wide(hots, block))
        sums.append(jnp.concatenate([part[0:8] + part[8:16], part[16:24] + part[24:32]], axis=1))
    return jnp.where(rows_of((8, SEG)) < 4, sums[0], sums[1])


def column_of(ref, at):
    row = rows_of((16, 1))
    column = jnp.zeros((16, 1), F32)
    for block in range(4):
        for k in range(3):
            column = jnp.where(row == 4 * block + k, ref[at(block, k)], column)
    return column


def prepare_kernel(*refs):
    slots, hots = refs[7:9]
    segment_ref, weight_ref, voxel_ref, flow_ref, count_ref, perm_ref, inlet_ref = refs[9:16]
    sems = refs[16]
    copies = [pltpu.make_async_copy(refs[i], refs[9 + i], sems.at[i]) for i in range(7)]
    for copy in copies:
        copy.start()
    for copy in copies:
        copy.wait()
    row = rows_of((8, 128))
    lane = lanes_of((1, 128))

    def brick(t, carry):
        for pair in range(2):
            weights, cells = [], []
            for block in (2 * pair, 2 * pair + 1):
                weight = weight_ref[block, pl.ds(t, 1), :]
                weight = jnp.where(lane < count_ref[block, t], weight, 0.0)
                segment = segment_ref[block, pl.ds(t, 1), :]
                weights.append(jnp.where(segment >= 128, -weight, weight))
                cells.append(voxel_ref[block, pl.ds(t, 1), :].astype(F32))
                hots[block, t] = onehot(segment & 127, 128)
            slots[WEIGHTS + pair, t] = jnp.where(row < 4, weights[0], weights[1])
            slots[CELLS + pair, t] = jnp.where(row < 4, cells[0], cells[1])
        return carry

    lax.fori_loop(0, BRICKS, brick, 0, unroll=4)
    row = rows_of((8, SEG))
    scale = jnp.broadcast_to(column_of(perm_ref, lambda block, k: k), (16, SEG))
    write_table(slots, SCALE, scale)
    inlet = column_of(inlet_ref, lambda block, k: (k, block))
    write_table(slots, INLET, jnp.broadcast_to(inlet, (16, SEG)))
    weight_sums, speeds = [], []
    for pair in range(2):
        weights = wide(slots, WEIGHTS + pair)
        weight_sums.append(sum_segments(jnp.abs(weights), pair, weights, hots))
        speeds.append(jnp.where(row < 4, flow_ref[2 * pair : 2 * pair + 1], flow_ref[2 * pair + 1 : 2 * pair + 2]))
    speed = jnp.concatenate(speeds, axis=0)
    inverse = 1.0 / (speed + scale * jnp.concatenate(weight_sums, axis=0))
    decay = speed * inverse
    write_table(slots, DECAY, decay)
    write_table(slots, GAIN, scale * inverse)
    lane = lanes_of(decay.shape)
    for i in range(SCAN_STEPS):
        inside = lane >= 2**i
        write_table(slots, i, jnp.where(inside, decay, 0.0))
        decay = decay * jnp.where(inside, pltpu.roll(decay, 2**i, 1), 1.0)


def solve_blocks(inflow, values, slots, hots, send_ref, narrow):
    gathered = []
    for pair in range(2):
        weights = wide(slots, WEIGHTS + pair)
        gathered.append(sum_segments(wide(values, pair) * jnp.abs(weights), pair, weights, hots))
    vessel = read_table(slots, GAIN) * jnp.concatenate(gathered, axis=0)
    vessel = vessel + jnp.where(lanes_of((16, SEG)) == 0, read_table(slots, DECAY) * inflow, 0.0)
    for i in range(SCAN_STEPS):
        vessel = vessel + read_table(slots, i) * pltpu.roll(vessel, 2**i, 1)

    send_ref[0, 32:48] = jnp.zeros((16, 128), F32)
    send_ref[BRICKS - 1, 16:32] = jnp.zeros((16, 128), F32)
    tile_row = rows_of((8, 128))
    scale = read_table(slots, SCALE)[0:8, 0:128]
    for pair in range(2):
        high, low = split(vessel[8 * pair : 8 * pair + 8])
        lhs = jnp.concatenate(
            [high[:, :128], low[:, :128], high[:, 128:], low[:, 128:]], axis=0
        ).astype(BF16)
        found = [matmul(lhs, wide(hots, block)) for block in (2 * pair, 2 * pair + 1)]
        for t in range(BRICKS):
            weights = slots[WEIGHTS + pair, t]
            part = [value[:, t * 128 : (t + 1) * 128] for value in found]
            part = [jnp.where(tile_row < 4, part[0][8 * i : 8 * i + 8], part[1][8 * i : 8 * i + 8]) for i in range(4)]
            at_slot = jnp.where(weights < 0.0, part[2] + part[3], part[0] + part[1])
            flux = scale * jnp.abs(weights) * (at_slot - values[pair, t])
            cell = slots[CELLS + pair, t]
            cell_row = (tile_row & 3) == 3
            here = slice(8 * pair, 8 * pair + 8)
            own = jnp.where(cell_row, cell, flux)
            first = last = own
            if narrow:
                is_first = ((cell.astype(jnp.int32) >> 7) & 7) < 4
                first = jnp.where(cell_row | is_first, own, 0.0)
                last = jnp.where(is_first & ~cell_row, 0.0, own)
            send_ref[t, here] = own
            if t > 0:
                send_ref[t - 1, 16 + 8 * pair : 24 + 8 * pair] = first
            if t < BRICKS - 1:
                send_ref[t + 1, 32 + 8 * pair : 40 + 8 * pair] = last
    return vessel


def first_solve_kernel(region_ref, slots, hots, send_ref, ends_ref, values):
    def brick(t, carry):
        cells = [slots[CELLS + block // 2, t, 4 * (block % 2) : 4 * (block % 2) + 1].astype(jnp.int32) for block in range(4)]
        found = gather_slots(split_brick(region_ref[t]), cells)
        for pair in range(2):
            values[pair, t] = pair_tile([*found[2 * pair], 0.0, *found[2 * pair + 1], 0.0])
        return carry

    lax.fori_loop(0, BRICKS, brick, 0, unroll=4)
    vessel = solve_blocks(read_table(slots, INLET), values, slots, hots, send_ref, False)
    spot = lanes_of((16, 128)) == rows_of((16, 128))
    ends = jnp.sum(jnp.where(spot, vessel[:, SEG - 1 : SEG], 0.0), axis=0, keepdims=True)
    ends_ref[...] = jnp.broadcast_to(ends[None], (PARTS, 8, 128))


def second_solve_kernel(upstream_ref, values_ref, slots, hots, send_ref, vessel_ref, values):
    spare = (rows_of((8, 128)) & 3) == 3
    for t in range(BRICKS):
        for pair in range(2):
            values[pair, t] = jnp.where(spare, 0.0, values_ref[t, 8 * pair : 8 * pair + 8])
    row, lane = rows_of((16, 128)), lanes_of((16, 128))
    picked = jnp.zeros((16, 128), F32)
    for block in range(4):
        feeder = upstream_ref[block]
        device = feeder >> 2
        ends = values_ref[device & 15, 3:4, :]
        spot = (device >> 4) * 16 + (feeder & 3) * 4
        picked = jnp.where(((row >> 2) == block) & (lane == spot + (row & 3)), ends, picked)
    inflow = 0.5 * (read_table(slots, INLET) + jnp.sum(picked, axis=1, keepdims=True))
    vessel = solve_blocks(inflow, values, slots, hots, send_ref, True)
    for block in range(4):
        for k in range(3):
            vessel_ref[k, block : block + 1, :] = vessel[4 * block + k : 4 * block + k + 1]


def scatter_slots(recv_ref, source, groups):
    source[...] = jnp.zeros((len(groups), 192, 128), F32)
    zero = jnp.zeros((16, 128), BF16)

    def senders(i, carry):
        for j, tiles in enumerate(groups):
            hots, parts = [], []
            for q in range(SENDERS):
                s = i * SENDERS + q
                for start in tiles:
                    for base in (start, start + 4):
                        cell = recv_ref[s, base + 3 : base + 4, :].astype(jnp.int32)
                        hots.append(onehot(cell & 127, 128))
                        here = matches(cell >> 7, 32)
                        highs, lows = [], []
                        for k in range(3):
                            flux = jnp.broadcast_to(recv_ref[s, base + k : base + k + 1, :], (16, 128))
                            high = flux.astype(BF16)
                            low = (flux - high.astype(F32)).astype(BF16)
                            highs += [jnp.where(hit, high, zero) for hit in here]
                            lows += [jnp.where(hit, low, zero) for hit in here]
                        parts.append(jnp.concatenate(highs + lows, axis=0))
            source[j] += matmul_nt(jnp.concatenate(parts, axis=1), jnp.concatenate(hots, axis=1))
        return carry

    lax.fori_loop(0, BRICKS // SENDERS, senders, 0, unroll=2)
    return [source[j, 0:96] + source[j, 96:192] for j in range(len(groups))]


def planes(value):
    return value.reshape(3, 4, 8, 128)


def write_messages(tissues, sources, up_ref, down_ref):
    for i, (value, source) in enumerate(zip(tissues, sources)):
        here = slice(8 * i, 8 * i + 8)
        value, source = planes(value), planes(source)
        up_ref[:, 0:4, here] = value
        down_ref[:, 0:4, here] = value
        up_ref[:, 4:7, here] = source[:, 1:4]
        down_ref[:, 4:7, here] = source[:, 0:3]


def first_scatter_kernel(recv_ref, both_ref, after_ref, before_ref, up_ref, down_ref, sources_ref, scratch):
    sources = scatter_slots(recv_ref, scratch, ((0, 8), (16, 24), (32, 40)))
    for i in range(3):
        sources_ref[i] = sources[i]
    ring = (both_ref, after_ref, before_ref)
    write_messages([ref[0] for ref in ring], sources, up_ref, down_ref)
    for i, ref in enumerate(ring):
        here = slice(8 * i, 8 * i + 8)
        value = planes(ref[1])
        up_ref[:, 7:10, here] = value[:, 1:4]
        down_ref[:, 7:10, here] = value[:, 0:3]


def second_scatter_kernel(recv_ref, tissue_ref, around_ref, up_ref, down_ref, sources_ref, scratch):
    sources = scatter_slots(recv_ref, scratch, ((0, 8), (16, 24, 32, 40)))
    for i in range(2):
        sources_ref[i] = sources[i]
    write_messages((tissue_ref[...], around_ref[...]), sources, up_ref, down_ref)


def fill(now, source, below, above, tissues, sources):
    for k in range(3):
        now[k, 0:4] = below[k, 0:4]
        now[k, 8:12] = above[k, 0:4]
        source[k, 1:4] = below[k, 4:7]
        source[k, 8:11] = above[k, 4:7]
        for i in range(len(tissues)):
            now[k, 4:8, 8 * i : 8 * i + 8] = planes(tissues[i])[k]
            source[k, 4:8, 8 * i : 8 * i + 8] = planes(sources[i])[k]


def run_sweeps(now, later, source, inverse, produced):
    count = now.shape[2]
    lane = lanes_of((count, 128))
    old, new = now, later
    for sweep in range(1, SWEEPS + 1):
        for k in range(3):
            for z in range(sweep, 12 - sweep):
                middle = old[k, z]
                total = old[k, z - 1] + old[k, z + 1]
                total = total + pltpu.roll(middle, 1, 0) + pltpu.roll(middle, count - 1, 0)
                total = total + jnp.where(lane > 0, pltpu.roll(middle, 1, 1), 0.0)
                total = total + jnp.where(lane < 127, pltpu.roll(middle, 127, 1), 0.0)
                total = source[k, z] + DIFFUSION[k] * total
                if k == 2:
                    total = total + produced[z] * old[1, z]
                new[k, z] = total * inverse[k, z]
        old, new = new, old
    return old


def beside(after, before):
    low = lax.broadcasted_iota(jnp.int32, after.shape, after.ndim - 2) < 4
    return jnp.where(low, after, before)


def first_sweeps_kernel(
    below, above, both_ref, after_ref, before_ref, sources_ref, recv_ref, ends_ref,
    out_ref, side_ref, inverse_ref, produced_ref, send_ref, now, later, source, inverse, produced,
):
    ring = (both_ref, after_ref, before_ref)
    fill(now, source, below, above, [ref[0] for ref in ring], [sources_ref[i] for i in range(3)])
    for k in range(3):
        rates = [planes(ref[1])[k] for ref in ring]
        for z in range(1, 11):
            if z < 4:
                rate = below[k, z + 6]
            elif z < 8:
                rate = jnp.concatenate([value[z - 4] for value in rates], axis=0)
            else:
                rate = above[k, z - 1]
            value = jnp.where(rate > 0.0, 1.0 / (6.0 * DIFFUSION[k] + rate), 0.0)
            inverse[k, z] = value
            inverse_ref[k, z, 0:8] = value[0:8]
            inverse_ref[k, z, 8:16] = beside(value[8:16], value[16:24])
            if k == 1:
                rate = 2.0 * rate
                produced[z] = rate
                produced_ref[z, 0:8] = rate[0:8]
                produced_ref[z, 8:16] = beside(rate[8:16], rate[16:24])
    final = run_sweeps(now, later, source, inverse, produced)
    brick = final[:, 4:8, 0:8].reshape(96, 128)
    out_ref[...] = brick
    side_ref[...] = beside(final[:, 4:8, 8:16], final[:, 4:8, 16:24]).reshape(96, 128)
    brick_split = split_brick(brick)
    ends = ends_ref[0, 0:1]
    for part in range(1, PARTS):
        ends = ends + pltpu.roll(ends_ref[part], 16 * part, 1)[0:1]

    def receiver(s, carry):
        cells = [recv_ref[s, 4 * b + 3 : 4 * b + 4, :].astype(jnp.int32) for b in range(4)]
        found = gather_slots(brick_split, cells)
        for pair in range(2):
            send_ref[s, 8 * pair : 8 * pair + 8] = pair_tile(
                [*found[2 * pair], ends, *found[2 * pair + 1], ends]
            )
        return carry

    lax.fori_loop(0, BRICKS, receiver, 0, unroll=4)


def second_sweeps_kernel(
    below, above, tissue_ref, side_ref, sources_ref, inverse, produced, out_ref, now, later, source
):
    fill(now, source, below, above, [tissue_ref[...], side_ref[...]], [sources_ref[i] for i in range(2)])
    final = run_sweeps(now, later, source, inverse, produced)
    out_ref[...] = final[:, 4:8, 0:8]


VMEM = pl.BlockSpec(memory_space=pltpu.VMEM)
SMEM = pl.BlockSpec(memory_space=pltpu.SMEM)
HBM = pl.BlockSpec(memory_space=pltpu.HBM)


def call(kernel, name, outs, args, scratch, spaces=None):
    spaces = spaces or [VMEM] * len(args)
    args = [
        arg if space is SMEM else pltpu.with_memory_space_constraint(arg, space.memory_space)
        for arg, space in zip(args, spaces)
    ]
    return pl.pallas_call(
        kernel,
        out_shape=[jax.ShapeDtypeStruct(out, F32) if isinstance(out, tuple) else out for out in outs],
        in_specs=spaces,
        out_specs=[VMEM] * len(outs),
        scratch_shapes=scratch,
        compiler_params=pltpu.CompilerParams(vmem_limit_bytes=VMEM_LIMIT),
        name=name,
    )(*args)


def shards(
    tissue_start,
    consumption,
    inlet,
    flow,
    permeability,
    intersection_count,
    intersection_segment,
    intersection_voxel,
    intersection_weight,
    upstream,
):
    def exchange(value, axis):
        return lax.all_to_all(value, axis, 0, 0, tiled=True)

    def shift(value, axis, step):
        size = lax.axis_size(axis)
        pairs = [(i, i + step) for i in range(size) if 0 <= i + step < size]
        return lax.ppermute(value, axis, pairs)

    ring, large_ring = (3, 12, 16, 128), (3, 12, 24, 128)
    values_scratch = [pltpu.VMEM((2, BRICKS, 8, 128), F32)]

    bricks, both = call(
        spread_kernel,
        "spread",
        [(BRICKS, 96, 128), (2, 96, 128)],
        [tissue_start.reshape(96, 128), consumption.reshape(96, 128)],
        [pltpu.SemaphoreType.DMA((2,))],
        [HBM] * 2,
    )
    region = exchange(bricks, "tissue")
    after = shift(both, "tissue", -1)
    before = shift(both, "tissue", 1)
    slot_array = intersection_voxel.shape
    prepared = call(
        prepare_kernel,
        "prepare",
        [
            (7, BRICKS, 8, 128),
            jax.ShapeDtypeStruct((4, BRICKS, 128, 128), BF16),
        ],
        [
            intersection_segment,
            intersection_weight,
            intersection_voxel,
            flow,
            intersection_count,
            permeability,
            inlet,
        ],
        [
            pltpu.VMEM(slot_array, jnp.int32),
            pltpu.VMEM(slot_array, F32),
            pltpu.VMEM(slot_array, jnp.int32),
            pltpu.VMEM(flow.shape, F32),
            pltpu.SMEM(intersection_count.shape, jnp.int32),
            pltpu.SMEM(permeability.shape, F32),
            pltpu.SMEM(inlet.shape, F32),
            pltpu.SemaphoreType.DMA((7,)),
        ],
        [HBM] * 7,
    )
    region, after, before = lax.optimization_barrier((region, after, before))
    send, ends = call(
        first_solve_kernel,
        "first_solve",
        [(BRICKS, 48, 128), (PARTS, 8, 128)],
        [region, *prepared],
        values_scratch,
    )
    received = exchange(send, "tissue")
    ends = exchange(ends, "vessel")
    up, down, sources = call(
        first_scatter_kernel,
        "first_scatter",
        [(3, 10, 24, 128), (3, 10, 24, 128), (3, 96, 128)],
        [received, both, after, before],
        [pltpu.VMEM((3, 192, 128), F32)],
    )
    below = shift(up, "vessel", 1)
    above = shift(down, "vessel", -1)
    tissue, side, inverse, produced, send = call(
        first_sweeps_kernel,
        "first_sweeps",
        [(96, 128), (96, 128), ring, ring[1:], (BRICKS, 16, 128)],
        [below, above, both, after, before, sources, received, ends],
        [pltpu.VMEM(large_ring, F32)] * 4 + [pltpu.VMEM(large_ring[1:], F32)],
    )
    values = exchange(send, "tissue")
    send, vessel = call(
        second_solve_kernel,
        "second_solve",
        [(BRICKS, 48, 128), (3, 4, SEG)],
        [upstream, values, *prepared],
        values_scratch,
        [SMEM] + [VMEM] * 3,
    )
    received = exchange(send, "tissue")
    up, down, sources = call(
        second_scatter_kernel,
        "second_scatter",
        [(3, 7, 16, 128), (3, 7, 16, 128), (2, 96, 128)],
        [received, tissue, side],
        [pltpu.VMEM((2, 192, 128), F32)],
    )
    below = shift(up, "vessel", 1)
    above = shift(down, "vessel", -1)
    (tissue,) = call(
        second_sweeps_kernel,
        "second_sweeps",
        [(3, 4, 8, 128)],
        [below, above, tissue, side, sources, inverse, produced],
        [pltpu.VMEM(ring, F32)] * 3,
    )
    return tissue, vessel


def solution(mesh):
    return jax.shard_map(
        shards,
        mesh=mesh,
        in_specs=(
            P(None, "vessel", "tissue", None),
            P(None, "vessel", "tissue", None),
            P(None, ("vessel", "tissue")),
            P(("vessel", "tissue"), None),
            P(),
            P(("vessel", "tissue"), None),
            P(("vessel", "tissue"), None, None),
            P(("vessel", "tissue"), None, None),
            P(("vessel", "tissue"), None, None),
            P(("vessel", "tissue")),
        ),
        out_specs=(P(None, "vessel", "tissue", None), P(None, ("vessel", "tissue"), None)),
        check_vma=False,
    )
```

```python
import jax
import jax.numpy as jnp
from jax import lax
from jax.experimental import pallas as pl
from jax.experimental.pallas import tpu as pltpu
from jax.sharding import PartitionSpec as P


SEG = 256
SWEEPS = 4
DIFFUSION = (1.0, 0.7, 0.7)
BRICKS = 16
PARTS = 8
F32 = jnp.float32
BF16 = jnp.bfloat16
VMEM_LIMIT = 16 * 1024 * 1024
SENDERS = 4
SCAN_STEPS = 8
WEIGHTS, CELLS, TABLES = 0, 2, 4
DECAY, GAIN, SCALE, INLET = 8, 9, 10, 11


def rows_of(shape):
    return lax.broadcasted_iota(jnp.int32, shape, 0)


def lanes_of(shape):
    return lax.broadcasted_iota(jnp.int32, shape, 1)


def matmul(lhs, rhs):
    return lax.dot_general(lhs, rhs, (((1,), (0,)), ((), ())), preferred_element_type=F32)


def matmul_nt(lhs, rhs):
    return lax.dot_general(lhs, rhs, (((1,), (1,)), ((), ())), preferred_element_type=F32)


def split(value):
    high = value.astype(BF16).astype(F32)
    return high, value - high


def packed(row):
    return jnp.broadcast_to(row, (16, 128)).astype(F32).astype(BF16)


def matches(index, size):
    row = rows_of((16, 128)).astype(F32).astype(BF16)
    wanted = packed(index)
    return [row + BF16(i) == wanted for i in range(0, size, 16)]


def onehot(index, size):
    one, zero = jnp.ones((16, 128), BF16), jnp.zeros((16, 128), BF16)
    return jnp.concatenate([jnp.where(hit, one, zero) for hit in matches(index, size)], axis=0)


def split_brick(brick):
    high, low = split(brick)
    return jnp.concatenate([high, low], axis=1).astype(BF16)


def gather_slots(brick_split, cells):
    hot = jnp.concatenate([onehot(cell & 127, 128) for cell in cells], axis=1)
    found = matmul(brick_split, jnp.concatenate([hot, hot], axis=0))
    values = []
    for i, cell in enumerate(cells):
        here = rows_of((32, 128)) == (cell >> 7)
        part = found[:, i * 128 : (i + 1) * 128]
        values.append(
            [
                jnp.sum(jnp.where(here, part[32 * k : 32 * k + 32], 0.0), axis=0, keepdims=True)
                for k in range(3)
            ]
        )
    return values


def pair_tile(rows):
    row = rows_of((8, 128))
    tile = jnp.broadcast_to(rows[7], (8, 128))
    for i in range(7):
        tile = jnp.where(row == i, rows[i], tile)
    return tile


def spread_kernel(tissue_hbm, rate_hbm, bricks_hbm, tissue_ref, rate_ref, sems):
    arguments = [
        pltpu.make_async_copy(tissue_hbm, tissue_ref, sems.at[BRICKS]),
        pltpu.make_async_copy(rate_hbm, rate_ref, sems.at[BRICKS + 1]),
    ]
    bricks = [pltpu.make_async_copy(tissue_ref, bricks_hbm.at[t], sems.at[t]) for t in range(BRICKS)]
    for copy in arguments:
        copy.start()
    arguments[0].wait()
    for copy in bricks:
        copy.start()
    arguments[1].wait()
    for copy in bricks:
        copy.wait()


def wide(ref, i):
    return jnp.concatenate([ref[i, t] for t in range(BRICKS)], axis=1)


def read_table(slots, i):
    tiles = [slots[TABLES + i // 4, 4 * (i % 4) + j] for j in range(4)]
    return jnp.concatenate([jnp.concatenate(tiles[:2], axis=1), jnp.concatenate(tiles[2:], axis=1)], axis=0)


def write_table(slots, i, value):
    for j in range(4):
        rows, lanes = 8 * (j // 2), 128 * (j % 2)
        slots[TABLES + i // 4, 4 * (i % 4) + j] = value[rows : rows + 8, lanes : lanes + 128]


def by_half(rows, upper):
    high, low = split(rows)
    return jnp.concatenate(
        [
            jnp.where(upper, 0.0, high),
            jnp.where(upper, 0.0, low),
            jnp.where(upper, high, 0.0),
            jnp.where(upper, low, 0.0),
        ],
        axis=0,
    ).astype(BF16)


def sum_segments(rows, pair, weights, hots):
    lhs = by_half(rows, weights < 0.0)
    sums = []
    for block in (2 * pair, 2 * pair + 1):
        part = matmul_nt(lhs, wide(hots, block))
        sums.append(jnp.concatenate([part[0:8] + part[8:16], part[16:24] + part[24:32]], axis=1))
    return jnp.where(rows_of((8, SEG)) < 4, sums[0], sums[1])


def column_of(ref, at):
    row = rows_of((16, 1))
    column = jnp.zeros((16, 1), F32)
    for block in range(4):
        for k in range(3):
            column = jnp.where(row == 4 * block + k, ref[at(block, k)], column)
    return column


def prepare_kernel(*refs):
    slots, hots = refs[7:9]
    segment_ref, weight_ref, voxel_ref, flow_ref, count_ref, perm_ref, inlet_ref = refs[9:16]
    sems = refs[16]
    copies = [pltpu.make_async_copy(refs[i], refs[9 + i], sems.at[i]) for i in range(7)]
    for copy in copies:
        copy.start()
    for copy in copies:
        copy.wait()
    row = rows_of((8, 128))
    lane = lanes_of((1, 128))

    def brick(t, carry):
        for pair in range(2):
            weights, cells = [], []
            for block in (2 * pair, 2 * pair + 1):
                weight = weight_ref[block, pl.ds(t, 1), :]
                weight = jnp.where(lane < count_ref[block, t], weight, 0.0)
                segment = segment_ref[block, pl.ds(t, 1), :]
                weights.append(jnp.where(segment >= 128, -weight, weight))
                cells.append(voxel_ref[block, pl.ds(t, 1), :].astype(F32))
                hots[block, t] = onehot(segment & 127, 128)
            slots[WEIGHTS + pair, t] = jnp.where(row < 4, weights[0], weights[1])
            slots[CELLS + pair, t] = jnp.where(row < 4, cells[0], cells[1])
        return carry

    lax.fori_loop(0, BRICKS, brick, 0, unroll=4)
    row = rows_of((8, SEG))
    scale = jnp.broadcast_to(column_of(perm_ref, lambda block, k: k), (16, SEG))
    write_table(slots, SCALE, scale)
    inlet = column_of(inlet_ref, lambda block, k: (k, block))
    write_table(slots, INLET, jnp.broadcast_to(inlet, (16, SEG)))
    weight_sums, speeds = [], []
    for pair in range(2):
        weights = wide(slots, WEIGHTS + pair)
        weight_sums.append(sum_segments(jnp.abs(weights), pair, weights, hots))
        speeds.append(jnp.where(row < 4, flow_ref[2 * pair : 2 * pair + 1], flow_ref[2 * pair + 1 : 2 * pair + 2]))
    speed = jnp.concatenate(speeds, axis=0)
    inverse = 1.0 / (speed + scale * jnp.concatenate(weight_sums, axis=0))
    decay = speed * inverse
    write_table(slots, DECAY, decay)
    write_table(slots, GAIN, scale * inverse)
    lane = lanes_of(decay.shape)
    for i in range(SCAN_STEPS):
        inside = lane >= 2**i
        write_table(slots, i, jnp.where(inside, decay, 0.0))
        decay = decay * jnp.where(inside, pltpu.roll(decay, 2**i, 1), 1.0)


def solve_blocks(inflow, values, slots, hots, send_ref, narrow):
    gathered = []
    for pair in range(2):
        weights = wide(slots, WEIGHTS + pair)
        gathered.append(sum_segments(wide(values, pair) * jnp.abs(weights), pair, weights, hots))
    vessel = read_table(slots, GAIN) * jnp.concatenate(gathered, axis=0)
    vessel = vessel + jnp.where(lanes_of((16, SEG)) == 0, read_table(slots, DECAY) * inflow, 0.0)
    for i in range(SCAN_STEPS):
        vessel = vessel + read_table(slots, i) * pltpu.roll(vessel, 2**i, 1)

    send_ref[0, 32:48] = jnp.zeros((16, 128), F32)
    send_ref[BRICKS - 1, 16:32] = jnp.zeros((16, 128), F32)
    tile_row = rows_of((8, 128))
    scale = read_table(slots, SCALE)[0:8, 0:128]
    for pair in range(2):
        high, low = split(vessel[8 * pair : 8 * pair + 8])
        lhs = jnp.concatenate(
            [high[:, :128], low[:, :128], high[:, 128:], low[:, 128:]], axis=0
        ).astype(BF16)
        found = [matmul(lhs, wide(hots, block)) for block in (2 * pair, 2 * pair + 1)]
        for t in range(BRICKS):
            weights = slots[WEIGHTS + pair, t]
            part = [value[:, t * 128 : (t + 1) * 128] for value in found]
            part = [jnp.where(tile_row < 4, part[0][8 * i : 8 * i + 8], part[1][8 * i : 8 * i + 8]) for i in range(4)]
            at_slot = jnp.where(weights < 0.0, part[2] + part[3], part[0] + part[1])
            flux = scale * jnp.abs(weights) * (at_slot - values[pair, t])
            cell = slots[CELLS + pair, t]
            cell_row = (tile_row & 3) == 3
            here = slice(8 * pair, 8 * pair + 8)
            own = jnp.where(cell_row, cell, flux)
            first = last = own
            if narrow:
                is_first = ((cell.astype(jnp.int32) >> 7) & 7) < 4
                first = jnp.where(cell_row | is_first, own, 0.0)
                last = jnp.where(is_first & ~cell_row, 0.0, own)
            send_ref[t, here] = own
            if t > 0:
                send_ref[t - 1, 16 + 8 * pair : 24 + 8 * pair] = first
            if t < BRICKS - 1:
                send_ref[t + 1, 32 + 8 * pair : 40 + 8 * pair] = last
    return vessel


def first_solve_kernel(region_ref, slots, hots, send_ref, ends_ref, around_ref, values):
    def brick(t, carry):
        cells = [slots[CELLS + block // 2, t, 4 * (block % 2) : 4 * (block % 2) + 1].astype(jnp.int32) for block in range(4)]
        found = gather_slots(split_brick(region_ref[t]), cells)
        for pair in range(2):
            values[pair, t] = pair_tile([*found[2 * pair], 0.0, *found[2 * pair + 1], 0.0])
        return carry

    lax.fori_loop(0, BRICKS, brick, 0, unroll=4)
    vessel = solve_blocks(read_table(slots, INLET), values, slots, hots, send_ref, False)
    spot = lanes_of((16, 128)) == rows_of((16, 128))
    ends = jnp.sum(jnp.where(spot, vessel[:, SEG - 1 : SEG], 0.0), axis=0, keepdims=True)
    ends_ref[...] = jnp.broadcast_to(ends[None], (PARTS, 8, 128))
    t = lax.axis_index("tissue")
    around_ref[0] = jnp.where(t < BRICKS - 1, region_ref[jnp.minimum(t + 1, BRICKS - 1)], 0.0)
    around_ref[1] = jnp.where(t > 0, region_ref[jnp.maximum(t - 1, 0)], 0.0)


def second_solve_kernel(upstream_ref, values_ref, slots, hots, send_ref, vessel_ref, values):
    spare = (rows_of((8, 128)) & 3) == 3
    for t in range(BRICKS):
        for pair in range(2):
            values[pair, t] = jnp.where(spare, 0.0, values_ref[t, 8 * pair : 8 * pair + 8])
    row, lane = rows_of((16, 128)), lanes_of((16, 128))
    picked = jnp.zeros((16, 128), F32)
    for block in range(4):
        feeder = upstream_ref[block]
        device = feeder >> 2
        ends = values_ref[device & 15, 3:4, :]
        spot = (device >> 4) * 16 + (feeder & 3) * 4
        picked = jnp.where(((row >> 2) == block) & (lane == spot + (row & 3)), ends, picked)
    inflow = 0.5 * (read_table(slots, INLET) + jnp.sum(picked, axis=1, keepdims=True))
    vessel = solve_blocks(inflow, values, slots, hots, send_ref, True)
    for block in range(4):
        for k in range(3):
            vessel_ref[k, block : block + 1, :] = vessel[4 * block + k : 4 * block + k + 1]


def scatter_slots(recv_ref, sources):
    zero = jnp.zeros((16, 128), BF16)
    for source, _, _ in sources:
        source[...] = jnp.zeros(source.shape, F32)

    def senders(i, carry):
        for source, tiles, size in sources:
            hots, parts = [], []
            for q in range(SENDERS):
                s = i * SENDERS + q
                for start in tiles:
                    for base in (start, start + 4):
                        cell = recv_ref[s, base + 3 : base + 4, :].astype(jnp.int32)
                        hots.append(onehot(cell & 127, 128))
                        row = cell >> 7
                        if size == 16:
                            row = (row >> 3) * 4 + (row & 3)
                        here = matches(row, size)
                        highs, lows = [], []
                        for k in range(3):
                            flux = jnp.broadcast_to(recv_ref[s, base + k : base + k + 1, :], (16, 128))
                            high = flux.astype(BF16)
                            low = (flux - high.astype(F32)).astype(BF16)
                            highs += [jnp.where(hit, high, zero) for hit in here]
                            lows += [jnp.where(hit, low, zero) for hit in here]
                        parts.append(jnp.concatenate(highs + lows, axis=0))
            source[...] += matmul_nt(jnp.concatenate(parts, axis=1), jnp.concatenate(hots, axis=1))
        return carry

    lax.fori_loop(0, BRICKS // SENDERS, senders, 0, unroll=2)
    return [source[0 : 3 * size] + source[3 * size : 6 * size] for source, _, size in sources]


def interleave(first, last):
    first, last = first.reshape(6, 8, 128), last.reshape(6, 8, 128)
    low = lax.broadcasted_iota(jnp.int32, (6, 8, 128), 1) < 4
    even = jnp.where(low, first, pltpu.roll(last, 4, 1))
    odd = jnp.where(low, pltpu.roll(first, 4, 1), last)
    return jnp.concatenate([value[i] for i in range(6) for value in (even, odd)], axis=0)


def planes(value):
    return value.reshape(3, 4, 8, 128)


def is_even():
    return lax.axis_index("vessel") % 2 == 0


def toward(value, near):
    upward = is_even() if near else ~is_even()
    return jnp.where(upward, value[:, 1:4], value[:, 0:3])


def write_messages(tissues, sources, near_ref, far_ref):
    for i, (value, source) in enumerate(zip(tissues, sources)):
        here = slice(8 * i, 8 * i + 8)
        value, source = planes(value), planes(source)
        for ref, near in ((near_ref, True), (far_ref, False)):
            ref[:, 0:4, here] = value
            ref[:, 4:7, here] = toward(source, near)


def first_scatter_kernel(
    recv_ref, tissue_ref, around_ref, rate_ref, after_ref, before_ref, near_ref, far_ref, sources_ref, *sums
):
    sources = scatter_slots(recv_ref, [(sums[i], (16 * i, 16 * i + 8), 32) for i in range(3)])
    for i in range(3):
        sources_ref[i] = sources[i]
    write_messages([tissue_ref[...], around_ref[0], around_ref[1]], sources, near_ref, far_ref)
    for i, ref in enumerate((rate_ref, after_ref, before_ref)):
        here = slice(8 * i, 8 * i + 8)
        value = planes(ref[...])
        near_ref[:, 7:10, here] = toward(value, True)
        far_ref[:, 7:10, here] = toward(value, False)


def second_scatter_kernel(recv_ref, tissue_ref, side_ref, near_ref, far_ref, sources_ref, *sums):
    own, first, last = scatter_slots(
        recv_ref, [(sums[i], (16 * i, 16 * i + 8), 32 if i == 0 else 16) for i in range(3)]
    )
    sources = [own, interleave(first, last)]
    for i in range(2):
        sources_ref[i] = sources[i]
    write_messages([tissue_ref[...], side_ref[...]], sources, near_ref, far_ref)


def neighbours(near, far, k, where):
    near, far = near[k, where], far[k, where]
    return jnp.where(is_even(), far, near), jnp.where(is_even(), near, far)


def fill(now, source, near, far, tissues, sources):
    for k in range(3):
        now[k, 0:4], now[k, 8:12] = neighbours(near, far, k, slice(0, 4))
        source[k, 1:4], source[k, 8:11] = neighbours(near, far, k, slice(4, 7))
        for i in range(len(tissues)):
            now[k, 4:8, 8 * i : 8 * i + 8] = planes(tissues[i])[k]
            source[k, 4:8, 8 * i : 8 * i + 8] = planes(sources[i])[k]


def run_sweeps(now, later, source, inverse, produced):
    count = now.shape[2]
    lane = lanes_of((count, 128))
    old, new = now, later
    for sweep in range(1, SWEEPS + 1):
        for k in range(3):
            for z in range(sweep, 12 - sweep):
                middle = old[k, z]
                total = old[k, z - 1] + old[k, z + 1]
                total = total + pltpu.roll(middle, 1, 0) + pltpu.roll(middle, count - 1, 0)
                total = total + jnp.where(lane > 0, pltpu.roll(middle, 1, 1), 0.0)
                total = total + jnp.where(lane < 127, pltpu.roll(middle, 127, 1), 0.0)
                total = source[k, z] + DIFFUSION[k] * total
                if k == 2:
                    total = total + produced[z] * old[1, z]
                new[k, z] = total * inverse[k, z]
        old, new = new, old
    return old


def beside(after, before):
    low = lax.broadcasted_iota(jnp.int32, after.shape, after.ndim - 2) < 4
    return jnp.where(low, after, before)


def first_sweeps_kernel(
    near, far, tissue_ref, around_ref, rate_ref, after_ref, before_ref, sources_ref, recv_ref, ends_ref,
    out_ref, side_ref, inverse_ref, produced_ref, send_ref, now, later, source, inverse, produced,
):
    tissues = [tissue_ref[...], around_ref[0], around_ref[1]]
    fill(now, source, near, far, tissues, [sources_ref[i] for i in range(3)])
    for k in range(3):
        rates = [planes(ref[...])[k] for ref in (rate_ref, after_ref, before_ref)]
        below, above = neighbours(near, far, k, slice(7, 10))
        for z in range(1, 11):
            if z < 4:
                rate = below[z - 1]
            elif z < 8:
                rate = jnp.concatenate([value[z - 4] for value in rates], axis=0)
            else:
                rate = above[z - 8]
            value = jnp.where(rate > 0.0, 1.0 / (6.0 * DIFFUSION[k] + rate), 0.0)
            inverse[k, z] = value
            inverse_ref[k, z, 0:8] = value[0:8]
            inverse_ref[k, z, 8:16] = beside(value[8:16], value[16:24])
            if k == 1:
                rate = 2.0 * rate
                produced[z] = rate
                produced_ref[z, 0:8] = rate[0:8]
                produced_ref[z, 8:16] = beside(rate[8:16], rate[16:24])
    final = run_sweeps(now, later, source, inverse, produced)
    brick = final[:, 4:8, 0:8].reshape(96, 128)
    out_ref[...] = brick
    side_ref[...] = beside(final[:, 4:8, 8:16], final[:, 4:8, 16:24]).reshape(96, 128)
    brick_split = split_brick(brick)
    ends = ends_ref[0, 0:1]
    for part in range(1, PARTS):
        ends = ends + pltpu.roll(ends_ref[part], 16 * part, 1)[0:1]

    def receiver(s, carry):
        cells = [recv_ref[s, 4 * b + 3 : 4 * b + 4, :].astype(jnp.int32) for b in range(4)]
        found = gather_slots(brick_split, cells)
        for pair in range(2):
            send_ref[s, 8 * pair : 8 * pair + 8] = pair_tile(
                [*found[2 * pair], ends, *found[2 * pair + 1], ends]
            )
        return carry

    lax.fori_loop(0, BRICKS, receiver, 0, unroll=4)


def second_sweeps_kernel(
    near, far, tissue_ref, side_ref, sources_ref, inverse, produced, out_ref, now, later, source
):
    fill(now, source, near, far, [tissue_ref[...], side_ref[...]], [sources_ref[i] for i in range(2)])
    final = run_sweeps(now, later, source, inverse, produced)
    out_ref[...] = final[:, 4:8, 0:8]


VMEM = pl.BlockSpec(memory_space=pltpu.VMEM)
SMEM = pl.BlockSpec(memory_space=pltpu.SMEM)
HBM = pl.BlockSpec(memory_space=pltpu.HBM)


def call(kernel, name, outs, args, scratch, spaces=None, out_spaces=None):
    spaces = spaces or [VMEM] * len(args)
    args = [
        arg if space is SMEM else pltpu.with_memory_space_constraint(arg, space.memory_space)
        for arg, space in zip(args, spaces)
    ]
    return pl.pallas_call(
        kernel,
        out_shape=[jax.ShapeDtypeStruct(out, F32) if isinstance(out, tuple) else out for out in outs],
        in_specs=spaces,
        out_specs=out_spaces or [VMEM] * len(outs),
        scratch_shapes=scratch,
        compiler_params=pltpu.CompilerParams(vmem_limit_bytes=VMEM_LIMIT),
        name=name,
    )(*args)


def shards(
    tissue_start,
    consumption,
    inlet,
    flow,
    permeability,
    intersection_count,
    intersection_segment,
    intersection_voxel,
    intersection_weight,
    upstream,
):
    def exchange(value, axis):
        return lax.all_to_all(value, axis, 0, 0, tiled=True)

    def shift(value, axis, step):
        size = lax.axis_size(axis)
        pairs = [(i, i + step) for i in range(size) if 0 <= i + step < size]
        return lax.ppermute(value, axis, pairs)

    def swap(value, first):
        starts = range(first, lax.axis_size("vessel") - 1, 2)
        return lax.ppermute(value, "vessel", [pair for i in starts for pair in ((i, i + 1), (i + 1, i))])

    ring, large_ring = (3, 12, 16, 128), (3, 12, 24, 128)
    values_scratch = [pltpu.VMEM((2, BRICKS, 8, 128), F32)]

    bricks, tissue, rate = call(
        spread_kernel,
        "spread",
        [(BRICKS, 96, 128), (96, 128), (96, 128)],
        [tissue_start.reshape(96, 128), consumption.reshape(96, 128)],
        [pltpu.SemaphoreType.DMA((BRICKS + 2,))],
        [HBM] * 2,
        [HBM, VMEM, VMEM],
    )
    region = exchange(bricks, "tissue")
    after = shift(rate, "tissue", -1)
    before = shift(rate, "tissue", 1)
    slot_array = intersection_voxel.shape
    prepared = call(
        prepare_kernel,
        "prepare",
        [
            (7, BRICKS, 8, 128),
            jax.ShapeDtypeStruct((4, BRICKS, 128, 128), BF16),
        ],
        [
            intersection_segment,
            intersection_weight,
            intersection_voxel,
            flow,
            intersection_count,
            permeability,
            inlet,
        ],
        [
            pltpu.VMEM(slot_array, jnp.int32),
            pltpu.VMEM(slot_array, F32),
            pltpu.VMEM(slot_array, jnp.int32),
            pltpu.VMEM(flow.shape, F32),
            pltpu.SMEM(intersection_count.shape, jnp.int32),
            pltpu.SMEM(permeability.shape, F32),
            pltpu.SMEM(inlet.shape, F32),
            pltpu.SemaphoreType.DMA((7,)),
        ],
        [HBM] * 7,
    )
    region, after, before = lax.optimization_barrier((region, after, before))
    send, ends, around = call(
        first_solve_kernel,
        "first_solve",
        [(BRICKS, 48, 128), (PARTS, 8, 128), (2, 96, 128)],
        [region, *prepared],
        values_scratch,
    )
    received = exchange(send, "tissue")
    ends = exchange(ends, "vessel")
    near, far, sources = call(
        first_scatter_kernel,
        "first_scatter",
        [(3, 10, 24, 128), (3, 10, 24, 128), (3, 96, 128)],
        [received, tissue, around, rate, after, before],
        [pltpu.VMEM((192, 128), F32)] * 3,
    )
    near, far = swap(near, 0), swap(far, 1)
    tissue, side, inverse, produced, send = call(
        first_sweeps_kernel,
        "first_sweeps",
        [(96, 128), (96, 128), ring, ring[1:], (BRICKS, 16, 128)],
        [near, far, tissue, around, rate, after, before, sources, received, ends],
        [pltpu.VMEM(large_ring, F32)] * 4 + [pltpu.VMEM(large_ring[1:], F32)],
    )
    values = exchange(send, "tissue")
    send, vessel = call(
        second_solve_kernel,
        "second_solve",
        [(BRICKS, 48, 128), (3, 4, SEG)],
        [upstream, values, *prepared],
        values_scratch,
        [SMEM] + [VMEM] * 3,
    )
    received = exchange(send, "tissue")
    near, far, sources = call(
        second_scatter_kernel,
        "second_scatter",
        [(3, 7, 16, 128), (3, 7, 16, 128), (2, 96, 128)],
        [received, tissue, side],
        [pltpu.VMEM((rows, 128), F32) for rows in (192, 96, 96)],
    )
    near, far = swap(near, 0), swap(far, 1)
    (tissue,) = call(
        second_sweeps_kernel,
        "second_sweeps",
        [(3, 4, 8, 128)],
        [near, far, tissue, side, sources, inverse, produced],
        [pltpu.VMEM(ring, F32)] * 3,
    )
    return tissue, vessel


def solution(mesh):
    return jax.shard_map(
        shards,
        mesh=mesh,
        in_specs=(
            P(None, "vessel", "tissue", None),
            P(None, "vessel", "tissue", None),
            P(None, ("vessel", "tissue")),
            P(("vessel", "tissue"), None),
            P(),
            P(("vessel", "tissue"), None),
            P(("vessel", "tissue"), None, None),
            P(("vessel", "tissue"), None, None),
            P(("vessel", "tissue"), None, None),
            P(("vessel", "tissue")),
        ),
        out_specs=(P(None, "vessel", "tissue", None), P(None, ("vessel", "tissue"), None)),
        check_vma=False,
    )
```

```python
import jax
import jax.numpy as jnp
from jax import lax
from jax.experimental import pallas as pl
from jax.experimental.pallas import tpu as pltpu
from jax.sharding import PartitionSpec as P


SEG = 256
SWEEPS = 4
DIFFUSION = (1.0, 0.7, 0.7)
BRICKS = 16
PARTS = 8
F32 = jnp.float32
BF16 = jnp.bfloat16
VMEM_LIMIT = 16 * 1024 * 1024
SENDERS = 4
SCAN_STEPS = 8
WEIGHTS, CELLS, TABLES = 0, 2, 4
DECAY, GAIN, SCALE, INLET = 8, 9, 10, 11


def rows_of(shape):
    return lax.broadcasted_iota(jnp.int32, shape, 0)


def lanes_of(shape):
    return lax.broadcasted_iota(jnp.int32, shape, 1)


def matmul(lhs, rhs):
    return lax.dot_general(lhs, rhs, (((1,), (0,)), ((), ())), preferred_element_type=F32)


def matmul_nt(lhs, rhs):
    return lax.dot_general(lhs, rhs, (((1,), (1,)), ((), ())), preferred_element_type=F32)


def split(value):
    high = value.astype(BF16).astype(F32)
    return high, value - high


def packed(row):
    return jnp.broadcast_to(row, (16, 128)).astype(F32).astype(BF16)


def matches(index, size):
    row = rows_of((16, 128)).astype(F32).astype(BF16)
    wanted = packed(index)
    return [row + BF16(i) == wanted for i in range(0, size, 16)]


def onehot(index, size):
    one, zero = jnp.ones((16, 128), BF16), jnp.zeros((16, 128), BF16)
    return jnp.concatenate([jnp.where(hit, one, zero) for hit in matches(index, size)], axis=0)


def split_brick(brick):
    high, low = split(brick)
    return jnp.concatenate([high, low], axis=1).astype(BF16)


def gather_slots(brick_split, cells):
    hot = jnp.concatenate([onehot(cell & 127, 128) for cell in cells], axis=1)
    found = matmul(brick_split, jnp.concatenate([hot, hot], axis=0))
    values = []
    for i, cell in enumerate(cells):
        here = rows_of((32, 128)) == (cell >> 7)
        part = found[:, i * 128 : (i + 1) * 128]
        values.append(
            [
                jnp.sum(jnp.where(here, part[32 * k : 32 * k + 32], 0.0), axis=0, keepdims=True)
                for k in range(3)
            ]
        )
    return values


def pair_tile(rows):
    row = rows_of((8, 128))
    tile = jnp.broadcast_to(rows[7], (8, 128))
    for i in range(7):
        tile = jnp.where(row == i, rows[i], tile)
    return tile


def spread_kernel(tissue_hbm, rate_hbm, bricks_hbm, tissue_ref, rate_ref, sems):
    arguments = [
        pltpu.make_async_copy(tissue_hbm, tissue_ref, sems.at[BRICKS]),
        pltpu.make_async_copy(rate_hbm, rate_ref, sems.at[BRICKS + 1]),
    ]
    bricks = [pltpu.make_async_copy(tissue_ref, bricks_hbm.at[t], sems.at[t]) for t in range(BRICKS)]
    for copy in arguments:
        copy.start()
    arguments[0].wait()
    for copy in bricks:
        copy.start()
    arguments[1].wait()
    for copy in bricks:
        copy.wait()


def wide(ref, i):
    return jnp.concatenate([ref[i, t] for t in range(BRICKS)], axis=1)


def read_table(slots, i):
    tiles = [slots[TABLES + i // 4, 4 * (i % 4) + j] for j in range(4)]
    return jnp.concatenate([jnp.concatenate(tiles[:2], axis=1), jnp.concatenate(tiles[2:], axis=1)], axis=0)


def write_table(slots, i, value):
    for j in range(4):
        rows, lanes = 8 * (j // 2), 128 * (j % 2)
        slots[TABLES + i // 4, 4 * (i % 4) + j] = value[rows : rows + 8, lanes : lanes + 128]


def by_half(rows, upper):
    high, low = split(rows)
    return jnp.concatenate(
        [
            jnp.where(upper, 0.0, high),
            jnp.where(upper, 0.0, low),
            jnp.where(upper, high, 0.0),
            jnp.where(upper, low, 0.0),
        ],
        axis=0,
    ).astype(BF16)


def sum_segments(rows, pair, weights, hots):
    lhs = by_half(rows, weights < 0.0)
    sums = []
    for block in (2 * pair, 2 * pair + 1):
        part = matmul_nt(lhs, wide(hots, block))
        sums.append(jnp.concatenate([part[0:8] + part[8:16], part[16:24] + part[24:32]], axis=1))
    return jnp.where(rows_of((8, SEG)) < 4, sums[0], sums[1])


def column_of(ref, at):
    row = rows_of((16, 1))
    column = jnp.zeros((16, 1), F32)
    for block in range(4):
        for k in range(3):
            column = jnp.where(row == 4 * block + k, ref[at(block, k)], column)
    return column


def prepare_kernel(*refs):
    slots, hots = refs[7:9]
    segment_ref, weight_ref, voxel_ref, flow_ref, count_ref, perm_ref, inlet_ref = refs[9:16]
    sems = refs[16]
    copies = [pltpu.make_async_copy(refs[i], refs[9 + i], sems.at[i]) for i in range(7)]
    for copy in copies:
        copy.start()
    for copy in copies:
        copy.wait()
    row = rows_of((8, 128))
    lane = lanes_of((1, 128))

    def brick(t, carry):
        for pair in range(2):
            weights, cells = [], []
            for block in (2 * pair, 2 * pair + 1):
                weight = weight_ref[block, pl.ds(t, 1), :]
                weight = jnp.where(lane < count_ref[block, t], weight, 0.0)
                segment = segment_ref[block, pl.ds(t, 1), :]
                weights.append(jnp.where(segment >= 128, -weight, weight))
                cells.append(voxel_ref[block, pl.ds(t, 1), :].astype(F32))
                hots[block, t] = onehot(segment & 127, 128)
            slots[WEIGHTS + pair, t] = jnp.where(row < 4, weights[0], weights[1])
            slots[CELLS + pair, t] = jnp.where(row < 4, cells[0], cells[1])
        return carry

    lax.fori_loop(0, BRICKS, brick, 0, unroll=4)
    row = rows_of((8, SEG))
    scale = jnp.broadcast_to(column_of(perm_ref, lambda block, k: k), (16, SEG))
    write_table(slots, SCALE, scale)
    inlet = column_of(inlet_ref, lambda block, k: (k, block))
    write_table(slots, INLET, jnp.broadcast_to(inlet, (16, SEG)))
    weight_sums, speeds = [], []
    for pair in range(2):
        weights = wide(slots, WEIGHTS + pair)
        weight_sums.append(sum_segments(jnp.abs(weights), pair, weights, hots))
        speeds.append(jnp.where(row < 4, flow_ref[2 * pair : 2 * pair + 1], flow_ref[2 * pair + 1 : 2 * pair + 2]))
    speed = jnp.concatenate(speeds, axis=0)
    inverse = 1.0 / (speed + scale * jnp.concatenate(weight_sums, axis=0))
    decay = speed * inverse
    write_table(slots, DECAY, decay)
    write_table(slots, GAIN, scale * inverse)
    lane = lanes_of(decay.shape)
    for i in range(SCAN_STEPS):
        inside = lane >= 2**i
        write_table(slots, i, jnp.where(inside, decay, 0.0))
        decay = decay * jnp.where(inside, pltpu.roll(decay, 2**i, 1), 1.0)


def solve_blocks(inflow, values, slots, hots, send_ref, narrow):
    gathered = []
    for pair in range(2):
        weights = wide(slots, WEIGHTS + pair)
        gathered.append(sum_segments(wide(values, pair) * jnp.abs(weights), pair, weights, hots))
    vessel = read_table(slots, GAIN) * jnp.concatenate(gathered, axis=0)
    vessel = vessel + jnp.where(lanes_of((16, SEG)) == 0, read_table(slots, DECAY) * inflow, 0.0)
    for i in range(SCAN_STEPS):
        vessel = vessel + read_table(slots, i) * pltpu.roll(vessel, 2**i, 1)

    send_ref[0, 32:48] = jnp.zeros((16, 128), F32)
    send_ref[BRICKS - 1, 16:32] = jnp.zeros((16, 128), F32)
    tile_row = rows_of((8, 128))
    scale = read_table(slots, SCALE)[0:8, 0:128]
    for pair in range(2):
        high, low = split(vessel[8 * pair : 8 * pair + 8])
        lhs = jnp.concatenate(
            [high[:, :128], low[:, :128], high[:, 128:], low[:, 128:]], axis=0
        ).astype(BF16)
        found = [matmul(lhs, wide(hots, block)) for block in (2 * pair, 2 * pair + 1)]
        for t in range(BRICKS):
            weights = slots[WEIGHTS + pair, t]
            part = [value[:, t * 128 : (t + 1) * 128] for value in found]
            part = [jnp.where(tile_row < 4, part[0][8 * i : 8 * i + 8], part[1][8 * i : 8 * i + 8]) for i in range(4)]
            at_slot = jnp.where(weights < 0.0, part[2] + part[3], part[0] + part[1])
            flux = scale * jnp.abs(weights) * (at_slot - values[pair, t])
            cell = slots[CELLS + pair, t]
            cell_row = (tile_row & 3) == 3
            here = slice(8 * pair, 8 * pair + 8)
            own = jnp.where(cell_row, cell, flux)
            first = last = own
            if narrow:
                is_first = ((cell.astype(jnp.int32) >> 7) & 7) < 4
                first = jnp.where(cell_row | is_first, own, 0.0)
                last = jnp.where(is_first & ~cell_row, 0.0, own)
            send_ref[t, here] = own
            if t > 0:
                send_ref[t - 1, 16 + 8 * pair : 24 + 8 * pair] = first
            if t < BRICKS - 1:
                send_ref[t + 1, 32 + 8 * pair : 40 + 8 * pair] = last
    return vessel


def first_solve_kernel(region_ref, slots, hots, send_ref, ends_ref, around_ref, values):
    def brick(t, carry):
        cells = [slots[CELLS + block // 2, t, 4 * (block % 2) : 4 * (block % 2) + 1].astype(jnp.int32) for block in range(4)]
        found = gather_slots(split_brick(region_ref[t]), cells)
        for pair in range(2):
            values[pair, t] = pair_tile([*found[2 * pair], 0.0, *found[2 * pair + 1], 0.0])
        return carry

    lax.fori_loop(0, BRICKS, brick, 0, unroll=4)
    vessel = solve_blocks(read_table(slots, INLET), values, slots, hots, send_ref, False)
    spot = lanes_of((16, 128)) == rows_of((16, 128))
    ends = jnp.sum(jnp.where(spot, vessel[:, SEG - 1 : SEG], 0.0), axis=0, keepdims=True)
    ends_ref[...] = jnp.broadcast_to(ends[None], (PARTS, 8, 128))
    t = lax.axis_index("tissue")
    around_ref[0] = jnp.where(t < BRICKS - 1, region_ref[jnp.minimum(t + 1, BRICKS - 1)], 0.0)
    around_ref[1] = jnp.where(t > 0, region_ref[jnp.maximum(t - 1, 0)], 0.0)


def second_solve_kernel(upstream_ref, values_ref, slots, hots, send_ref, vessel_ref, values):
    spare = (rows_of((8, 128)) & 3) == 3
    for t in range(BRICKS):
        for pair in range(2):
            values[pair, t] = jnp.where(spare, 0.0, values_ref[t, 8 * pair : 8 * pair + 8])
    row, lane = rows_of((16, 128)), lanes_of((16, 128))
    picked = jnp.zeros((16, 128), F32)
    for block in range(4):
        feeder = upstream_ref[block]
        device = feeder >> 2
        ends = values_ref[device & 15, 3:4, :]
        spot = (device >> 4) * 16 + (feeder & 3) * 4
        picked = jnp.where(((row >> 2) == block) & (lane == spot + (row & 3)), ends, picked)
    inflow = 0.5 * (read_table(slots, INLET) + jnp.sum(picked, axis=1, keepdims=True))
    vessel = solve_blocks(inflow, values, slots, hots, send_ref, True)
    for block in range(4):
        for k in range(3):
            vessel_ref[k, block : block + 1, :] = vessel[4 * block + k : 4 * block + k + 1]


def scatter_slots(recv_ref, sources):
    zero = jnp.zeros((16, 128), BF16)
    for source, _, _ in sources:
        source[...] = jnp.zeros(source.shape, F32)

    def senders(i, carry):
        for source, tiles, size in sources:
            hots, parts = [], []
            for q in range(SENDERS):
                s = i * SENDERS + q
                for start in tiles:
                    for base in (start, start + 4):
                        cell = recv_ref[s, base + 3 : base + 4, :].astype(jnp.int32)
                        hots.append(onehot(cell & 127, 128))
                        row = cell >> 7
                        if size == 16:
                            row = (row >> 3) * 4 + (row & 3)
                        here = matches(row, size)
                        highs, lows = [], []
                        for k in range(3):
                            flux = jnp.broadcast_to(recv_ref[s, base + k : base + k + 1, :], (16, 128))
                            high = flux.astype(BF16)
                            low = (flux - high.astype(F32)).astype(BF16)
                            highs += [jnp.where(hit, high, zero) for hit in here]
                            lows += [jnp.where(hit, low, zero) for hit in here]
                        parts.append(jnp.concatenate(highs + lows, axis=0))
            source[...] += matmul_nt(jnp.concatenate(parts, axis=1), jnp.concatenate(hots, axis=1))
        return carry

    lax.fori_loop(0, BRICKS // SENDERS, senders, 0, unroll=4)
    return [source[0 : 3 * size] + source[3 * size : 6 * size] for source, _, size in sources]


def interleave(first, last):
    first, last = first.reshape(6, 8, 128), last.reshape(6, 8, 128)
    low = lax.broadcasted_iota(jnp.int32, (6, 8, 128), 1) < 4
    even = jnp.where(low, first, pltpu.roll(last, 4, 1))
    odd = jnp.where(low, pltpu.roll(first, 4, 1), last)
    return jnp.concatenate([value[i] for i in range(6) for value in (even, odd)], axis=0)


def planes(value):
    return value.reshape(3, 4, 8, 128)


def is_even(axis):
    return lax.axis_index(axis) % 2 == 0


def in_order(axis, near, far):
    even = is_even(axis)
    return jnp.where(even, far, near), jnp.where(even, near, far)


def toward(value, near, count=3):
    upward = is_even("vessel") if near else ~is_even("vessel")
    return jnp.where(upward, value[:, 4 - count : 4], value[:, 0:count])


def write_messages(tissues, sources, near_ref, far_ref):
    for i, (value, source) in enumerate(zip(tissues, sources)):
        here = slice(8 * i, 8 * i + 8)
        value, source = planes(value), planes(source)
        for ref, near in ((near_ref, True), (far_ref, False)):
            ref[:, 0:4, here] = value
            ref[:, 4:7, here] = toward(source, near)


def first_scatter_kernel(
    recv_ref, tissue_ref, around_ref, rate_ref, rate_near_ref, rate_far_ref, near_ref, far_ref, sources_ref, *sums
):
    sources = scatter_slots(recv_ref, [(sums[i], (16 * i, 16 * i + 8), 32) for i in range(3)])
    for i in range(3):
        sources_ref[i] = sources[i]
    write_messages([tissue_ref[...], around_ref[0], around_ref[1]], sources, near_ref, far_ref)
    before, after = in_order("tissue", rate_near_ref[...], rate_far_ref[...])
    for i, value in enumerate((rate_ref[...], after, before)):
        here = slice(8 * i, 8 * i + 8)
        near_ref[:, 7:10, here] = toward(planes(value), True)
        far_ref[:, 7:10, here] = toward(planes(value), False)


def second_scatter_kernel(recv_ref, tissue_ref, side_ref, near_ref, far_ref, sources_ref, *sums):
    own, first, last = scatter_slots(
        recv_ref, [(sums[i], (16 * i, 16 * i + 8), 32 if i == 0 else 16) for i in range(3)]
    )
    sources = [own, interleave(first, last)]
    for i in range(2):
        sources_ref[i] = sources[i]
    tissue, side = planes(tissue_ref[...]), planes(side_ref[...])
    own, beyond = planes(sources[0]), planes(sources[1])
    for ref, near in ((near_ref, True), (far_ref, False)):
        ref[:, 0:4] = tissue
        ref[:, 4:7] = toward(own, near)
        ref[:, 7:10] = toward(side, near)
        ref[:, 10:12] = toward(beyond, near, 2)


def fill(now, source, tissues, sources):
    for k in range(3):
        for i in range(len(tissues)):
            now[k, 4:8, 8 * i : 8 * i + 8] = planes(tissues[i])[k]
            source[k, 4:8, 8 * i : 8 * i + 8] = planes(sources[i])[k]


def run_sweeps(now, later, source, inverse, produced):
    count = now.shape[2]
    lane = lanes_of((count, 128))
    old, new = now, later
    for sweep in range(1, SWEEPS + 1):
        for k in range(3):
            for z in range(sweep, 12 - sweep):
                middle = old[k, z]
                total = old[k, z - 1] + old[k, z + 1]
                total = total + pltpu.roll(middle, 1, 0) + pltpu.roll(middle, count - 1, 0)
                total = total + jnp.where(lane > 0, pltpu.roll(middle, 1, 1), 0.0)
                total = total + jnp.where(lane < 127, pltpu.roll(middle, 127, 1), 0.0)
                total = source[k, z] + DIFFUSION[k] * total
                if k == 2:
                    total = total + produced[z] * old[1, z]
                new[k, z] = total * inverse[k, z]
        old, new = new, old
    return old


def beside(after, before):
    low = lax.broadcasted_iota(jnp.int32, after.shape, after.ndim - 2) < 4
    return jnp.where(low, after, before)


def first_sweeps_kernel(
    near, far, tissue_ref, around_ref, rate_ref, rate_near_ref, rate_far_ref, sources_ref, recv_ref, ends_ref,
    out_ref, side_ref, inverse_ref, produced_ref, send_ref, now, later, source, inverse, produced,
):
    tissues = [tissue_ref[...], around_ref[0], around_ref[1]]
    fill(now, source, tissues, [sources_ref[i] for i in range(3)])
    before, after = in_order("tissue", rate_near_ref[...], rate_far_ref[...])
    for k in range(3):
        now[k, 0:4], now[k, 8:12] = in_order("vessel", near[k, 0:4], far[k, 0:4])
        source[k, 1:4], source[k, 8:11] = in_order("vessel", near[k, 4:7], far[k, 4:7])
        rates = [planes(value)[k] for value in (rate_ref[...], after, before)]
        below, above = in_order("vessel", near[k, 7:10], far[k, 7:10])
        for z in range(1, 11):
            if z < 4:
                rate = below[z - 1]
            elif z < 8:
                rate = jnp.concatenate([value[z - 4] for value in rates], axis=0)
            else:
                rate = above[z - 8]
            value = jnp.where(rate > 0.0, 1.0 / (6.0 * DIFFUSION[k] + rate), 0.0)
            inverse[k, z] = value
            inverse_ref[k, z, 0:8] = value[0:8]
            inverse_ref[k, z, 8:16] = beside(value[8:16], value[16:24])
            if k == 1:
                rate = 2.0 * rate
                produced[z] = rate
                produced_ref[z, 0:8] = rate[0:8]
                produced_ref[z, 8:16] = beside(rate[8:16], rate[16:24])
    final = run_sweeps(now, later, source, inverse, produced)
    brick = final[:, 4:8, 0:8].reshape(96, 128)
    out_ref[...] = brick
    side_ref[...] = beside(final[:, 4:8, 8:16], final[:, 4:8, 16:24]).reshape(96, 128)
    brick_split = split_brick(brick)
    ends = ends_ref[0, 0:1]
    for part in range(1, PARTS):
        ends = ends + pltpu.roll(ends_ref[part], 16 * part, 1)[0:1]

    def receiver(s, carry):
        cells = [recv_ref[s, 4 * b + 3 : 4 * b + 4, :].astype(jnp.int32) for b in range(4)]
        found = gather_slots(brick_split, cells)
        for pair in range(2):
            send_ref[s, 8 * pair : 8 * pair + 8] = pair_tile(
                [*found[2 * pair], ends, *found[2 * pair + 1], ends]
            )
        return carry

    lax.fori_loop(0, BRICKS, receiver, 0, unroll=4)


def second_sweeps_kernel(
    near, far, tissue_ref, side_ref, sources_ref, inverse, produced, out_ref, now, later, source
):
    fill(now, source, [tissue_ref[...], side_ref[...]], [sources_ref[i] for i in range(2)])
    zero = jnp.zeros((8, 128), F32)
    for k in range(3):
        below, above = in_order("vessel", near[k], far[k])
        now[k, 0:4, 0:8], now[k, 8:12, 0:8] = below[0:4], above[0:4]
        source[k, 1:4, 0:8], source[k, 8:11, 0:8] = below[4:7], above[4:7]
        now[k, 1:4, 8:16], now[k, 8:11, 8:16] = below[7:10], above[7:10]
        source[k, 2:4, 8:16], source[k, 8:10, 8:16] = below[10:12], above[10:12]
        now[k, 0, 8:16] = now[k, 11, 8:16] = zero
        source[k, 1, 8:16] = source[k, 10, 8:16] = zero
    final = run_sweeps(now, later, source, inverse, produced)
    out_ref[...] = final[:, 4:8, 0:8]


VMEM = pl.BlockSpec(memory_space=pltpu.VMEM)
SMEM = pl.BlockSpec(memory_space=pltpu.SMEM)
HBM = pl.BlockSpec(memory_space=pltpu.HBM)


def call(kernel, name, outs, args, scratch, spaces=None, out_spaces=None):
    spaces = spaces or [VMEM] * len(args)
    args = [
        arg if space is SMEM else pltpu.with_memory_space_constraint(arg, space.memory_space)
        for arg, space in zip(args, spaces)
    ]
    return pl.pallas_call(
        kernel,
        out_shape=[jax.ShapeDtypeStruct(out, F32) if isinstance(out, tuple) else out for out in outs],
        in_specs=spaces,
        out_specs=out_spaces or [VMEM] * len(outs),
        scratch_shapes=scratch,
        compiler_params=pltpu.CompilerParams(vmem_limit_bytes=VMEM_LIMIT),
        name=name,
    )(*args)


def shards(
    tissue_start,
    consumption,
    inlet,
    flow,
    permeability,
    intersection_count,
    intersection_segment,
    intersection_voxel,
    intersection_weight,
    upstream,
):
    def exchange(value, axis):
        return lax.all_to_all(value, axis, 0, 0, tiled=True)

    def swap(value, axis, first):
        starts = range(first, lax.axis_size(axis) - 1, 2)
        return lax.ppermute(value, axis, [pair for i in starts for pair in ((i, i + 1), (i + 1, i))])

    ring, large_ring = (3, 12, 16, 128), (3, 12, 24, 128)
    values_scratch = [pltpu.VMEM((2, BRICKS, 8, 128), F32)]

    bricks, tissue, rate = call(
        spread_kernel,
        "spread",
        [(BRICKS, 96, 128), (96, 128), (96, 128)],
        [tissue_start.reshape(96, 128), consumption.reshape(96, 128)],
        [pltpu.SemaphoreType.DMA((BRICKS + 2,))],
        [HBM] * 2,
        [HBM, VMEM, VMEM],
    )
    region = exchange(bricks, "tissue")
    rate_near, rate_far = swap(rate, "tissue", 0), swap(rate, "tissue", 1)
    slot_array = intersection_voxel.shape
    prepared = call(
        prepare_kernel,
        "prepare",
        [
            (7, BRICKS, 8, 128),
            jax.ShapeDtypeStruct((4, BRICKS, 128, 128), BF16),
        ],
        [
            intersection_segment,
            intersection_weight,
            intersection_voxel,
            flow,
            intersection_count,
            permeability,
            inlet,
        ],
        [
            pltpu.VMEM(slot_array, jnp.int32),
            pltpu.VMEM(slot_array, F32),
            pltpu.VMEM(slot_array, jnp.int32),
            pltpu.VMEM(flow.shape, F32),
            pltpu.SMEM(intersection_count.shape, jnp.int32),
            pltpu.SMEM(permeability.shape, F32),
            pltpu.SMEM(inlet.shape, F32),
            pltpu.SemaphoreType.DMA((7,)),
        ],
        [HBM] * 7,
    )
    region, rate_near, rate_far = lax.optimization_barrier((region, rate_near, rate_far))
    send, ends, around = call(
        first_solve_kernel,
        "first_solve",
        [(BRICKS, 48, 128), (PARTS, 8, 128), (2, 96, 128)],
        [region, *prepared],
        values_scratch,
    )
    received = exchange(send, "tissue")
    ends = exchange(ends, "vessel")
    near, far, sources = call(
        first_scatter_kernel,
        "first_scatter",
        [(3, 10, 24, 128), (3, 10, 24, 128), (3, 96, 128)],
        [received, tissue, around, rate, rate_near, rate_far],
        [pltpu.VMEM((192, 128), F32)] * 3,
    )
    near, far = swap(near, "vessel", 0), swap(far, "vessel", 1)
    tissue, side, inverse, produced, send = call(
        first_sweeps_kernel,
        "first_sweeps",
        [(96, 128), (96, 128), ring, ring[1:], (BRICKS, 16, 128)],
        [near, far, tissue, around, rate, rate_near, rate_far, sources, received, ends],
        [pltpu.VMEM(large_ring, F32)] * 4 + [pltpu.VMEM(large_ring[1:], F32)],
    )
    values = exchange(send, "tissue")
    send, vessel = call(
        second_solve_kernel,
        "second_solve",
        [(BRICKS, 48, 128), (3, 4, SEG)],
        [upstream, values, *prepared],
        values_scratch,
        [SMEM] + [VMEM] * 3,
    )
    received = exchange(send, "tissue")
    near, far, sources = call(
        second_scatter_kernel,
        "second_scatter",
        [(3, 12, 8, 128), (3, 12, 8, 128), (2, 96, 128)],
        [received, tissue, side],
        [pltpu.VMEM((rows, 128), F32) for rows in (192, 96, 96)],
    )
    near, far = swap(near, "vessel", 0), swap(far, "vessel", 1)
    (tissue,) = call(
        second_sweeps_kernel,
        "second_sweeps",
        [(3, 4, 8, 128)],
        [near, far, tissue, side, sources, inverse, produced],
        [pltpu.VMEM(ring, F32)] * 3,
    )
    return tissue, vessel


def solution(mesh):
    return jax.shard_map(
        shards,
        mesh=mesh,
        in_specs=(
            P(None, "vessel", "tissue", None),
            P(None, "vessel", "tissue", None),
            P(None, ("vessel", "tissue")),
            P(("vessel", "tissue"), None),
            P(),
            P(("vessel", "tissue"), None),
            P(("vessel", "tissue"), None, None),
            P(("vessel", "tissue"), None, None),
            P(("vessel", "tissue"), None, None),
            P(("vessel", "tissue")),
        ),
        out_specs=(P(None, "vessel", "tissue", None), P(None, ("vessel", "tissue"), None)),
        check_vma=False,
    )
```

```python
import jax
import jax.numpy as jnp
from jax import lax
from jax.experimental import pallas as pl
from jax.experimental.pallas import tpu as pltpu
from jax.sharding import PartitionSpec as P


SEG = 256
SWEEPS = 4
DIFFUSION = (1.0, 0.7, 0.7)
BRICKS = 16
PARTS = 8
F32 = jnp.float32
BF16 = jnp.bfloat16
VMEM_LIMIT = 16 * 1024 * 1024
SENDERS = 4
SCAN_STEPS = 4
CELLS, WEIGHTS, TABLES = 0, 4, 1
DECAY, GAIN, SCALE, INLET = 12, 13, 14, 15


def rows_of(shape):
    return lax.broadcasted_iota(jnp.int32, shape, 0)


def lanes_of(shape):
    return lax.broadcasted_iota(jnp.int32, shape, 1)


def matmul(lhs, rhs):
    return lax.dot_general(lhs, rhs, (((1,), (0,)), ((), ())), preferred_element_type=F32)


def matmul_nt(lhs, rhs):
    return lax.dot_general(lhs, rhs, (((1,), (1,)), ((), ())), preferred_element_type=F32)


def split(value):
    high = value.astype(BF16).astype(F32)
    return high, value - high


def packed(row):
    return jnp.broadcast_to(row, (16, 128)).astype(F32).astype(BF16)


def matches(index, size):
    row = rows_of((16, 128)).astype(F32).astype(BF16)
    wanted = packed(index)
    return [row + BF16(i) == wanted for i in range(0, size, 16)]


def onehot(index, size):
    one, zero = jnp.ones((16, 128), BF16), jnp.zeros((16, 128), BF16)
    return jnp.concatenate([jnp.where(hit, one, zero) for hit in matches(index, size)], axis=0)


def split_brick(brick):
    high, low = split(brick)
    return jnp.concatenate([high, low], axis=1).astype(BF16)


def gather_slots(brick_split, cells):
    hot = jnp.concatenate([onehot(cell & 127, 128) for cell in cells], axis=1)
    found = matmul(brick_split, jnp.concatenate([hot, hot], axis=0))
    values = []
    for i, cell in enumerate(cells):
        here = rows_of((32, 128)) == (cell >> 7)
        part = found[:, i * 128 : (i + 1) * 128]
        values.append(
            [
                jnp.sum(jnp.where(here, part[32 * k : 32 * k + 32], 0.0), axis=0, keepdims=True)
                for k in range(3)
            ]
        )
    return values


def pair_tile(rows):
    row = rows_of((8, 128))
    tile = jnp.broadcast_to(rows[7], (8, 128))
    for i in range(7):
        tile = jnp.where(row == i, rows[i], tile)
    return tile


def spread_kernel(tissue_hbm, rate_hbm, bricks_hbm, tissue_ref, rate_ref, sems):
    arguments = [
        pltpu.make_async_copy(tissue_hbm, tissue_ref, sems.at[BRICKS]),
        pltpu.make_async_copy(rate_hbm, rate_ref, sems.at[BRICKS + 1]),
    ]
    bricks = [pltpu.make_async_copy(tissue_ref, bricks_hbm.at[t], sems.at[t]) for t in range(BRICKS)]
    for copy in arguments:
        copy.start()
    arguments[0].wait()
    for copy in bricks:
        copy.start()
    arguments[1].wait()
    for copy in bricks:
        copy.wait()


def wide(ref, i):
    return jnp.concatenate([ref[i, t] for t in range(BRICKS)], axis=1)


def pair_slots(slots, t, kind, pair):
    even = kind + 2 * pair
    return jnp.where(rows_of((8, 128)) < 4, slots[0, t, even : even + 1], slots[0, t, even + 1 : even + 2])


def pair_weights(slots, pair):
    return jnp.concatenate([pair_slots(slots, t, WEIGHTS, pair) for t in range(BRICKS)], axis=1)


def read_table(slots, i):
    tiles = [slots[TABLES + i // 4, 4 * (i % 4) + j] for j in range(4)]
    return jnp.concatenate([jnp.concatenate(tiles[:2], axis=1), jnp.concatenate(tiles[2:], axis=1)], axis=0)


def write_table(slots, i, value):
    for j in range(4):
        rows, lanes = 8 * (j // 2), 128 * (j % 2)
        slots[TABLES + i // 4, 4 * (i % 4) + j] = value[rows : rows + 8, lanes : lanes + 128]


def by_half(rows, upper):
    high, low = split(rows)
    return jnp.concatenate(
        [
            jnp.where(upper, 0.0, high),
            jnp.where(upper, 0.0, low),
            jnp.where(upper, high, 0.0),
            jnp.where(upper, low, 0.0),
        ],
        axis=0,
    ).astype(BF16)


def sum_segments(rows, pair, weights, hots):
    lhs = by_half(rows, weights < 0.0)
    sums = []
    for block in (2 * pair, 2 * pair + 1):
        part = matmul_nt(lhs, wide(hots, block))
        sums.append(jnp.concatenate([part[0:8] + part[8:16], part[16:24] + part[24:32]], axis=1))
    return jnp.where(rows_of((8, SEG)) < 4, sums[0], sums[1])


def column_of(ref, at):
    row = rows_of((16, 1))
    column = jnp.zeros((16, 1), F32)
    for block in range(4):
        for k in range(3):
            column = jnp.where(row == 4 * block + k, ref[at(block, k)], column)
    return column


def prepare_kernel(*refs):
    slots, hots = refs[7:9]
    segment_ref, weight_ref, voxel_ref, flow_ref, count_ref, perm_ref, inlet_ref = refs[9:16]
    sems = refs[16]
    copies = [pltpu.make_async_copy(refs[i], refs[9 + i], sems.at[i]) for i in range(7)]
    for copy in copies:
        copy.start()
    for copy in copies:
        copy.wait()
    lane = lanes_of((1, 128))

    def brick(t, carry):
        for block in range(4):
            weight = weight_ref[block, pl.ds(t, 1), :]
            weight = jnp.where(lane < count_ref[block, t], weight, 0.0)
            segment = segment_ref[block, pl.ds(t, 1), :]
            hots[block, t] = onehot(segment & 127, 128)
            slots[0, t, CELLS + block : CELLS + block + 1] = voxel_ref[block, pl.ds(t, 1), :].astype(F32)
            slots[0, t, WEIGHTS + block : WEIGHTS + block + 1] = jnp.where(segment >= 128, -weight, weight)
        return carry

    lax.fori_loop(0, BRICKS, brick, 0, unroll=4)
    row = rows_of((8, SEG))
    scale = jnp.broadcast_to(column_of(perm_ref, lambda block, k: k), (16, SEG))
    write_table(slots, SCALE, scale)
    inlet = column_of(inlet_ref, lambda block, k: (k, block))
    write_table(slots, INLET, jnp.broadcast_to(inlet, (16, SEG)))
    weight_sums, speeds = [], []
    for pair in range(2):
        weights = pair_weights(slots, pair)
        weight_sums.append(sum_segments(jnp.abs(weights), pair, weights, hots))
        speeds.append(jnp.where(row < 4, flow_ref[2 * pair : 2 * pair + 1], flow_ref[2 * pair + 1 : 2 * pair + 2]))
    speed = jnp.concatenate(speeds, axis=0)
    inverse = 1.0 / (speed + scale * jnp.concatenate(weight_sums, axis=0))
    decay = speed * inverse
    write_table(slots, DECAY, decay)
    write_table(slots, GAIN, scale * inverse)
    lane = lanes_of(decay.shape)
    for i in range(SCAN_STEPS):
        step = 4**i
        once = jnp.where(lane >= step, decay, 0.0)
        twice = once * pltpu.roll(once, step, 1)
        thrice = once * pltpu.roll(twice, step, 1)
        for j, value in enumerate((once, twice, thrice)):
            write_table(slots, 3 * i + j, value)
        decay = thrice * pltpu.roll(once, 3 * step, 1)


def solve_blocks(inflow, values, slots, hots, send_ref, narrow):
    gathered = []
    for pair in range(2):
        weights = pair_weights(slots, pair)
        gathered.append(sum_segments(wide(values, pair) * jnp.abs(weights), pair, weights, hots))
    vessel = read_table(slots, GAIN) * jnp.concatenate(gathered, axis=0)
    vessel = vessel + jnp.where(lanes_of((16, SEG)) == 0, read_table(slots, DECAY) * inflow, 0.0)
    for i in range(SCAN_STEPS):
        earlier = [read_table(slots, 3 * i + j) * pltpu.roll(vessel, (j + 1) * 4**i, 1) for j in range(3)]
        vessel = (vessel + earlier[0]) + (earlier[1] + earlier[2])

    send_ref[0, 32:48] = jnp.zeros((16, 128), F32)
    send_ref[BRICKS - 1, 16:32] = jnp.zeros((16, 128), F32)
    tile_row = rows_of((8, 128))
    scale = read_table(slots, SCALE)[0:8, 0:128]
    for pair in range(2):
        high, low = split(vessel[8 * pair : 8 * pair + 8])
        lhs = jnp.concatenate(
            [high[:, :128], low[:, :128], high[:, 128:], low[:, 128:]], axis=0
        ).astype(BF16)
        found = [matmul(lhs, wide(hots, block)) for block in (2 * pair, 2 * pair + 1)]
        for t in range(BRICKS):
            weights = pair_slots(slots, t, WEIGHTS, pair)
            part = [value[:, t * 128 : (t + 1) * 128] for value in found]
            part = [jnp.where(tile_row < 4, part[0][8 * i : 8 * i + 8], part[1][8 * i : 8 * i + 8]) for i in range(4)]
            at_slot = jnp.where(weights < 0.0, part[2] + part[3], part[0] + part[1])
            flux = scale * jnp.abs(weights) * (at_slot - values[pair, t])
            cell = pair_slots(slots, t, CELLS, pair)
            cell_row = (tile_row & 3) == 3
            here = slice(8 * pair, 8 * pair + 8)
            own = jnp.where(cell_row, cell, flux)
            first = last = own
            if narrow:
                is_first = ((cell.astype(jnp.int32) >> 7) & 7) < 4
                first = jnp.where(cell_row | is_first, own, 0.0)
                last = jnp.where(is_first & ~cell_row, 0.0, own)
            send_ref[t, here] = own
            if t > 0:
                send_ref[t - 1, 16 + 8 * pair : 24 + 8 * pair] = first
            if t < BRICKS - 1:
                send_ref[t + 1, 32 + 8 * pair : 40 + 8 * pair] = last
    return vessel


def first_solve_kernel(region_ref, slots, hots, send_ref, ends_ref, around_ref, values):
    def brick(t, carry):
        cells = [slots[0, t, CELLS + block : CELLS + block + 1].astype(jnp.int32) for block in range(4)]
        found = gather_slots(split_brick(region_ref[t]), cells)
        for pair in range(2):
            values[pair, t] = pair_tile([*found[2 * pair], 0.0, *found[2 * pair + 1], 0.0])
        return carry

    lax.fori_loop(0, BRICKS, brick, 0, unroll=4)
    vessel = solve_blocks(read_table(slots, INLET), values, slots, hots, send_ref, False)
    spot = lanes_of((16, 128)) == rows_of((16, 128))
    ends = jnp.sum(jnp.where(spot, vessel[:, SEG - 1 : SEG], 0.0), axis=0, keepdims=True)
    ends_ref[...] = jnp.broadcast_to(ends[None], (PARTS, 8, 128))
    t = lax.axis_index("tissue")
    around_ref[0] = jnp.where(t < BRICKS - 1, region_ref[jnp.minimum(t + 1, BRICKS - 1)], 0.0)
    around_ref[1] = jnp.where(t > 0, region_ref[jnp.maximum(t - 1, 0)], 0.0)


def second_solve_kernel(upstream_ref, values_ref, slots, hots, send_ref, vessel_ref, values):
    spare = (rows_of((8, 128)) & 3) == 3
    for t in range(BRICKS):
        for pair in range(2):
            values[pair, t] = jnp.where(spare, 0.0, values_ref[t, 8 * pair : 8 * pair + 8])
    row, lane = rows_of((16, 128)), lanes_of((16, 128))
    picked = jnp.zeros((16, 128), F32)
    for block in range(4):
        feeder = upstream_ref[block]
        device = feeder >> 2
        ends = values_ref[device & 15, 3:4, :]
        spot = (device >> 4) * 16 + (feeder & 3) * 4
        picked = jnp.where(((row >> 2) == block) & (lane == spot + (row & 3)), ends, picked)
    inflow = 0.5 * (read_table(slots, INLET) + jnp.sum(picked, axis=1, keepdims=True))
    vessel = solve_blocks(inflow, values, slots, hots, send_ref, True)
    for block in range(4):
        for k in range(3):
            vessel_ref[k, block : block + 1, :] = vessel[4 * block + k : 4 * block + k + 1]


def scatter_slots(recv_ref, sources):
    zero = jnp.zeros((16, 128), BF16)
    for source, _, _ in sources:
        source[...] = jnp.zeros(source.shape, F32)

    def senders(i, carry):
        for source, tiles, size in sources:
            hots, parts = [], []
            for q in range(SENDERS):
                s = i * SENDERS + q
                for start in tiles:
                    for base in (start, start + 4):
                        cell = recv_ref[s, base + 3 : base + 4, :].astype(jnp.int32)
                        hots.append(onehot(cell & 127, 128))
                        row = cell >> 7
                        if size == 16:
                            row = (row >> 3) * 4 + (row & 3)
                        here = matches(row, size)
                        highs, lows = [], []
                        for k in range(3):
                            flux = jnp.broadcast_to(recv_ref[s, base + k : base + k + 1, :], (16, 128))
                            high = flux.astype(BF16)
                            low = (flux - high.astype(F32)).astype(BF16)
                            highs += [jnp.where(hit, high, zero) for hit in here]
                            lows += [jnp.where(hit, low, zero) for hit in here]
                        parts.append(jnp.concatenate(highs + lows, axis=0))
            source[...] += matmul_nt(jnp.concatenate(parts, axis=1), jnp.concatenate(hots, axis=1))
        return carry

    lax.fori_loop(0, BRICKS // SENDERS, senders, 0, unroll=4)
    return [source[0 : 3 * size] + source[3 * size : 6 * size] for source, _, size in sources]


def interleave(first, last):
    first, last = first.reshape(6, 8, 128), last.reshape(6, 8, 128)
    low = lax.broadcasted_iota(jnp.int32, (6, 8, 128), 1) < 4
    even = jnp.where(low, first, pltpu.roll(last, 4, 1))
    odd = jnp.where(low, pltpu.roll(first, 4, 1), last)
    return jnp.concatenate([value[i] for i in range(6) for value in (even, odd)], axis=0)


def planes(value):
    return value.reshape(3, 4, 8, 128)


def is_even(axis):
    return lax.axis_index(axis) % 2 == 0


def in_order(axis, near, far):
    even = is_even(axis)
    return jnp.where(even, far, near), jnp.where(even, near, far)


def toward(value, near, count=3):
    upward = is_even("vessel") if near else ~is_even("vessel")
    return jnp.where(upward, value[:, 4 - count : 4], value[:, 0:count])


def write_messages(tissues, sources, near_ref, far_ref):
    for i, (value, source) in enumerate(zip(tissues, sources)):
        here = slice(8 * i, 8 * i + 8)
        value, source = planes(value), planes(source)
        for ref, near in ((near_ref, True), (far_ref, False)):
            ref[:, 0:4, here] = value
            ref[:, 4:7, here] = toward(source, near)


def first_scatter_kernel(
    recv_ref, tissue_ref, around_ref, rate_ref, rate_near_ref, rate_far_ref, near_ref, far_ref, sources_ref, *sums
):
    sources = scatter_slots(recv_ref, [(sums[i], (16 * i, 16 * i + 8), 32) for i in range(3)])
    for i in range(3):
        sources_ref[i] = sources[i]
    write_messages([tissue_ref[...], around_ref[0], around_ref[1]], sources, near_ref, far_ref)
    before, after = in_order("tissue", rate_near_ref[...], rate_far_ref[...])
    for i, value in enumerate((rate_ref[...], after, before)):
        here = slice(8 * i, 8 * i + 8)
        near_ref[:, 7:10, here] = toward(planes(value), True)
        far_ref[:, 7:10, here] = toward(planes(value), False)


def second_scatter_kernel(recv_ref, tissue_ref, side_ref, near_ref, far_ref, sources_ref, *sums):
    own, first, last = scatter_slots(
        recv_ref, [(sums[i], (16 * i, 16 * i + 8), 32 if i == 0 else 16) for i in range(3)]
    )
    sources = [own, interleave(first, last)]
    for i in range(2):
        sources_ref[i] = sources[i]
    tissue, side = planes(tissue_ref[...]), planes(side_ref[...])
    own, beyond = planes(sources[0]), planes(sources[1])
    for ref, near in ((near_ref, True), (far_ref, False)):
        ref[:, 0:4] = tissue
        ref[:, 4:7] = toward(own, near)
        ref[:, 7:10] = toward(side, near)
        ref[:, 10:12] = toward(beyond, near, 2)


def fill(now, source, tissues, sources):
    for k in range(3):
        for i in range(len(tissues)):
            now[k, 4:8, 8 * i : 8 * i + 8] = planes(tissues[i])[k]
            source[k, 4:8, 8 * i : 8 * i + 8] = planes(sources[i])[k]


def run_sweeps(now, later, source, inverse, produced):
    count = now.shape[2]
    lane = lanes_of((count, 128))
    old, new = now, later
    for sweep in range(1, SWEEPS + 1):
        for k in range(3):
            for z in range(sweep, 12 - sweep):
                middle = old[k, z]
                total = old[k, z - 1] + old[k, z + 1]
                total = total + pltpu.roll(middle, 1, 0) + pltpu.roll(middle, count - 1, 0)
                total = total + jnp.where(lane > 0, pltpu.roll(middle, 1, 1), 0.0)
                total = total + jnp.where(lane < 127, pltpu.roll(middle, 127, 1), 0.0)
                total = source[k, z] + DIFFUSION[k] * total
                if k == 2:
                    total = total + produced[z] * old[1, z]
                new[k, z] = total * inverse[k, z]
        old, new = new, old
    return old


def beside(after, before):
    low = lax.broadcasted_iota(jnp.int32, after.shape, after.ndim - 2) < 4
    return jnp.where(low, after, before)


def first_sweeps_kernel(
    far, near, tissue_ref, around_ref, rate_ref, rate_near_ref, rate_far_ref, sources_ref, recv_ref, ends_ref,
    out_ref, side_ref, inverse_ref, produced_ref, send_ref, now, later, source, inverse, produced,
):
    tissues = [tissue_ref[...], around_ref[0], around_ref[1]]
    fill(now, source, tissues, [sources_ref[i] for i in range(3)])
    before, after = in_order("tissue", rate_near_ref[...], rate_far_ref[...])
    for k in range(3):
        now[k, 0:4], now[k, 8:12] = in_order("vessel", near[k, 0:4], far[k, 0:4])
        source[k, 1:4], source[k, 8:11] = in_order("vessel", near[k, 4:7], far[k, 4:7])
        rates = [planes(value)[k] for value in (rate_ref[...], after, before)]
        below, above = in_order("vessel", near[k, 7:10], far[k, 7:10])
        for z in range(1, 11):
            if z < 4:
                rate = below[z - 1]
            elif z < 8:
                rate = jnp.concatenate([value[z - 4] for value in rates], axis=0)
            else:
                rate = above[z - 8]
            value = jnp.where(rate > 0.0, 1.0 / (6.0 * DIFFUSION[k] + rate), 0.0)
            inverse[k, z] = value
            inverse_ref[k, z, 0:8] = value[0:8]
            inverse_ref[k, z, 8:16] = beside(value[8:16], value[16:24])
            if k == 1:
                rate = 2.0 * rate
                produced[z] = rate
                produced_ref[z, 0:8] = rate[0:8]
                produced_ref[z, 8:16] = beside(rate[8:16], rate[16:24])
    final = run_sweeps(now, later, source, inverse, produced)
    brick = final[:, 4:8, 0:8].reshape(96, 128)
    out_ref[...] = brick
    side_ref[...] = beside(final[:, 4:8, 8:16], final[:, 4:8, 16:24]).reshape(96, 128)
    brick_split = split_brick(brick)
    ends = ends_ref[0, 0:1]
    for part in range(1, PARTS):
        ends = ends + pltpu.roll(ends_ref[part], 16 * part, 1)[0:1]

    def receiver(s, carry):
        cells = [recv_ref[s, 4 * b + 3 : 4 * b + 4, :].astype(jnp.int32) for b in range(4)]
        found = gather_slots(brick_split, cells)
        for pair in range(2):
            send_ref[s, 8 * pair : 8 * pair + 8] = pair_tile(
                [*found[2 * pair], ends, *found[2 * pair + 1], ends]
            )
        return carry

    lax.fori_loop(0, BRICKS, receiver, 0, unroll=4)


def second_sweeps_kernel(
    far, near, tissue_ref, side_ref, sources_ref, inverse, produced, out_ref, now, later, source
):
    fill(now, source, [tissue_ref[...], side_ref[...]], [sources_ref[i] for i in range(2)])
    zero = jnp.zeros((8, 128), F32)
    for k in range(3):
        below, above = in_order("vessel", near[k], far[k])
        now[k, 0:4, 0:8], now[k, 8:12, 0:8] = below[0:4], above[0:4]
        source[k, 1:4, 0:8], source[k, 8:11, 0:8] = below[4:7], above[4:7]
        now[k, 1:4, 8:16], now[k, 8:11, 8:16] = below[7:10], above[7:10]
        source[k, 2:4, 8:16], source[k, 8:10, 8:16] = below[10:12], above[10:12]
        now[k, 0, 8:16] = now[k, 11, 8:16] = zero
        source[k, 1, 8:16] = source[k, 10, 8:16] = zero
    final = run_sweeps(now, later, source, inverse, produced)
    out_ref[...] = final[:, 4:8, 0:8]


VMEM = pl.BlockSpec(memory_space=pltpu.VMEM)
SMEM = pl.BlockSpec(memory_space=pltpu.SMEM)
HBM = pl.BlockSpec(memory_space=pltpu.HBM)


def call(kernel, name, outs, args, scratch, spaces=None, out_spaces=None):
    spaces = spaces or [VMEM] * len(args)
    args = [
        arg if space is SMEM else pltpu.with_memory_space_constraint(arg, space.memory_space)
        for arg, space in zip(args, spaces)
    ]
    return pl.pallas_call(
        kernel,
        out_shape=[jax.ShapeDtypeStruct(out, F32) if isinstance(out, tuple) else out for out in outs],
        in_specs=spaces,
        out_specs=out_spaces or [VMEM] * len(outs),
        scratch_shapes=scratch,
        compiler_params=pltpu.CompilerParams(vmem_limit_bytes=VMEM_LIMIT),
        name=name,
    )(*args)


def shards(
    tissue_start,
    consumption,
    inlet,
    flow,
    permeability,
    intersection_count,
    intersection_segment,
    intersection_voxel,
    intersection_weight,
    upstream,
):
    def exchange(value, axis):
        return lax.all_to_all(value, axis, 0, 0, tiled=True)

    def swap(value, axis, first):
        starts = range(first, lax.axis_size(axis) - 1, 2)
        return lax.ppermute(value, axis, [pair for i in starts for pair in ((i, i + 1), (i + 1, i))])

    ring, large_ring = (3, 12, 16, 128), (3, 12, 24, 128)
    values_scratch = [pltpu.VMEM((2, BRICKS, 8, 128), F32)]

    bricks, tissue, rate = call(
        spread_kernel,
        "spread",
        [(BRICKS, 96, 128), (96, 128), (96, 128)],
        [tissue_start.reshape(96, 128), consumption.reshape(96, 128)],
        [pltpu.SemaphoreType.DMA((BRICKS + 2,))],
        [HBM] * 2,
        [HBM, VMEM, VMEM],
    )
    region = exchange(bricks, "tissue")
    rate_near, rate_far = swap(rate, "tissue", 0), swap(rate, "tissue", 1)
    slot_array = intersection_voxel.shape
    prepared = call(
        prepare_kernel,
        "prepare",
        [
            (5, BRICKS, 8, 128),
            jax.ShapeDtypeStruct((4, BRICKS, 128, 128), BF16),
        ],
        [
            intersection_segment,
            intersection_weight,
            intersection_voxel,
            flow,
            intersection_count,
            permeability,
            inlet,
        ],
        [
            pltpu.VMEM(slot_array, jnp.int32),
            pltpu.VMEM(slot_array, F32),
            pltpu.VMEM(slot_array, jnp.int32),
            pltpu.VMEM(flow.shape, F32),
            pltpu.SMEM(intersection_count.shape, jnp.int32),
            pltpu.SMEM(permeability.shape, F32),
            pltpu.SMEM(inlet.shape, F32),
            pltpu.SemaphoreType.DMA((7,)),
        ],
        [HBM] * 7,
    )
    region, rate_near, rate_far = lax.optimization_barrier((region, rate_near, rate_far))
    send, ends, around = call(
        first_solve_kernel,
        "first_solve",
        [(BRICKS, 48, 128), (PARTS, 8, 128), (2, 96, 128)],
        [region, *prepared],
        values_scratch,
    )
    received = exchange(send, "tissue")
    ends = exchange(ends, "vessel")
    near, far, sources = call(
        first_scatter_kernel,
        "first_scatter",
        [(3, 10, 24, 128), (3, 10, 24, 128), (3, 96, 128)],
        [received, tissue, around, rate, rate_near, rate_far],
        [pltpu.VMEM((192, 128), F32)] * 3,
    )
    far, near = swap(far, "vessel", 1), swap(near, "vessel", 0)
    tissue, side, inverse, produced, send = call(
        first_sweeps_kernel,
        "first_sweeps",
        [(96, 128), (96, 128), ring, ring[1:], (BRICKS, 16, 128)],
        [far, near, tissue, around, rate, rate_near, rate_far, sources, received, ends],
        [pltpu.VMEM(large_ring, F32)] * 4 + [pltpu.VMEM(large_ring[1:], F32)],
    )
    values = exchange(send, "tissue")
    send, vessel = call(
        second_solve_kernel,
        "second_solve",
        [(BRICKS, 48, 128), (3, 4, SEG)],
        [upstream, values, *prepared],
        values_scratch,
        [SMEM] + [VMEM] * 3,
    )
    received = exchange(send, "tissue")
    near, far, sources = call(
        second_scatter_kernel,
        "second_scatter",
        [(3, 12, 8, 128), (3, 12, 8, 128), (2, 96, 128)],
        [received, tissue, side],
        [pltpu.VMEM((rows, 128), F32) for rows in (192, 96, 96)],
    )
    far, near = swap(far, "vessel", 1), swap(near, "vessel", 0)
    (tissue,) = call(
        second_sweeps_kernel,
        "second_sweeps",
        [(3, 4, 8, 128)],
        [far, near, tissue, side, sources, inverse, produced],
        [pltpu.VMEM(ring, F32)] * 3,
    )
    return tissue, vessel


def solution(mesh):
    return jax.shard_map(
        shards,
        mesh=mesh,
        in_specs=(
            P(None, "vessel", "tissue", None),
            P(None, "vessel", "tissue", None),
            P(None, ("vessel", "tissue")),
            P(("vessel", "tissue"), None),
            P(),
            P(("vessel", "tissue"), None),
            P(("vessel", "tissue"), None, None),
            P(("vessel", "tissue"), None, None),
            P(("vessel", "tissue"), None, None),
            P(("vessel", "tissue")),
        ),
        out_specs=(P(None, "vessel", "tissue", None), P(None, ("vessel", "tissue"), None)),
        check_vma=False,
    )
```

```python
import jax
import jax.numpy as jnp
from jax import lax
from jax.experimental import pallas as pl
from jax.experimental.pallas import tpu as pltpu
from jax.sharding import PartitionSpec as P


SEG = 256
SWEEPS = 4
DIFFUSION = (1.0, 0.7, 0.7)
BRICKS = 16
PARTS = 8
F32 = jnp.float32
BF16 = jnp.bfloat16
VMEM_LIMIT = 16 * 1024 * 1024
SENDERS = 4
SCAN_STEPS = 4
CELLS, WEIGHTS, TABLES = 0, 4, 1
DECAY, GAIN, SCALE, INLET = 12, 13, 14, 15


def rows_of(shape):
    return lax.broadcasted_iota(jnp.int32, shape, 0)


def lanes_of(shape):
    return lax.broadcasted_iota(jnp.int32, shape, 1)


def matmul(lhs, rhs):
    return lax.dot_general(lhs, rhs, (((1,), (0,)), ((), ())), preferred_element_type=F32)


def matmul_nt(lhs, rhs):
    return lax.dot_general(lhs, rhs, (((1,), (1,)), ((), ())), preferred_element_type=F32)


def split(value):
    high = value.astype(BF16).astype(F32)
    return high, value - high


def packed(row):
    return jnp.broadcast_to(row, (16, 128)).astype(F32).astype(BF16)


def matches(index, size):
    row = rows_of((16, 128)).astype(F32).astype(BF16)
    wanted = packed(index)
    return [row + BF16(i) == wanted for i in range(0, size, 16)]


def onehot(index, size):
    one, zero = jnp.ones((16, 128), BF16), jnp.zeros((16, 128), BF16)
    return jnp.concatenate([jnp.where(hit, one, zero) for hit in matches(index, size)], axis=0)


def split_brick(brick):
    high, low = split(brick)
    return jnp.concatenate([high, low], axis=1).astype(BF16)


def gather_slots(brick_split, cells):
    hot = jnp.concatenate([onehot(cell & 127, 128) for cell in cells], axis=1)
    found = matmul(brick_split, jnp.concatenate([hot, hot], axis=0))
    values = []
    for i, cell in enumerate(cells):
        here = rows_of((32, 128)) == (cell >> 7)
        part = found[:, i * 128 : (i + 1) * 128]
        values.append(
            [
                jnp.sum(jnp.where(here, part[32 * k : 32 * k + 32], 0.0), axis=0, keepdims=True)
                for k in range(3)
            ]
        )
    return values


def pair_tile(rows):
    row = rows_of((8, 128))
    tile = jnp.broadcast_to(rows[7], (8, 128))
    for i in range(7):
        tile = jnp.where(row == i, rows[i], tile)
    return tile


def spread_kernel(tissue_hbm, rate_hbm, bricks_hbm, tissue_ref, rate_ref, sems):
    arguments = [
        pltpu.make_async_copy(tissue_hbm, tissue_ref, sems.at[BRICKS]),
        pltpu.make_async_copy(rate_hbm, rate_ref, sems.at[BRICKS + 1]),
    ]
    bricks = [pltpu.make_async_copy(tissue_ref, bricks_hbm.at[t], sems.at[t]) for t in range(BRICKS)]
    for copy in arguments:
        copy.start()
    arguments[0].wait()
    for copy in bricks:
        copy.start()
    arguments[1].wait()
    for copy in bricks:
        copy.wait()


def wide(ref, i):
    return jnp.concatenate([ref[i, t] for t in range(BRICKS)], axis=1)


def pair_slots(slots, t, kind, pair):
    even = kind + 2 * pair
    return jnp.where(rows_of((8, 128)) < 4, slots[0, t, even : even + 1], slots[0, t, even + 1 : even + 2])


def pair_weights(slots, pair):
    return jnp.concatenate([pair_slots(slots, t, WEIGHTS, pair) for t in range(BRICKS)], axis=1)


def read_table(slots, i):
    tiles = [slots[TABLES + i // 4, 4 * (i % 4) + j] for j in range(4)]
    return jnp.concatenate([jnp.concatenate(tiles[:2], axis=1), jnp.concatenate(tiles[2:], axis=1)], axis=0)


def write_table(slots, i, value):
    for j in range(4):
        rows, lanes = 8 * (j // 2), 128 * (j % 2)
        slots[TABLES + i // 4, 4 * (i % 4) + j] = value[rows : rows + 8, lanes : lanes + 128]


def by_half(rows, upper):
    high, low = split(rows)
    return jnp.concatenate(
        [
            jnp.where(upper, 0.0, high),
            jnp.where(upper, 0.0, low),
            jnp.where(upper, high, 0.0),
            jnp.where(upper, low, 0.0),
        ],
        axis=0,
    ).astype(BF16)


def sum_segments(rows, pair, weights, hots):
    lhs = by_half(rows, weights < 0.0)
    sums = []
    for block in (2 * pair, 2 * pair + 1):
        part = matmul_nt(lhs, wide(hots, block))
        sums.append(jnp.concatenate([part[0:8] + part[8:16], part[16:24] + part[24:32]], axis=1))
    return jnp.where(rows_of((8, SEG)) < 4, sums[0], sums[1])


def column_of(ref, at):
    row = rows_of((16, 1))
    column = jnp.zeros((16, 1), F32)
    for block in range(4):
        for k in range(3):
            column = jnp.where(row == 4 * block + k, ref[at(block, k)], column)
    return column


def prepare_kernel(*refs):
    slots, hots = refs[7:9]
    segment_ref, weight_ref, voxel_ref, flow_ref, count_ref, perm_ref, inlet_ref = refs[9:16]
    sems = refs[16]
    copies = [pltpu.make_async_copy(refs[i], refs[9 + i], sems.at[i]) for i in range(7)]
    for copy in copies:
        copy.start()
    for copy in copies:
        copy.wait()
    lane = lanes_of((1, 128))

    def brick(t, carry):
        for block in range(4):
            weight = weight_ref[block, pl.ds(t, 1), :]
            weight = jnp.where(lane < count_ref[block, t], weight, 0.0)
            segment = segment_ref[block, pl.ds(t, 1), :]
            hots[block, t] = onehot(segment & 127, 128)
            slots[0, t, CELLS + block : CELLS + block + 1] = voxel_ref[block, pl.ds(t, 1), :].astype(F32)
            slots[0, t, WEIGHTS + block : WEIGHTS + block + 1] = jnp.where(segment >= 128, -weight, weight)
        return carry

    lax.fori_loop(0, BRICKS, brick, 0, unroll=4)
    row = rows_of((8, SEG))
    scale = jnp.broadcast_to(column_of(perm_ref, lambda block, k: k), (16, SEG))
    write_table(slots, SCALE, scale)
    inlet = column_of(inlet_ref, lambda block, k: (k, block))
    write_table(slots, INLET, jnp.broadcast_to(inlet, (16, SEG)))
    weight_sums, speeds = [], []
    for pair in range(2):
        weights = pair_weights(slots, pair)
        weight_sums.append(sum_segments(jnp.abs(weights), pair, weights, hots))
        speeds.append(jnp.where(row < 4, flow_ref[2 * pair : 2 * pair + 1], flow_ref[2 * pair + 1 : 2 * pair + 2]))
    speed = jnp.concatenate(speeds, axis=0)
    inverse = 1.0 / (speed + scale * jnp.concatenate(weight_sums, axis=0))
    decay = speed * inverse
    write_table(slots, DECAY, decay)
    write_table(slots, GAIN, scale * inverse)
    lane = lanes_of(decay.shape)
    for i in range(SCAN_STEPS):
        step = 4**i
        once = jnp.where(lane >= step, decay, 0.0)
        twice = once * pltpu.roll(once, step, 1)
        thrice = once * pltpu.roll(twice, step, 1)
        for j, value in enumerate((once, twice, thrice)):
            write_table(slots, 3 * i + j, value)
        decay = thrice * pltpu.roll(once, 3 * step, 1)


def solve_blocks(inflow, values, slots, hots, send_ref, narrow):
    gathered = []
    for pair in range(2):
        weights = pair_weights(slots, pair)
        gathered.append(sum_segments(wide(values, pair) * jnp.abs(weights), pair, weights, hots))
    vessel = read_table(slots, GAIN) * jnp.concatenate(gathered, axis=0)
    vessel = vessel + jnp.where(lanes_of((16, SEG)) == 0, read_table(slots, DECAY) * inflow, 0.0)
    for i in range(SCAN_STEPS):
        earlier = [read_table(slots, 3 * i + j) * pltpu.roll(vessel, (j + 1) * 4**i, 1) for j in range(3)]
        vessel = (vessel + earlier[0]) + (earlier[1] + earlier[2])

    send_ref[0, 32:48] = jnp.zeros((16, 128), F32)
    send_ref[BRICKS - 1, 16:32] = jnp.zeros((16, 128), F32)
    tile_row = rows_of((8, 128))
    scale = read_table(slots, SCALE)[0:8, 0:128]
    for pair in range(2):
        high, low = split(vessel[8 * pair : 8 * pair + 8])
        lhs = jnp.concatenate(
            [high[:, :128], low[:, :128], high[:, 128:], low[:, 128:]], axis=0
        ).astype(BF16)
        found = [matmul(lhs, wide(hots, block)) for block in (2 * pair, 2 * pair + 1)]
        for t in range(BRICKS):
            weights = pair_slots(slots, t, WEIGHTS, pair)
            part = [value[:, t * 128 : (t + 1) * 128] for value in found]
            part = [jnp.where(tile_row < 4, part[0][8 * i : 8 * i + 8], part[1][8 * i : 8 * i + 8]) for i in range(4)]
            at_slot = jnp.where(weights < 0.0, part[2] + part[3], part[0] + part[1])
            flux = scale * jnp.abs(weights) * (at_slot - values[pair, t])
            cell = pair_slots(slots, t, CELLS, pair)
            cell_row = (tile_row & 3) == 3
            here = slice(8 * pair, 8 * pair + 8)
            own = jnp.where(cell_row, cell, flux)
            first = last = own
            if narrow:
                is_first = ((cell.astype(jnp.int32) >> 7) & 7) < 4
                first = jnp.where(cell_row | is_first, own, 0.0)
                last = jnp.where(is_first & ~cell_row, 0.0, own)
            send_ref[t, here] = own
            if t > 0:
                send_ref[t - 1, 16 + 8 * pair : 24 + 8 * pair] = first
            if t < BRICKS - 1:
                send_ref[t + 1, 32 + 8 * pair : 40 + 8 * pair] = last
    return vessel


def first_solve_kernel(region_ref, slots, hots, send_ref, ends_ref, around_ref, values):
    def brick(t, carry):
        cells = [slots[0, t, CELLS + block : CELLS + block + 1].astype(jnp.int32) for block in range(4)]
        found = gather_slots(split_brick(region_ref[t]), cells)
        for pair in range(2):
            values[pair, t] = pair_tile([*found[2 * pair], 0.0, *found[2 * pair + 1], 0.0])
        return carry

    lax.fori_loop(0, BRICKS, brick, 0, unroll=BRICKS)
    vessel = solve_blocks(read_table(slots, INLET), values, slots, hots, send_ref, False)
    spot = lanes_of((16, 128)) == rows_of((16, 128))
    ends = jnp.sum(jnp.where(spot, vessel[:, SEG - 1 : SEG], 0.0), axis=0, keepdims=True)
    ends_ref[...] = jnp.broadcast_to(ends[None], (PARTS, 8, 128))
    t = lax.axis_index("tissue")
    around_ref[0] = jnp.where(t < BRICKS - 1, region_ref[jnp.minimum(t + 1, BRICKS - 1)], 0.0)
    around_ref[1] = jnp.where(t > 0, region_ref[jnp.maximum(t - 1, 0)], 0.0)


def second_solve_kernel(upstream_ref, values_ref, slots, hots, send_ref, vessel_ref, values):
    spare = (rows_of((8, 128)) & 3) == 3
    for t in range(BRICKS):
        for pair in range(2):
            values[pair, t] = jnp.where(spare, 0.0, values_ref[t, 8 * pair : 8 * pair + 8])
    row, lane = rows_of((16, 128)), lanes_of((16, 128))
    picked = jnp.zeros((16, 128), F32)
    for block in range(4):
        feeder = upstream_ref[block]
        device = feeder >> 2
        ends = values_ref[device & 15, 3:4, :]
        spot = (device >> 4) * 16 + (feeder & 3) * 4
        picked = jnp.where(((row >> 2) == block) & (lane == spot + (row & 3)), ends, picked)
    inflow = 0.5 * (read_table(slots, INLET) + jnp.sum(picked, axis=1, keepdims=True))
    vessel = solve_blocks(inflow, values, slots, hots, send_ref, True)
    for block in range(4):
        for k in range(3):
            vessel_ref[k, block : block + 1, :] = vessel[4 * block + k : 4 * block + k + 1]


def scatter_slots(recv_ref, sources):
    zero = jnp.zeros((16, 128), BF16)
    for source, _, _ in sources:
        source[...] = jnp.zeros(source.shape, F32)

    def senders(i, carry):
        for source, tiles, size in sources:
            hots, parts = [], []
            for q in range(SENDERS):
                s = i * SENDERS + q
                for start in tiles:
                    for base in (start, start + 4):
                        cell = recv_ref[s, base + 3 : base + 4, :].astype(jnp.int32)
                        hots.append(onehot(cell & 127, 128))
                        row = cell >> 7
                        if size == 16:
                            row = (row >> 3) * 4 + (row & 3)
                        here = matches(row, size)
                        highs, lows = [], []
                        for k in range(3):
                            flux = jnp.broadcast_to(recv_ref[s, base + k : base + k + 1, :], (16, 128))
                            high = flux.astype(BF16)
                            low = (flux - high.astype(F32)).astype(BF16)
                            highs += [jnp.where(hit, high, zero) for hit in here]
                            lows += [jnp.where(hit, low, zero) for hit in here]
                        parts.append(jnp.concatenate(highs + lows, axis=0))
            source[...] += matmul_nt(jnp.concatenate(parts, axis=1), jnp.concatenate(hots, axis=1))
        return carry

    lax.fori_loop(0, BRICKS // SENDERS, senders, 0, unroll=4)
    return [source[0 : 3 * size] + source[3 * size : 6 * size] for source, _, size in sources]


def interleave(first, last):
    first, last = first.reshape(6, 8, 128), last.reshape(6, 8, 128)
    low = lax.broadcasted_iota(jnp.int32, (6, 8, 128), 1) < 4
    even = jnp.where(low, first, pltpu.roll(last, 4, 1))
    odd = jnp.where(low, pltpu.roll(first, 4, 1), last)
    return jnp.concatenate([value[i] for i in range(6) for value in (even, odd)], axis=0)


def planes(value):
    return value.reshape(3, 4, 8, 128)


def is_even(axis):
    return lax.axis_index(axis) % 2 == 0


def in_order(axis, near, far):
    even = is_even(axis)
    return jnp.where(even, far, near), jnp.where(even, near, far)


def toward(value, near, count=3):
    upward = is_even("vessel") if near else ~is_even("vessel")
    return jnp.where(upward, value[:, 4 - count : 4], value[:, 0:count])


def write_messages(tissues, sources, near_ref, far_ref):
    for i, (value, source) in enumerate(zip(tissues, sources)):
        here = slice(8 * i, 8 * i + 8)
        value, source = planes(value), planes(source)
        for ref, near in ((near_ref, True), (far_ref, False)):
            ref[:, 0:4, here] = value
            ref[:, 4:7, here] = toward(source, near)


def first_scatter_kernel(
    recv_ref, tissue_ref, around_ref, rate_ref, rate_near_ref, rate_far_ref, near_ref, far_ref, sources_ref, *sums
):
    sources = scatter_slots(recv_ref, [(sums[i], (16 * i, 16 * i + 8), 32) for i in range(3)])
    for i in range(3):
        sources_ref[i] = sources[i]
    write_messages([tissue_ref[...], around_ref[0], around_ref[1]], sources, near_ref, far_ref)
    before, after = in_order("tissue", rate_near_ref[...], rate_far_ref[...])
    for i, value in enumerate((rate_ref[...], after, before)):
        here = slice(8 * i, 8 * i + 8)
        near_ref[:, 7:10, here] = toward(planes(value), True)
        far_ref[:, 7:10, here] = toward(planes(value), False)


def second_scatter_kernel(recv_ref, tissue_ref, side_ref, near_ref, far_ref, sources_ref, *sums):
    own, first, last = scatter_slots(
        recv_ref, [(sums[i], (16 * i, 16 * i + 8), 32 if i == 0 else 16) for i in range(3)]
    )
    sources = [own, interleave(first, last)]
    for i in range(2):
        sources_ref[i] = sources[i]
    tissue, side = planes(tissue_ref[...]), planes(side_ref[...])
    own, beyond = planes(sources[0]), planes(sources[1])
    for ref, near in ((near_ref, True), (far_ref, False)):
        ref[:, 0:4] = tissue
        ref[:, 4:7] = toward(own, near)
        ref[:, 7:10] = toward(side, near)
        ref[:, 10:12] = toward(beyond, near, 2)


def fill(now, source, tissues, sources):
    for k in range(3):
        for i in range(len(tissues)):
            now[k, 4:8, 8 * i : 8 * i + 8] = planes(tissues[i])[k]
            source[k, 4:8, 8 * i : 8 * i + 8] = planes(sources[i])[k]


def run_sweeps(now, later, source, inverse, produced):
    count = now.shape[2]
    lane = lanes_of((count, 128))
    old, new = now, later
    for sweep in range(1, SWEEPS + 1):
        for k in range(3):
            for z in range(sweep, 12 - sweep):
                middle = old[k, z]
                total = old[k, z - 1] + old[k, z + 1]
                total = total + pltpu.roll(middle, 1, 0) + pltpu.roll(middle, count - 1, 0)
                total = total + jnp.where(lane > 0, pltpu.roll(middle, 1, 1), 0.0)
                total = total + jnp.where(lane < 127, pltpu.roll(middle, 127, 1), 0.0)
                total = source[k, z] + DIFFUSION[k] * total
                if k == 2:
                    total = total + produced[z] * old[1, z]
                new[k, z] = total * inverse[k, z]
        old, new = new, old
    return old


def beside(after, before):
    low = lax.broadcasted_iota(jnp.int32, after.shape, after.ndim - 2) < 4
    return jnp.where(low, after, before)


def first_sweeps_kernel(
    far, near, tissue_ref, around_ref, rate_ref, rate_near_ref, rate_far_ref, sources_ref, recv_ref, ends_ref,
    out_ref, side_ref, inverse_ref, produced_ref, send_ref, now, later, source, inverse, produced,
):
    tissues = [tissue_ref[...], around_ref[0], around_ref[1]]
    fill(now, source, tissues, [sources_ref[i] for i in range(3)])
    before, after = in_order("tissue", rate_near_ref[...], rate_far_ref[...])
    for k in range(3):
        now[k, 0:4], now[k, 8:12] = in_order("vessel", near[k, 0:4], far[k, 0:4])
        source[k, 1:4], source[k, 8:11] = in_order("vessel", near[k, 4:7], far[k, 4:7])
        rates = [planes(value)[k] for value in (rate_ref[...], after, before)]
        below, above = in_order("vessel", near[k, 7:10], far[k, 7:10])
        for z in range(1, 11):
            if z < 4:
                rate = below[z - 1]
            elif z < 8:
                rate = jnp.concatenate([value[z - 4] for value in rates], axis=0)
            else:
                rate = above[z - 8]
            value = jnp.where(rate > 0.0, 1.0 / (6.0 * DIFFUSION[k] + rate), 0.0)
            inverse[k, z] = value
            inverse_ref[k, z, 0:8] = value[0:8]
            inverse_ref[k, z, 8:16] = beside(value[8:16], value[16:24])
            if k == 1:
                rate = 2.0 * rate
                produced[z] = rate
                produced_ref[z, 0:8] = rate[0:8]
                produced_ref[z, 8:16] = beside(rate[8:16], rate[16:24])
    final = run_sweeps(now, later, source, inverse, produced)
    brick = final[:, 4:8, 0:8].reshape(96, 128)
    out_ref[...] = brick
    side_ref[...] = beside(final[:, 4:8, 8:16], final[:, 4:8, 16:24]).reshape(96, 128)
    brick_split = split_brick(brick)
    ends = ends_ref[0, 0:1]
    for part in range(1, PARTS):
        ends = ends + pltpu.roll(ends_ref[part], 16 * part, 1)[0:1]

    def receiver(s, carry):
        cells = [recv_ref[s, 4 * b + 3 : 4 * b + 4, :].astype(jnp.int32) for b in range(4)]
        found = gather_slots(brick_split, cells)
        for pair in range(2):
            send_ref[s, 8 * pair : 8 * pair + 8] = pair_tile(
                [*found[2 * pair], ends, *found[2 * pair + 1], ends]
            )
        return carry

    lax.fori_loop(0, BRICKS, receiver, 0, unroll=BRICKS)


def second_sweeps_kernel(
    far, near, tissue_ref, side_ref, sources_ref, inverse, produced, out_ref, now, later, source
):
    fill(now, source, [tissue_ref[...], side_ref[...]], [sources_ref[i] for i in range(2)])
    zero = jnp.zeros((8, 128), F32)
    for k in range(3):
        below, above = in_order("vessel", near[k], far[k])
        now[k, 0:4, 0:8], now[k, 8:12, 0:8] = below[0:4], above[0:4]
        source[k, 1:4, 0:8], source[k, 8:11, 0:8] = below[4:7], above[4:7]
        now[k, 1:4, 8:16], now[k, 8:11, 8:16] = below[7:10], above[7:10]
        source[k, 2:4, 8:16], source[k, 8:10, 8:16] = below[10:12], above[10:12]
        now[k, 0, 8:16] = now[k, 11, 8:16] = zero
        source[k, 1, 8:16] = source[k, 10, 8:16] = zero
    final = run_sweeps(now, later, source, inverse, produced)
    out_ref[...] = final[:, 4:8, 0:8]


VMEM = pl.BlockSpec(memory_space=pltpu.VMEM)
SMEM = pl.BlockSpec(memory_space=pltpu.SMEM)
HBM = pl.BlockSpec(memory_space=pltpu.HBM)


def call(kernel, name, outs, args, scratch, spaces=None, out_spaces=None):
    spaces = spaces or [VMEM] * len(args)
    args = [
        arg if space is SMEM else pltpu.with_memory_space_constraint(arg, space.memory_space)
        for arg, space in zip(args, spaces)
    ]
    return pl.pallas_call(
        kernel,
        out_shape=[jax.ShapeDtypeStruct(out, F32) if isinstance(out, tuple) else out for out in outs],
        in_specs=spaces,
        out_specs=out_spaces or [VMEM] * len(outs),
        scratch_shapes=scratch,
        compiler_params=pltpu.CompilerParams(vmem_limit_bytes=VMEM_LIMIT),
        name=name,
    )(*args)


def shards(
    tissue_start,
    consumption,
    inlet,
    flow,
    permeability,
    intersection_count,
    intersection_segment,
    intersection_voxel,
    intersection_weight,
    upstream,
):
    def exchange(value, axis):
        return lax.all_to_all(value, axis, 0, 0, tiled=True)

    def swap(value, axis, first):
        starts = range(first, lax.axis_size(axis) - 1, 2)
        return lax.ppermute(value, axis, [pair for i in starts for pair in ((i, i + 1), (i + 1, i))])

    ring, large_ring = (3, 12, 16, 128), (3, 12, 24, 128)
    values_scratch = [pltpu.VMEM((2, BRICKS, 8, 128), F32)]

    bricks, tissue, rate = call(
        spread_kernel,
        "spread",
        [(BRICKS, 96, 128), (96, 128), (96, 128)],
        [tissue_start.reshape(96, 128), consumption.reshape(96, 128)],
        [pltpu.SemaphoreType.DMA((BRICKS + 2,))],
        [HBM] * 2,
        [HBM, VMEM, VMEM],
    )
    region = exchange(bricks, "tissue")
    rate_near, rate_far = swap(rate, "tissue", 0), swap(rate, "tissue", 1)
    slot_array = intersection_voxel.shape
    prepared = call(
        prepare_kernel,
        "prepare",
        [
            (5, BRICKS, 8, 128),
            jax.ShapeDtypeStruct((4, BRICKS, 128, 128), BF16),
        ],
        [
            intersection_segment,
            intersection_weight,
            intersection_voxel,
            flow,
            intersection_count,
            permeability,
            inlet,
        ],
        [
            pltpu.VMEM(slot_array, jnp.int32),
            pltpu.VMEM(slot_array, F32),
            pltpu.VMEM(slot_array, jnp.int32),
            pltpu.VMEM(flow.shape, F32),
            pltpu.SMEM(intersection_count.shape, jnp.int32),
            pltpu.SMEM(permeability.shape, F32),
            pltpu.SMEM(inlet.shape, F32),
            pltpu.SemaphoreType.DMA((7,)),
        ],
        [HBM] * 7,
    )
    region, rate_near, rate_far = lax.optimization_barrier((region, rate_near, rate_far))
    send, ends, around = call(
        first_solve_kernel,
        "first_solve",
        [(BRICKS, 48, 128), (PARTS, 8, 128), (2, 96, 128)],
        [region, *prepared],
        values_scratch,
    )
    received = exchange(send, "tissue")
    ends = exchange(ends, "vessel")
    near, far, sources = call(
        first_scatter_kernel,
        "first_scatter",
        [(3, 10, 24, 128), (3, 10, 24, 128), (3, 96, 128)],
        [received, tissue, around, rate, rate_near, rate_far],
        [pltpu.VMEM((192, 128), F32)] * 3,
    )
    far, near = swap(far, "vessel", 1), swap(near, "vessel", 0)
    tissue, side, inverse, produced, send = call(
        first_sweeps_kernel,
        "first_sweeps",
        [(96, 128), (96, 128), ring, ring[1:], (BRICKS, 16, 128)],
        [far, near, tissue, around, rate, rate_near, rate_far, sources, received, ends],
        [pltpu.VMEM(large_ring, F32)] * 4 + [pltpu.VMEM(large_ring[1:], F32)],
    )
    values = exchange(send, "tissue")
    send, vessel = call(
        second_solve_kernel,
        "second_solve",
        [(BRICKS, 48, 128), (3, 4, SEG)],
        [upstream, values, *prepared],
        values_scratch,
        [SMEM] + [VMEM] * 3,
    )
    received = exchange(send, "tissue")
    near, far, sources = call(
        second_scatter_kernel,
        "second_scatter",
        [(3, 12, 8, 128), (3, 12, 8, 128), (2, 96, 128)],
        [received, tissue, side],
        [pltpu.VMEM((rows, 128), F32) for rows in (192, 96, 96)],
    )
    far, near = swap(far, "vessel", 1), swap(near, "vessel", 0)
    (tissue,) = call(
        second_sweeps_kernel,
        "second_sweeps",
        [(3, 4, 8, 128)],
        [far, near, tissue, side, sources, inverse, produced],
        [pltpu.VMEM(ring, F32)] * 3,
    )
    return tissue, vessel


def solution(mesh):
    return jax.shard_map(
        shards,
        mesh=mesh,
        in_specs=(
            P(None, "vessel", "tissue", None),
            P(None, "vessel", "tissue", None),
            P(None, ("vessel", "tissue")),
            P(("vessel", "tissue"), None),
            P(),
            P(("vessel", "tissue"), None),
            P(("vessel", "tissue"), None, None),
            P(("vessel", "tissue"), None, None),
            P(("vessel", "tissue"), None, None),
            P(("vessel", "tissue")),
        ),
        out_specs=(P(None, "vessel", "tissue", None), P(None, ("vessel", "tissue"), None)),
        check_vma=False,
    )
```

```python
import jax
import jax.numpy as jnp
from jax import lax
from jax.experimental import pallas as pl
from jax.experimental.pallas import tpu as pltpu
from jax.sharding import PartitionSpec as P


SEG = 256
SWEEPS = 4
DIFFUSION = (1.0, 0.7, 0.7)
BRICKS = 16
PARTS = 8
F32 = jnp.float32
BF16 = jnp.bfloat16
VMEM_LIMIT = 16 * 1024 * 1024
SENDERS = 4
SCAN_STEPS = 4
CELLS, WEIGHTS, TABLES = 0, 4, 1
DECAY, GAIN, SCALE, INLET = 12, 13, 14, 15


def rows_of(shape):
    return lax.broadcasted_iota(jnp.int32, shape, 0)


def lanes_of(shape):
    return lax.broadcasted_iota(jnp.int32, shape, 1)


def matmul(lhs, rhs):
    return lax.dot_general(lhs, rhs, (((1,), (0,)), ((), ())), preferred_element_type=F32)


def matmul_nt(lhs, rhs):
    return lax.dot_general(lhs, rhs, (((1,), (1,)), ((), ())), preferred_element_type=F32)


def split(value):
    high = value.astype(BF16).astype(F32)
    return high, value - high


def packed(row):
    return jnp.broadcast_to(row, (16, 128)).astype(F32).astype(BF16)


def matches(index, size):
    row = rows_of((16, 128)).astype(F32).astype(BF16)
    wanted = packed(index)
    return [row + BF16(i) == wanted for i in range(0, size, 16)]


def onehot(index, size):
    one, zero = jnp.ones((16, 128), BF16), jnp.zeros((16, 128), BF16)
    return jnp.concatenate([jnp.where(hit, one, zero) for hit in matches(index, size)], axis=0)


def split_brick(brick):
    high, low = split(brick)
    return jnp.concatenate([high, low], axis=1).astype(BF16)


def gather_slots(brick_split, cells):
    hot = jnp.concatenate([onehot(cell & 127, 128) for cell in cells], axis=1)
    found = matmul(brick_split, jnp.concatenate([hot, hot], axis=0))
    values = []
    for i, cell in enumerate(cells):
        here = rows_of((32, 128)) == (cell >> 7)
        part = found[:, i * 128 : (i + 1) * 128]
        values.append(
            [
                jnp.sum(jnp.where(here, part[32 * k : 32 * k + 32], 0.0), axis=0, keepdims=True)
                for k in range(3)
            ]
        )
    return values


def pair_tile(rows):
    row = rows_of((8, 128))
    tile = jnp.broadcast_to(rows[7], (8, 128))
    for i in range(7):
        tile = jnp.where(row == i, rows[i], tile)
    return tile


def spread_kernel(tissue_hbm, rate_hbm, bricks_hbm, tissue_ref, rate_ref, sems):
    arguments = [
        pltpu.make_async_copy(tissue_hbm, tissue_ref, sems.at[BRICKS]),
        pltpu.make_async_copy(rate_hbm, rate_ref, sems.at[BRICKS + 1]),
    ]
    bricks = [pltpu.make_async_copy(tissue_ref, bricks_hbm.at[t], sems.at[t]) for t in range(BRICKS)]
    for copy in arguments:
        copy.start()
    arguments[0].wait()
    for copy in bricks:
        copy.start()
    arguments[1].wait()
    for copy in bricks:
        copy.wait()


def wide(ref, i):
    return jnp.concatenate([ref[i, t] for t in range(BRICKS)], axis=1)


def pair_slots(slots, t, kind, pair):
    even = kind + 2 * pair
    return jnp.where(rows_of((8, 128)) < 4, slots[0, t, even : even + 1], slots[0, t, even + 1 : even + 2])


def pair_weights(slots, pair):
    return jnp.concatenate([pair_slots(slots, t, WEIGHTS, pair) for t in range(BRICKS)], axis=1)


def read_table(slots, i):
    tiles = [slots[TABLES + i // 4, 4 * (i % 4) + j] for j in range(4)]
    return jnp.concatenate([jnp.concatenate(tiles[:2], axis=1), jnp.concatenate(tiles[2:], axis=1)], axis=0)


def write_table(slots, i, value):
    for j in range(4):
        rows, lanes = 8 * (j // 2), 128 * (j % 2)
        slots[TABLES + i // 4, 4 * (i % 4) + j] = value[rows : rows + 8, lanes : lanes + 128]


def by_half(rows, upper):
    high, low = split(rows)
    return jnp.concatenate(
        [
            jnp.where(upper, 0.0, high),
            jnp.where(upper, 0.0, low),
            jnp.where(upper, high, 0.0),
            jnp.where(upper, low, 0.0),
        ],
        axis=0,
    ).astype(BF16)


def sum_segments(rows, pair, weights, hots):
    lhs = by_half(rows, weights < 0.0)
    sums = []
    for block in (2 * pair, 2 * pair + 1):
        part = matmul_nt(lhs, wide(hots, block))
        sums.append(jnp.concatenate([part[0:8] + part[8:16], part[16:24] + part[24:32]], axis=1))
    return jnp.where(rows_of((8, SEG)) < 4, sums[0], sums[1])


def column_of(ref, at):
    row = rows_of((16, 1))
    column = jnp.zeros((16, 1), F32)
    for block in range(4):
        for k in range(3):
            column = jnp.where(row == 4 * block + k, ref[at(block, k)], column)
    return column


def prepare_kernel(*refs):
    slots, hots = refs[7:9]
    segment_ref, weight_ref, voxel_ref, flow_ref, count_ref, perm_ref, inlet_ref = refs[9:16]
    sems = refs[16]
    copies = [pltpu.make_async_copy(refs[i], refs[9 + i], sems.at[i]) for i in range(7)]
    for copy in copies:
        copy.start()
    for copy in copies:
        copy.wait()
    lane = lanes_of((1, 128))

    def brick(t, carry):
        for block in range(4):
            weight = weight_ref[block, pl.ds(t, 1), :]
            weight = jnp.where(lane < count_ref[block, t], weight, 0.0)
            segment = segment_ref[block, pl.ds(t, 1), :]
            hots[block, t] = onehot(segment & 127, 128)
            slots[0, t, CELLS + block : CELLS + block + 1] = voxel_ref[block, pl.ds(t, 1), :].astype(F32)
            slots[0, t, WEIGHTS + block : WEIGHTS + block + 1] = jnp.where(segment >= 128, -weight, weight)
        return carry

    lax.fori_loop(0, BRICKS, brick, 0, unroll=4)
    row = rows_of((8, SEG))
    scale = jnp.broadcast_to(column_of(perm_ref, lambda block, k: k), (16, SEG))
    write_table(slots, SCALE, scale)
    inlet = column_of(inlet_ref, lambda block, k: (k, block))
    write_table(slots, INLET, jnp.broadcast_to(inlet, (16, SEG)))
    weight_sums, speeds = [], []
    for pair in range(2):
        weights = pair_weights(slots, pair)
        weight_sums.append(sum_segments(jnp.abs(weights), pair, weights, hots))
        speeds.append(jnp.where(row < 4, flow_ref[2 * pair : 2 * pair + 1], flow_ref[2 * pair + 1 : 2 * pair + 2]))
    speed = jnp.concatenate(speeds, axis=0)
    inverse = 1.0 / (speed + scale * jnp.concatenate(weight_sums, axis=0))
    decay = speed * inverse
    write_table(slots, DECAY, decay)
    write_table(slots, GAIN, scale * inverse)
    lane = lanes_of(decay.shape)
    for i in range(SCAN_STEPS):
        step = 4**i
        once = jnp.where(lane >= step, decay, 0.0)
        twice = once * pltpu.roll(once, step, 1)
        thrice = once * pltpu.roll(twice, step, 1)
        for j, value in enumerate((once, twice, thrice)):
            write_table(slots, 3 * i + j, value)
        decay = thrice * pltpu.roll(once, 3 * step, 1)


def solve_blocks(inflow, values, slots, hots, send_ref, narrow):
    gathered = []
    for pair in range(2):
        weights = pair_weights(slots, pair)
        gathered.append(sum_segments(wide(values, pair) * jnp.abs(weights), pair, weights, hots))
    vessel = read_table(slots, GAIN) * jnp.concatenate(gathered, axis=0)
    vessel = vessel + jnp.where(lanes_of((16, SEG)) == 0, read_table(slots, DECAY) * inflow, 0.0)
    for i in range(SCAN_STEPS):
        earlier = [read_table(slots, 3 * i + j) * pltpu.roll(vessel, (j + 1) * 4**i, 1) for j in range(3)]
        vessel = (vessel + earlier[0]) + (earlier[1] + earlier[2])

    send_ref[0, 32:48] = jnp.zeros((16, 128), F32)
    send_ref[BRICKS - 1, 16:32] = jnp.zeros((16, 128), F32)
    tile_row = rows_of((8, 128))
    scale = read_table(slots, SCALE)[0:8, 0:128]
    for pair in range(2):
        high, low = split(vessel[8 * pair : 8 * pair + 8])
        lhs = jnp.concatenate(
            [high[:, :128], low[:, :128], high[:, 128:], low[:, 128:]], axis=0
        ).astype(BF16)
        found = [matmul(lhs, wide(hots, block)) for block in (2 * pair, 2 * pair + 1)]
        for t in range(BRICKS):
            weights = pair_slots(slots, t, WEIGHTS, pair)
            part = [value[:, t * 128 : (t + 1) * 128] for value in found]
            part = [jnp.where(tile_row < 4, part[0][8 * i : 8 * i + 8], part[1][8 * i : 8 * i + 8]) for i in range(4)]
            at_slot = jnp.where(weights < 0.0, part[2] + part[3], part[0] + part[1])
            flux = scale * jnp.abs(weights) * (at_slot - values[pair, t])
            cell = pair_slots(slots, t, CELLS, pair)
            cell_row = (tile_row & 3) == 3
            here = slice(8 * pair, 8 * pair + 8)
            own = jnp.where(cell_row, cell, flux)
            first = last = own
            if narrow:
                is_first = ((cell.astype(jnp.int32) >> 7) & 7) < 4
                first = jnp.where(cell_row | is_first, own, 0.0)
                last = jnp.where(is_first & ~cell_row, 0.0, own)
            send_ref[t, here] = own
            if t > 0:
                send_ref[t - 1, 16 + 8 * pair : 24 + 8 * pair] = first
            if t < BRICKS - 1:
                send_ref[t + 1, 32 + 8 * pair : 40 + 8 * pair] = last
    return vessel


def first_solve_kernel(region_ref, slots, hots, send_ref, ends_ref, around_ref, values):
    def brick(t, carry):
        cells = [slots[0, t, CELLS + block : CELLS + block + 1].astype(jnp.int32) for block in range(4)]
        found = gather_slots(split_brick(region_ref[t]), cells)
        for pair in range(2):
            values[pair, t] = pair_tile([*found[2 * pair], 0.0, *found[2 * pair + 1], 0.0])
        return carry

    lax.fori_loop(0, BRICKS, brick, 0, unroll=BRICKS)
    vessel = solve_blocks(read_table(slots, INLET), values, slots, hots, send_ref, False)
    spot = lanes_of((16, 128)) == rows_of((16, 128))
    ends = jnp.sum(jnp.where(spot, vessel[:, SEG - 1 : SEG], 0.0), axis=0, keepdims=True)
    ends_ref[...] = jnp.broadcast_to(ends[None], (PARTS, 8, 128))
    t = lax.axis_index("tissue")
    around_ref[0] = jnp.where(t < BRICKS - 1, region_ref[jnp.minimum(t + 1, BRICKS - 1)], 0.0)
    around_ref[1] = jnp.where(t > 0, region_ref[jnp.maximum(t - 1, 0)], 0.0)


def second_solve_kernel(upstream_ref, values_ref, slots, hots, send_ref, vessel_ref, values):
    spare = (rows_of((8, 128)) & 3) == 3
    for t in range(BRICKS):
        for pair in range(2):
            values[pair, t] = jnp.where(spare, 0.0, values_ref[t, 8 * pair : 8 * pair + 8])
    row, lane = rows_of((16, 128)), lanes_of((16, 128))
    picked = jnp.zeros((16, 128), F32)
    for block in range(4):
        feeder = upstream_ref[block]
        device = feeder >> 2
        ends = values_ref[device & 15, 3:4, :]
        spot = (device >> 4) * 16 + (feeder & 3) * 4
        picked = jnp.where(((row >> 2) == block) & (lane == spot + (row & 3)), ends, picked)
    inflow = 0.5 * (read_table(slots, INLET) + jnp.sum(picked, axis=1, keepdims=True))
    vessel = solve_blocks(inflow, values, slots, hots, send_ref, True)
    for block in range(4):
        for k in range(3):
            vessel_ref[k, block : block + 1, :] = vessel[4 * block + k : 4 * block + k + 1]


def scatter_slots(recv_ref, sources):
    zero = jnp.zeros((16, 128), BF16)
    for source, _, _ in sources:
        source[...] = jnp.zeros(source.shape, F32)

    def senders(i, carry):
        for source, tiles, size in sources:
            hots, parts = [], []
            for q in range(SENDERS):
                s = i * SENDERS + q
                for start in tiles:
                    for base in (start, start + 4):
                        cell = recv_ref[s, base + 3 : base + 4, :].astype(jnp.int32)
                        hots.append(onehot(cell & 127, 128))
                        row = cell >> 7
                        if size == 16:
                            row = (row >> 3) * 4 + (row & 3)
                        here = matches(row, size)
                        highs, lows = [], []
                        for k in range(3):
                            flux = jnp.broadcast_to(recv_ref[s, base + k : base + k + 1, :], (16, 128))
                            high = flux.astype(BF16)
                            low = (flux - high.astype(F32)).astype(BF16)
                            highs += [jnp.where(hit, high, zero) for hit in here]
                            lows += [jnp.where(hit, low, zero) for hit in here]
                        parts.append(jnp.concatenate(highs + lows, axis=0))
            source[...] += matmul_nt(jnp.concatenate(parts, axis=1), jnp.concatenate(hots, axis=1))
        return carry

    lax.fori_loop(0, BRICKS // SENDERS, senders, 0, unroll=4)
    return [source[0 : 3 * size] + source[3 * size : 6 * size] for source, _, size in sources]


def interleave(first, last):
    first, last = first.reshape(6, 8, 128), last.reshape(6, 8, 128)
    low = lax.broadcasted_iota(jnp.int32, (6, 8, 128), 1) < 4
    even = jnp.where(low, first, pltpu.roll(last, 4, 1))
    odd = jnp.where(low, pltpu.roll(first, 4, 1), last)
    return jnp.concatenate([value[i] for i in range(6) for value in (even, odd)], axis=0)


def planes(value):
    return value.reshape(3, 4, 8, 128)


def is_even(axis):
    return lax.axis_index(axis) % 2 == 0


def in_order(axis, near, far):
    even = is_even(axis)
    return jnp.where(even, far, near), jnp.where(even, near, far)


def toward(value, near, count=3):
    upward = is_even("vessel") if near else ~is_even("vessel")
    return jnp.where(upward, value[:, 4 - count : 4], value[:, 0:count])


def write_messages(tissues, sources, near_ref, far_ref):
    for i, (value, source) in enumerate(zip(tissues, sources)):
        here = slice(8 * i, 8 * i + 8)
        value, source = planes(value), planes(source)
        for ref, near in ((near_ref, True), (far_ref, False)):
            ref[:, 0:4, here] = value
            ref[:, 4:7, here] = toward(source, near)


def first_scatter_kernel(
    recv_ref, tissue_ref, around_ref, rate_ref, rate_near_ref, rate_far_ref, near_ref, far_ref, sources_ref, *sums
):
    sources = scatter_slots(recv_ref, [(sums[i], (16 * i, 16 * i + 8), 32) for i in range(3)])
    for i in range(3):
        sources_ref[i] = sources[i]
    write_messages([tissue_ref[...], around_ref[0], around_ref[1]], sources, near_ref, far_ref)
    before, after = in_order("tissue", rate_near_ref[...], rate_far_ref[...])
    for i, value in enumerate((rate_ref[...], after, before)):
        here = slice(8 * i, 8 * i + 8)
        near_ref[:, 7:10, here] = toward(planes(value), True)
        far_ref[:, 7:10, here] = toward(planes(value), False)


def second_scatter_kernel(recv_ref, tissue_ref, side_ref, near_ref, far_ref, sources_ref, *sums):
    own, first, last = scatter_slots(
        recv_ref, [(sums[i], (16 * i, 16 * i + 8), 32 if i == 0 else 16) for i in range(3)]
    )
    sources = [own, interleave(first, last)]
    for i in range(2):
        sources_ref[i] = sources[i]
    tissue, side = planes(tissue_ref[...]), planes(side_ref[...])
    own, beyond = planes(sources[0]), planes(sources[1])
    for ref, near in ((near_ref, True), (far_ref, False)):
        ref[:, 0:4] = tissue
        ref[:, 4:7] = toward(own, near)
        ref[:, 7:10] = toward(side, near)
        ref[:, 10:12] = toward(beyond, near, 2)


def fill(now, source, tissues, sources):
    for k in range(3):
        for i in range(len(tissues)):
            now[k, 4:8, 8 * i : 8 * i + 8] = planes(tissues[i])[k]
            source[k, 4:8, 8 * i : 8 * i + 8] = planes(sources[i])[k]


def run_sweeps(now, later, source, inverse, produced):
    count = now.shape[2]
    lane = lanes_of((count, 128))
    old, new = now, later
    for sweep in range(1, SWEEPS + 1):
        for k in range(3):
            for z in range(sweep, 12 - sweep):
                middle = old[k, z]
                total = old[k, z - 1] + old[k, z + 1]
                total = total + pltpu.roll(middle, 1, 0) + pltpu.roll(middle, count - 1, 0)
                total = total + jnp.where(lane > 0, pltpu.roll(middle, 1, 1), 0.0)
                total = total + jnp.where(lane < 127, pltpu.roll(middle, 127, 1), 0.0)
                total = source[k, z] + DIFFUSION[k] * total
                if k == 2:
                    total = total + produced[z] * old[1, z]
                new[k, z] = total * inverse[k, z]
        old, new = new, old
    return old


def beside(after, before):
    low = lax.broadcasted_iota(jnp.int32, after.shape, after.ndim - 2) < 4
    return jnp.where(low, after, before)


def first_sweeps_kernel(
    far, near, tissue_ref, around_ref, rate_ref, rate_near_ref, rate_far_ref, sources_ref, recv_ref, ends_ref,
    out_ref, side_ref, inverse_ref, produced_ref, send_ref, now, later, source, inverse, produced,
):
    tissues = [tissue_ref[...], around_ref[0], around_ref[1]]
    fill(now, source, tissues, [sources_ref[i] for i in range(3)])
    before, after = in_order("tissue", rate_near_ref[...], rate_far_ref[...])
    for k in range(3):
        now[k, 0:4], now[k, 8:12] = in_order("vessel", near[k, 0:4], far[k, 0:4])
        source[k, 1:4], source[k, 8:11] = in_order("vessel", near[k, 4:7], far[k, 4:7])
        rates = [planes(value)[k] for value in (rate_ref[...], after, before)]
        below, above = in_order("vessel", near[k, 7:10], far[k, 7:10])
        for z in range(1, 11):
            if z < 4:
                rate = below[z - 1]
            elif z < 8:
                rate = jnp.concatenate([value[z - 4] for value in rates], axis=0)
            else:
                rate = above[z - 8]
            value = jnp.where(rate > 0.0, 1.0 / (6.0 * DIFFUSION[k] + rate), 0.0)
            inverse[k, z] = value
            inverse_ref[k, z, 0:8] = value[0:8]
            inverse_ref[k, z, 8:16] = beside(value[8:16], value[16:24])
            if k == 1:
                rate = 2.0 * rate
                produced[z] = rate
                produced_ref[z, 0:8] = rate[0:8]
                produced_ref[z, 8:16] = beside(rate[8:16], rate[16:24])
    final = run_sweeps(now, later, source, inverse, produced)
    brick = final[:, 4:8, 0:8].reshape(96, 128)
    out_ref[...] = brick
    side_ref[...] = beside(final[:, 4:8, 8:16], final[:, 4:8, 16:24]).reshape(96, 128)
    brick_split = split_brick(brick)
    ends = ends_ref[0, 0:1]
    for part in range(1, PARTS):
        ends = ends + pltpu.roll(ends_ref[part], 16 * part, 1)[0:1]

    def receiver(s, carry):
        cells = [recv_ref[s, 4 * b + 3 : 4 * b + 4, :].astype(jnp.int32) for b in range(4)]
        found = gather_slots(brick_split, cells)
        for pair in range(2):
            send_ref[s, 8 * pair : 8 * pair + 8] = pair_tile(
                [*found[2 * pair], ends, *found[2 * pair + 1], ends]
            )
        return carry

    lax.fori_loop(0, BRICKS, receiver, 0, unroll=BRICKS)


def second_sweeps_kernel(
    far, near, tissue_ref, side_ref, sources_ref, inverse, produced, out_ref, now, later, source
):
    fill(now, source, [tissue_ref[...], side_ref[...]], [sources_ref[i] for i in range(2)])
    zero = jnp.zeros((8, 128), F32)
    for k in range(3):
        below, above = in_order("vessel", near[k], far[k])
        now[k, 0:4, 0:8], now[k, 8:12, 0:8] = below[0:4], above[0:4]
        source[k, 1:4, 0:8], source[k, 8:11, 0:8] = below[4:7], above[4:7]
        now[k, 1:4, 8:16], now[k, 8:11, 8:16] = below[7:10], above[7:10]
        source[k, 2:4, 8:16], source[k, 8:10, 8:16] = below[10:12], above[10:12]
        now[k, 0, 8:16] = now[k, 11, 8:16] = zero
        source[k, 1, 8:16] = source[k, 10, 8:16] = zero
    final = run_sweeps(now, later, source, inverse, produced)
    out_ref[...] = final[:, 4:8, 0:8]


VMEM = pl.BlockSpec(memory_space=pltpu.VMEM)
SMEM = pl.BlockSpec(memory_space=pltpu.SMEM)
HBM = pl.BlockSpec(memory_space=pltpu.HBM)


def call(kernel, name, outs, args, scratch, spaces=None, out_spaces=None):
    spaces = spaces or [VMEM] * len(args)
    args = [
        arg if space is SMEM else pltpu.with_memory_space_constraint(arg, space.memory_space)
        for arg, space in zip(args, spaces)
    ]
    return pl.pallas_call(
        kernel,
        out_shape=[jax.ShapeDtypeStruct(out, F32) if isinstance(out, tuple) else out for out in outs],
        in_specs=spaces,
        out_specs=out_spaces or [VMEM] * len(outs),
        scratch_shapes=scratch,
        compiler_params=pltpu.CompilerParams(vmem_limit_bytes=VMEM_LIMIT),
        name=name,
    )(*args)


def shards(
    tissue_start,
    consumption,
    inlet,
    flow,
    permeability,
    intersection_count,
    intersection_segment,
    intersection_voxel,
    intersection_weight,
    upstream,
):
    def exchange(value, axis):
        return lax.all_to_all(value, axis, 0, 0, tiled=True)

    def swap(value, axis, first):
        starts = range(first, lax.axis_size(axis) - 1, 2)
        return lax.ppermute(value, axis, [pair for i in starts for pair in ((i, i + 1), (i + 1, i))])

    ring, large_ring = (3, 12, 16, 128), (3, 12, 24, 128)
    values_scratch = [pltpu.VMEM((2, BRICKS, 8, 128), F32)]

    bricks, tissue, rate = call(
        spread_kernel,
        "spread",
        [(BRICKS, 96, 128), (96, 128), (96, 128)],
        [tissue_start.reshape(96, 128), consumption.reshape(96, 128)],
        [pltpu.SemaphoreType.DMA((BRICKS + 2,))],
        [HBM] * 2,
        [HBM, VMEM, VMEM],
    )
    region = exchange(bricks, "tissue")
    rate_near, rate_far = swap(rate, "tissue", 0), swap(rate, "tissue", 1)
    slot_array = intersection_voxel.shape
    prepared = call(
        prepare_kernel,
        "prepare",
        [
            (5, BRICKS, 8, 128),
            jax.ShapeDtypeStruct((4, BRICKS, 128, 128), BF16),
        ],
        [
            intersection_segment,
            intersection_weight,
            intersection_voxel,
            flow,
            intersection_count,
            permeability,
            inlet,
        ],
        [
            pltpu.VMEM(slot_array, jnp.int32),
            pltpu.VMEM(slot_array, F32),
            pltpu.VMEM(slot_array, jnp.int32),
            pltpu.VMEM(flow.shape, F32),
            pltpu.SMEM(intersection_count.shape, jnp.int32),
            pltpu.SMEM(permeability.shape, F32),
            pltpu.SMEM(inlet.shape, F32),
            pltpu.SemaphoreType.DMA((7,)),
        ],
        [HBM] * 7,
    )
    send, ends, around = call(
        first_solve_kernel,
        "first_solve",
        [(BRICKS, 48, 128), (PARTS, 8, 128), (2, 96, 128)],
        [region, *prepared],
        values_scratch,
    )
    send, rate_near, rate_far = lax.optimization_barrier((send, rate_near, rate_far))
    received = exchange(send, "tissue")
    ends = exchange(ends, "vessel")
    near, far, sources = call(
        first_scatter_kernel,
        "first_scatter",
        [(3, 10, 24, 128), (3, 10, 24, 128), (3, 96, 128)],
        [received, tissue, around, rate, rate_near, rate_far],
        [pltpu.VMEM((192, 128), F32)] * 3,
    )
    far, near = swap(far, "vessel", 1), swap(near, "vessel", 0)
    tissue, side, inverse, produced, send = call(
        first_sweeps_kernel,
        "first_sweeps",
        [(96, 128), (96, 128), ring, ring[1:], (BRICKS, 16, 128)],
        [far, near, tissue, around, rate, rate_near, rate_far, sources, received, ends],
        [pltpu.VMEM(large_ring, F32)] * 4 + [pltpu.VMEM(large_ring[1:], F32)],
    )
    values = exchange(send, "tissue")
    send, vessel = call(
        second_solve_kernel,
        "second_solve",
        [(BRICKS, 48, 128), (3, 4, SEG)],
        [upstream, values, *prepared],
        values_scratch,
        [SMEM] + [VMEM] * 3,
    )
    received = exchange(send, "tissue")
    near, far, sources = call(
        second_scatter_kernel,
        "second_scatter",
        [(3, 12, 8, 128), (3, 12, 8, 128), (2, 96, 128)],
        [received, tissue, side],
        [pltpu.VMEM((rows, 128), F32) for rows in (192, 96, 96)],
    )
    far, near = swap(far, "vessel", 1), swap(near, "vessel", 0)
    (tissue,) = call(
        second_sweeps_kernel,
        "second_sweeps",
        [(3, 4, 8, 128)],
        [far, near, tissue, side, sources, inverse, produced],
        [pltpu.VMEM(ring, F32)] * 3,
    )
    return tissue, vessel


def solution(mesh):
    return jax.shard_map(
        shards,
        mesh=mesh,
        in_specs=(
            P(None, "vessel", "tissue", None),
            P(None, "vessel", "tissue", None),
            P(None, ("vessel", "tissue")),
            P(("vessel", "tissue"), None),
            P(),
            P(("vessel", "tissue"), None),
            P(("vessel", "tissue"), None, None),
            P(("vessel", "tissue"), None, None),
            P(("vessel", "tissue"), None, None),
            P(("vessel", "tissue")),
        ),
        out_specs=(P(None, "vessel", "tissue", None), P(None, ("vessel", "tissue"), None)),
        check_vma=False,
    )
```

```python
import jax
import jax.numpy as jnp
from jax import lax
from jax.experimental import pallas as pl
from jax.experimental.pallas import tpu as pltpu
from jax.sharding import PartitionSpec as P


SEG = 256
SWEEPS = 4
DIFFUSION = (1.0, 0.7, 0.7)
BRICKS = 16
PARTS = 8
F32 = jnp.float32
BF16 = jnp.bfloat16
VMEM_LIMIT = 16 * 1024 * 1024
SENDERS = 4
SCAN_STEPS = 4
CELLS, WEIGHTS, TABLES = 0, 4, 1
DECAY, GAIN, SCALE, INLET = 12, 13, 14, 15


def rows_of(shape):
    return lax.broadcasted_iota(jnp.int32, shape, 0)


def lanes_of(shape):
    return lax.broadcasted_iota(jnp.int32, shape, 1)


def matmul(lhs, rhs):
    return lax.dot_general(lhs, rhs, (((1,), (0,)), ((), ())), preferred_element_type=F32)


def matmul_nt(lhs, rhs):
    return lax.dot_general(lhs, rhs, (((1,), (1,)), ((), ())), preferred_element_type=F32)


def split(value):
    high = value.astype(BF16).astype(F32)
    return high, value - high


def packed(row):
    return jnp.broadcast_to(row, (16, 128)).astype(F32).astype(BF16)


def matches(index, size):
    row = rows_of((16, 128)).astype(F32).astype(BF16)
    wanted = packed(index)
    return [row + BF16(i) == wanted for i in range(0, size, 16)]


def onehot(index, size):
    one, zero = jnp.ones((16, 128), BF16), jnp.zeros((16, 128), BF16)
    return jnp.concatenate([jnp.where(hit, one, zero) for hit in matches(index, size)], axis=0)


def split_brick(brick):
    high, low = split(brick)
    return jnp.concatenate([high, low], axis=1).astype(BF16)


def gather_slots(brick_split, cells):
    hot = jnp.concatenate([onehot(cell & 127, 128) for cell in cells], axis=1)
    found = matmul(brick_split, jnp.concatenate([hot, hot], axis=0))
    values = []
    for i, cell in enumerate(cells):
        here = rows_of((32, 128)) == (cell >> 7)
        part = found[:, i * 128 : (i + 1) * 128]
        values.append(
            [
                jnp.sum(jnp.where(here, part[32 * k : 32 * k + 32], 0.0), axis=0, keepdims=True)
                for k in range(3)
            ]
        )
    return values


def pair_tile(rows):
    row = rows_of((8, 128))
    tile = jnp.broadcast_to(rows[7], (8, 128))
    for i in range(7):
        tile = jnp.where(row == i, rows[i], tile)
    return tile


def spread_kernel(tissue_hbm, rate_hbm, bricks_hbm, tissue_ref, rate_ref, sems):
    arguments = [
        pltpu.make_async_copy(tissue_hbm, tissue_ref, sems.at[BRICKS]),
        pltpu.make_async_copy(rate_hbm, rate_ref, sems.at[BRICKS + 1]),
    ]
    bricks = [pltpu.make_async_copy(tissue_ref, bricks_hbm.at[t], sems.at[t]) for t in range(BRICKS)]
    for copy in arguments:
        copy.start()
    arguments[0].wait()
    for copy in bricks:
        copy.start()
    arguments[1].wait()
    for copy in bricks:
        copy.wait()


def wide(ref, i):
    return jnp.concatenate([ref[i, t] for t in range(BRICKS)], axis=1)


def pair_slots(slots, t, kind, pair):
    even = kind + 2 * pair
    return jnp.where(rows_of((8, 128)) < 4, slots[0, t, even : even + 1], slots[0, t, even + 1 : even + 2])


def pair_weights(slots, pair):
    return jnp.concatenate([pair_slots(slots, t, WEIGHTS, pair) for t in range(BRICKS)], axis=1)


def read_table(slots, i):
    tiles = [slots[TABLES + i // 4, 4 * (i % 4) + j] for j in range(4)]
    return jnp.concatenate([jnp.concatenate(tiles[:2], axis=1), jnp.concatenate(tiles[2:], axis=1)], axis=0)


def write_table(slots, i, value):
    for j in range(4):
        rows, lanes = 8 * (j // 2), 128 * (j % 2)
        slots[TABLES + i // 4, 4 * (i % 4) + j] = value[rows : rows + 8, lanes : lanes + 128]


def by_half(rows, upper):
    high, low = split(rows)
    return jnp.concatenate(
        [
            jnp.where(upper, 0.0, high),
            jnp.where(upper, 0.0, low),
            jnp.where(upper, high, 0.0),
            jnp.where(upper, low, 0.0),
        ],
        axis=0,
    ).astype(BF16)


def sum_segments(rows, pair, weights, hots):
    lhs = by_half(rows, weights < 0.0)
    sums = []
    for block in (2 * pair, 2 * pair + 1):
        part = matmul_nt(lhs, wide(hots, block))
        sums.append(jnp.concatenate([part[0:8] + part[8:16], part[16:24] + part[24:32]], axis=1))
    return jnp.where(rows_of((8, SEG)) < 4, sums[0], sums[1])


def column_of(ref, at):
    row = rows_of((16, 1))
    column = jnp.zeros((16, 1), F32)
    for block in range(4):
        for k in range(3):
            column = jnp.where(row == 4 * block + k, ref[at(block, k)], column)
    return column


def prepare_kernel(*refs):
    slots, hots = refs[7:9]
    segment_ref, weight_ref, voxel_ref, flow_ref, count_ref, perm_ref, inlet_ref = refs[9:16]
    sems = refs[16]
    copies = [pltpu.make_async_copy(refs[i], refs[9 + i], sems.at[i]) for i in range(7)]
    for copy in copies:
        copy.start()
    for copy in copies:
        copy.wait()
    lane = lanes_of((1, 128))

    def brick(t, carry):
        for block in range(4):
            weight = weight_ref[block, pl.ds(t, 1), :]
            weight = jnp.where(lane < count_ref[block, t], weight, 0.0)
            segment = segment_ref[block, pl.ds(t, 1), :]
            hots[block, t] = onehot(segment & 127, 128)
            slots[0, t, CELLS + block : CELLS + block + 1] = voxel_ref[block, pl.ds(t, 1), :].astype(F32)
            slots[0, t, WEIGHTS + block : WEIGHTS + block + 1] = jnp.where(segment >= 128, -weight, weight)
        return carry

    lax.fori_loop(0, BRICKS, brick, 0, unroll=BRICKS)
    row = rows_of((8, SEG))
    scale = jnp.broadcast_to(column_of(perm_ref, lambda block, k: k), (16, SEG))
    write_table(slots, SCALE, scale)
    inlet = column_of(inlet_ref, lambda block, k: (k, block))
    write_table(slots, INLET, jnp.broadcast_to(inlet, (16, SEG)))
    weight_sums, speeds = [], []
    for pair in range(2):
        weights = pair_weights(slots, pair)
        weight_sums.append(sum_segments(jnp.abs(weights), pair, weights, hots))
        speeds.append(jnp.where(row < 4, flow_ref[2 * pair : 2 * pair + 1], flow_ref[2 * pair + 1 : 2 * pair + 2]))
    speed = jnp.concatenate(speeds, axis=0)
    inverse = 1.0 / (speed + scale * jnp.concatenate(weight_sums, axis=0))
    decay = speed * inverse
    write_table(slots, DECAY, decay)
    write_table(slots, GAIN, scale * inverse)
    lane = lanes_of(decay.shape)
    for i in range(SCAN_STEPS):
        step = 4**i
        once = jnp.where(lane >= step, decay, 0.0)
        twice = once * pltpu.roll(once, step, 1)
        thrice = once * pltpu.roll(twice, step, 1)
        for j, value in enumerate((once, twice, thrice)):
            write_table(slots, 3 * i + j, value)
        decay = thrice * pltpu.roll(once, 3 * step, 1)


def solve_blocks(inflow, values, slots, hots, send_ref, narrow):
    gathered = []
    for pair in range(2):
        weights = pair_weights(slots, pair)
        gathered.append(sum_segments(wide(values, pair) * jnp.abs(weights), pair, weights, hots))
    vessel = read_table(slots, GAIN) * jnp.concatenate(gathered, axis=0)
    vessel = vessel + jnp.where(lanes_of((16, SEG)) == 0, read_table(slots, DECAY) * inflow, 0.0)
    for i in range(SCAN_STEPS):
        earlier = [read_table(slots, 3 * i + j) * pltpu.roll(vessel, (j + 1) * 4**i, 1) for j in range(3)]
        vessel = (vessel + earlier[0]) + (earlier[1] + earlier[2])

    send_ref[0, 32:48] = jnp.zeros((16, 128), F32)
    send_ref[BRICKS - 1, 16:32] = jnp.zeros((16, 128), F32)
    tile_row = rows_of((8, 128))
    scale = read_table(slots, SCALE)[0:8, 0:128]
    for pair in range(2):
        high, low = split(vessel[8 * pair : 8 * pair + 8])
        lhs = jnp.concatenate(
            [high[:, :128], low[:, :128], high[:, 128:], low[:, 128:]], axis=0
        ).astype(BF16)
        found = [matmul(lhs, wide(hots, block)) for block in (2 * pair, 2 * pair + 1)]
        for t in range(BRICKS):
            weights = pair_slots(slots, t, WEIGHTS, pair)
            part = [value[:, t * 128 : (t + 1) * 128] for value in found]
            part = [jnp.where(tile_row < 4, part[0][8 * i : 8 * i + 8], part[1][8 * i : 8 * i + 8]) for i in range(4)]
            at_slot = jnp.where(weights < 0.0, part[2] + part[3], part[0] + part[1])
            flux = scale * jnp.abs(weights) * (at_slot - values[pair, t])
            cell = pair_slots(slots, t, CELLS, pair)
            cell_row = (tile_row & 3) == 3
            here = slice(8 * pair, 8 * pair + 8)
            own = jnp.where(cell_row, cell, flux)
            first = last = own
            if narrow:
                is_first = ((cell.astype(jnp.int32) >> 7) & 7) < 4
                first = jnp.where(cell_row | is_first, own, 0.0)
                last = jnp.where(is_first & ~cell_row, 0.0, own)
            send_ref[t, here] = own
            if t > 0:
                send_ref[t - 1, 16 + 8 * pair : 24 + 8 * pair] = first
            if t < BRICKS - 1:
                send_ref[t + 1, 32 + 8 * pair : 40 + 8 * pair] = last
    return vessel


def first_solve_kernel(region_ref, slots, hots, send_ref, ends_ref, around_ref, values):
    def brick(t, carry):
        cells = [slots[0, t, CELLS + block : CELLS + block + 1].astype(jnp.int32) for block in range(4)]
        found = gather_slots(split_brick(region_ref[t]), cells)
        for pair in range(2):
            values[pair, t] = pair_tile([*found[2 * pair], 0.0, *found[2 * pair + 1], 0.0])
        return carry

    lax.fori_loop(0, BRICKS, brick, 0, unroll=BRICKS)
    vessel = solve_blocks(read_table(slots, INLET), values, slots, hots, send_ref, False)
    spot = lanes_of((16, 128)) == rows_of((16, 128))
    ends = jnp.sum(jnp.where(spot, vessel[:, SEG - 1 : SEG], 0.0), axis=0, keepdims=True)
    ends_ref[...] = jnp.broadcast_to(ends[None], (PARTS, 1, 128))
    t = lax.axis_index("tissue")
    around_ref[0] = jnp.where(t < BRICKS - 1, region_ref[jnp.minimum(t + 1, BRICKS - 1)], 0.0)
    around_ref[1] = jnp.where(t > 0, region_ref[jnp.maximum(t - 1, 0)], 0.0)


def second_solve_kernel(upstream_ref, values_ref, slots, hots, send_ref, vessel_ref, values):
    spare = (rows_of((8, 128)) & 3) == 3
    for t in range(BRICKS):
        for pair in range(2):
            values[pair, t] = jnp.where(spare, 0.0, values_ref[t, 8 * pair : 8 * pair + 8])
    row, lane = rows_of((16, 128)), lanes_of((16, 128))
    picked = jnp.zeros((16, 128), F32)
    for block in range(4):
        feeder = upstream_ref[block]
        device = feeder >> 2
        ends = values_ref[device & 15, 3:4, :]
        spot = (device >> 4) * 16 + (feeder & 3) * 4
        picked = jnp.where(((row >> 2) == block) & (lane == spot + (row & 3)), ends, picked)
    inflow = 0.5 * (read_table(slots, INLET) + jnp.sum(picked, axis=1, keepdims=True))
    vessel = solve_blocks(inflow, values, slots, hots, send_ref, True)
    for block in range(4):
        for k in range(3):
            vessel_ref[k, block : block + 1, :] = vessel[4 * block + k : 4 * block + k + 1]


def scatter_slots(recv_ref, sources):
    zero = jnp.zeros((16, 128), BF16)
    for source, _, _ in sources:
        source[...] = jnp.zeros(source.shape, F32)

    def senders(i, carry):
        for source, tiles, size in sources:
            hots, parts = [], []
            for q in range(SENDERS):
                s = i * SENDERS + q
                for start in tiles:
                    for base in (start, start + 4):
                        cell = recv_ref[s, base + 3 : base + 4, :].astype(jnp.int32)
                        hots.append(onehot(cell & 127, 128))
                        row = cell >> 7
                        if size == 16:
                            row = (row >> 3) * 4 + (row & 3)
                        here = matches(row, size)
                        highs, lows = [], []
                        for k in range(3):
                            flux = jnp.broadcast_to(recv_ref[s, base + k : base + k + 1, :], (16, 128))
                            high = flux.astype(BF16)
                            low = (flux - high.astype(F32)).astype(BF16)
                            highs += [jnp.where(hit, high, zero) for hit in here]
                            lows += [jnp.where(hit, low, zero) for hit in here]
                        parts.append(jnp.concatenate(highs + lows, axis=0))
            source[...] += matmul_nt(jnp.concatenate(parts, axis=1), jnp.concatenate(hots, axis=1))
        return carry

    lax.fori_loop(0, BRICKS // SENDERS, senders, 0, unroll=4)
    return [source[0 : 3 * size] + source[3 * size : 6 * size] for source, _, size in sources]


def interleave(first, last):
    first, last = first.reshape(6, 8, 128), last.reshape(6, 8, 128)
    low = lax.broadcasted_iota(jnp.int32, (6, 8, 128), 1) < 4
    even = jnp.where(low, first, pltpu.roll(last, 4, 1))
    odd = jnp.where(low, pltpu.roll(first, 4, 1), last)
    return jnp.concatenate([value[i] for i in range(6) for value in (even, odd)], axis=0)


def planes(value):
    return value.reshape(3, 4, 8, 128)


def is_even(axis):
    return lax.axis_index(axis) % 2 == 0


def in_order(axis, near, far):
    even = is_even(axis)
    return jnp.where(even, far, near), jnp.where(even, near, far)


def toward(value, near, count=3):
    upward = is_even("vessel") if near else ~is_even("vessel")
    return jnp.where(upward, value[:, 4 - count : 4], value[:, 0:count])


def write_messages(tissues, sources, near_ref, far_ref):
    for i, (value, source) in enumerate(zip(tissues, sources)):
        here = slice(8 * i, 8 * i + 8)
        value, source = planes(value), planes(source)
        for ref, near in ((near_ref, True), (far_ref, False)):
            ref[:, 0:4, here] = value
            ref[:, 4:7, here] = toward(source, near)


def first_scatter_kernel(
    recv_ref, tissue_ref, around_ref, rate_ref, rate_near_ref, rate_far_ref, near_ref, far_ref, sources_ref, *sums
):
    sources = scatter_slots(recv_ref, [(sums[i], (16 * i, 16 * i + 8), 32) for i in range(3)])
    for i in range(3):
        sources_ref[i] = sources[i]
    write_messages([tissue_ref[...], around_ref[0], around_ref[1]], sources, near_ref, far_ref)
    before, after = in_order("tissue", rate_near_ref[...], rate_far_ref[...])
    for i, value in enumerate((rate_ref[...], after, before)):
        here = slice(8 * i, 8 * i + 8)
        near_ref[:, 7:10, here] = toward(planes(value), True)
        far_ref[:, 7:10, here] = toward(planes(value), False)


def second_scatter_kernel(recv_ref, tissue_ref, side_ref, near_ref, far_ref, sources_ref, *sums):
    own, first, last = scatter_slots(
        recv_ref, [(sums[i], (16 * i, 16 * i + 8), 32 if i == 0 else 16) for i in range(3)]
    )
    sources = [own, interleave(first, last)]
    for i in range(2):
        sources_ref[i] = sources[i]
    tissue, side = planes(tissue_ref[...]), planes(side_ref[...])
    own, beyond = planes(sources[0]), planes(sources[1])
    for ref, near in ((near_ref, True), (far_ref, False)):
        ref[:, 0:4] = tissue
        ref[:, 4:7] = toward(own, near)
        ref[:, 7:10] = toward(side, near)
        ref[:, 10:12] = toward(beyond, near, 2)


def fill(now, source, tissues, sources):
    for k in range(3):
        for i in range(len(tissues)):
            now[k, 4:8, 8 * i : 8 * i + 8] = planes(tissues[i])[k]
            source[k, 4:8, 8 * i : 8 * i + 8] = planes(sources[i])[k]


def run_sweeps(now, later, source, inverse, produced):
    count = now.shape[2]
    lane = lanes_of((count, 128))
    old, new = now, later
    for sweep in range(1, SWEEPS + 1):
        for k in range(3):
            for z in range(sweep, 12 - sweep):
                middle = old[k, z]
                total = old[k, z - 1] + old[k, z + 1]
                total = total + pltpu.roll(middle, 1, 0) + pltpu.roll(middle, count - 1, 0)
                total = total + jnp.where(lane > 0, pltpu.roll(middle, 1, 1), 0.0)
                total = total + jnp.where(lane < 127, pltpu.roll(middle, 127, 1), 0.0)
                total = source[k, z] + DIFFUSION[k] * total
                if k == 2:
                    total = total + produced[z] * old[1, z]
                new[k, z] = total * inverse[k, z]
        old, new = new, old
    return old


def beside(after, before):
    low = lax.broadcasted_iota(jnp.int32, after.shape, after.ndim - 2) < 4
    return jnp.where(low, after, before)


def first_sweeps_kernel(
    far, near, tissue_ref, around_ref, rate_ref, rate_near_ref, rate_far_ref, sources_ref, recv_ref, ends_ref,
    out_ref, side_ref, inverse_ref, produced_ref, send_ref, now, later, source, inverse, produced,
):
    tissues = [tissue_ref[...], around_ref[0], around_ref[1]]
    fill(now, source, tissues, [sources_ref[i] for i in range(3)])
    before, after = in_order("tissue", rate_near_ref[...], rate_far_ref[...])
    for k in range(3):
        now[k, 0:4], now[k, 8:12] = in_order("vessel", near[k, 0:4], far[k, 0:4])
        source[k, 1:4], source[k, 8:11] = in_order("vessel", near[k, 4:7], far[k, 4:7])
        rates = [planes(value)[k] for value in (rate_ref[...], after, before)]
        below, above = in_order("vessel", near[k, 7:10], far[k, 7:10])
        for z in range(1, 11):
            if z < 4:
                rate = below[z - 1]
            elif z < 8:
                rate = jnp.concatenate([value[z - 4] for value in rates], axis=0)
            else:
                rate = above[z - 8]
            value = jnp.where(rate > 0.0, 1.0 / (6.0 * DIFFUSION[k] + rate), 0.0)
            inverse[k, z] = value
            inverse_ref[k, z, 0:8] = value[0:8]
            inverse_ref[k, z, 8:16] = beside(value[8:16], value[16:24])
            if k == 1:
                rate = 2.0 * rate
                produced[z] = rate
                produced_ref[z, 0:8] = rate[0:8]
                produced_ref[z, 8:16] = beside(rate[8:16], rate[16:24])
    final = run_sweeps(now, later, source, inverse, produced)
    brick = final[:, 4:8, 0:8].reshape(96, 128)
    out_ref[...] = brick
    side_ref[...] = beside(final[:, 4:8, 8:16], final[:, 4:8, 16:24]).reshape(96, 128)
    brick_split = split_brick(brick)
    ends = ends_ref[0, 0:1]
    for part in range(1, PARTS):
        ends = ends + pltpu.roll(ends_ref[part], 16 * part, 1)

    def receiver(s, carry):
        cells = [recv_ref[s, 4 * b + 3 : 4 * b + 4, :].astype(jnp.int32) for b in range(4)]
        found = gather_slots(brick_split, cells)
        for pair in range(2):
            send_ref[s, 8 * pair : 8 * pair + 8] = pair_tile(
                [*found[2 * pair], ends, *found[2 * pair + 1], ends]
            )
        return carry

    lax.fori_loop(0, BRICKS, receiver, 0, unroll=BRICKS)


def second_sweeps_kernel(
    far, near, tissue_ref, side_ref, sources_ref, inverse, produced, out_ref, now, later, source
):
    fill(now, source, [tissue_ref[...], side_ref[...]], [sources_ref[i] for i in range(2)])
    zero = jnp.zeros((8, 128), F32)
    for k in range(3):
        below, above = in_order("vessel", near[k], far[k])
        now[k, 0:4, 0:8], now[k, 8:12, 0:8] = below[0:4], above[0:4]
        source[k, 1:4, 0:8], source[k, 8:11, 0:8] = below[4:7], above[4:7]
        now[k, 1:4, 8:16], now[k, 8:11, 8:16] = below[7:10], above[7:10]
        source[k, 2:4, 8:16], source[k, 8:10, 8:16] = below[10:12], above[10:12]
        now[k, 0, 8:16] = now[k, 11, 8:16] = zero
        source[k, 1, 8:16] = source[k, 10, 8:16] = zero
    final = run_sweeps(now, later, source, inverse, produced)
    out_ref[...] = final[:, 4:8, 0:8]


VMEM = pl.BlockSpec(memory_space=pltpu.VMEM)
SMEM = pl.BlockSpec(memory_space=pltpu.SMEM)
HBM = pl.BlockSpec(memory_space=pltpu.HBM)


def call(kernel, name, outs, args, scratch, spaces=None, out_spaces=None):
    spaces = spaces or [VMEM] * len(args)
    args = [
        arg if space is SMEM else pltpu.with_memory_space_constraint(arg, space.memory_space)
        for arg, space in zip(args, spaces)
    ]
    return pl.pallas_call(
        kernel,
        out_shape=[jax.ShapeDtypeStruct(out, F32) if isinstance(out, tuple) else out for out in outs],
        in_specs=spaces,
        out_specs=out_spaces or [VMEM] * len(outs),
        scratch_shapes=scratch,
        compiler_params=pltpu.CompilerParams(vmem_limit_bytes=VMEM_LIMIT),
        name=name,
    )(*args)


def shards(
    tissue_start,
    consumption,
    inlet,
    flow,
    permeability,
    intersection_count,
    intersection_segment,
    intersection_voxel,
    intersection_weight,
    upstream,
):
    def exchange(value, axis):
        return lax.all_to_all(value, axis, 0, 0, tiled=True)

    def swap(value, axis, first):
        starts = range(first, lax.axis_size(axis) - 1, 2)
        return lax.ppermute(value, axis, [pair for i in starts for pair in ((i, i + 1), (i + 1, i))])

    ring, large_ring = (3, 12, 16, 128), (3, 12, 24, 128)
    values_scratch = [pltpu.VMEM((2, BRICKS, 8, 128), F32)]

    bricks, tissue, rate = call(
        spread_kernel,
        "spread",
        [(BRICKS, 96, 128), (96, 128), (96, 128)],
        [tissue_start.reshape(96, 128), consumption.reshape(96, 128)],
        [pltpu.SemaphoreType.DMA((BRICKS + 2,))],
        [HBM] * 2,
        [HBM, VMEM, VMEM],
    )
    region = exchange(bricks, "tissue")
    rate_near, rate_far = swap(rate, "tissue", 0), swap(rate, "tissue", 1)
    slot_array = intersection_voxel.shape
    prepared = call(
        prepare_kernel,
        "prepare",
        [
            (5, BRICKS, 8, 128),
            jax.ShapeDtypeStruct((4, BRICKS, 128, 128), BF16),
        ],
        [
            intersection_segment,
            intersection_weight,
            intersection_voxel,
            flow,
            intersection_count,
            permeability,
            inlet,
        ],
        [
            pltpu.VMEM(slot_array, jnp.int32),
            pltpu.VMEM(slot_array, F32),
            pltpu.VMEM(slot_array, jnp.int32),
            pltpu.VMEM(flow.shape, F32),
            pltpu.SMEM(intersection_count.shape, jnp.int32),
            pltpu.SMEM(permeability.shape, F32),
            pltpu.SMEM(inlet.shape, F32),
            pltpu.SemaphoreType.DMA((7,)),
        ],
        [HBM] * 7,
    )
    send, ends, around = call(
        first_solve_kernel,
        "first_solve",
        [(BRICKS, 48, 128), (PARTS, 1, 128), (2, 96, 128)],
        [region, *prepared],
        values_scratch,
    )
    send, rate_near, rate_far = lax.optimization_barrier((send, rate_near, rate_far))
    received = exchange(send, "tissue")
    ends = exchange(ends, "vessel")
    near, far, sources = call(
        first_scatter_kernel,
        "first_scatter",
        [(3, 10, 24, 128), (3, 10, 24, 128), (3, 96, 128)],
        [received, tissue, around, rate, rate_near, rate_far],
        [pltpu.VMEM((192, 128), F32)] * 3,
    )
    far, near = swap(far, "vessel", 1), swap(near, "vessel", 0)
    tissue, side, inverse, produced, send = call(
        first_sweeps_kernel,
        "first_sweeps",
        [(96, 128), (96, 128), ring, ring[1:], (BRICKS, 16, 128)],
        [far, near, tissue, around, rate, rate_near, rate_far, sources, received, ends],
        [pltpu.VMEM(large_ring, F32)] * 4 + [pltpu.VMEM(large_ring[1:], F32)],
    )
    values = exchange(send, "tissue")
    send, vessel = call(
        second_solve_kernel,
        "second_solve",
        [(BRICKS, 48, 128), (3, 4, SEG)],
        [upstream, values, *prepared],
        values_scratch,
        [SMEM] + [VMEM] * 3,
    )
    received = exchange(send, "tissue")
    near, far, sources = call(
        second_scatter_kernel,
        "second_scatter",
        [(3, 12, 8, 128), (3, 12, 8, 128), (2, 96, 128)],
        [received, tissue, side],
        [pltpu.VMEM((rows, 128), F32) for rows in (192, 96, 96)],
    )
    far, near = swap(far, "vessel", 1), swap(near, "vessel", 0)
    (tissue,) = call(
        second_sweeps_kernel,
        "second_sweeps",
        [(3, 4, 8, 128)],
        [far, near, tissue, side, sources, inverse, produced],
        [pltpu.VMEM(ring, F32)] * 3,
    )
    return tissue, vessel


def solution(mesh):
    return jax.shard_map(
        shards,
        mesh=mesh,
        in_specs=(
            P(None, "vessel", "tissue", None),
            P(None, "vessel", "tissue", None),
            P(None, ("vessel", "tissue")),
            P(("vessel", "tissue"), None),
            P(),
            P(("vessel", "tissue"), None),
            P(("vessel", "tissue"), None, None),
            P(("vessel", "tissue"), None, None),
            P(("vessel", "tissue"), None, None),
            P(("vessel", "tissue")),
        ),
        out_specs=(P(None, "vessel", "tissue", None), P(None, ("vessel", "tissue"), None)),
        check_vma=False,
    )
```
